32 devices in a mesh: sample: 4 (over y, x), fsdp: 8 (over z, core).
Axes of the slice: x: 2, y: 2, z: 4, core: 2. Of those that a mesh axis runs over, the one named last changes fastest.
Arguments:
- seed_step: int32 [2], replicated, may hold values from 0 to 16777215
- attn: bfloat16 [16384, 2048], P(('sample', 'fsdp')), may hold values from -6 to 6
- resid: bfloat16 [16384, 4096], P(('sample', 'fsdp')), may hold values from -36 to 36
- cotangent: bfloat16 [16384, 4096], P(('sample', 'fsdp')), may hold values from -6 to 6
- gain: bfloat16 [4096], replicated, may hold values from 0.099609375 to 1.8984375
- mean: float32 [2048, 4096], P('fsdp'), may hold values from -6 to 6
- hess: float32 [2048, 4096], P('fsdp'), may hold values from 0.25 to 4
- momentum: float32 [2048, 4096], P('fsdp'), may hold values from -3 to 3
Outputs:
- new_mean: float32 [2048, 4096], P('fsdp')
- new_hess: float32 [2048, 4096], P('fsdp')
- new_momentum: float32 [2048, 4096], P('fsdp')
The draws below stay inside these ranges and needn't reach their ends.
All inputs are finite; a program needn't handle non-finite values.
Results may differ from the reference program's by a relative error of at most 0.0035.
Values may be sent and summed in bfloat16 or wider, within the bound.
A program may use at most 192 MiB of HBM per device.

```python
import math
import jax
import jax.numpy as jnp
from jax import lax

D = 4096
IN = 2048
TOK_DEV = 512
TOKENS = 16384
N_SAMPLE = 4
N_FSDP = 8


def draw_resid(key, part):
    first_key, second_key, third_key = jax.random.split(key, 3)
    base = jnp.clip(jax.random.normal(first_key, (TOKENS, D), jnp.float32), -4.0, 4.0)
    row_scale = jnp.exp(jax.random.uniform(second_key, (TOKENS, 1), jnp.float32, -1.2039728, 1.0986123))
    col_scale = jnp.exp(jax.random.uniform(third_key, (1, D), jnp.float32, -1.2039728, 1.0986123))
    return (base * row_scale * col_scale).astype(jnp.bfloat16)


def levels(key, dims, shards, least, largest):
    factor_of, own = 1.0, jax.random.fold_in(key, 6)
    for position, parts in shards:
        steps = jnp.exp(jax.random.uniform(jax.random.fold_in(own, position), (parts,), jnp.float32, least / len(shards), largest / len(shards)))
        factor_of = factor_of * jnp.repeat(steps, dims[position] // parts).reshape([-1 if axis == position else 1 for axis in range(len(dims))])
    return factor_of


def scatter_about(key, dims, scale, most, shards=(), held_as=jnp.bfloat16):
    loudness = levels(key, dims, shards, -0.22, 0.18) if shards else 1.0
    result = jax.random.normal(key, dims, jnp.float32) * scale * loudness
    return jnp.minimum(jnp.maximum(result, -most), most).astype(held_as)


def setup_inputs(seed: int = 0) -> dict:
    seeds = jax.random.split(jax.random.key(seed), 9)
    seed_step = jax.random.randint(seeds[0], (2,), 0, 16777216).astype(jnp.int32)
    attn = scatter_about(seeds[1], (TOKENS, IN), 1.0, 6.0, ((0, 32),))
    resid = draw_resid(jax.random.fold_in(seeds[8], 71), 0)
    cotangent = scatter_about(seeds[3], (TOKENS, D), 1.0, 6.0, ((0, 32),))
    gain = jnp.clip(1.0 + 0.18 * jax.random.normal(seeds[4], (D,), jnp.float32), 0.099609375, 1.8984375).astype(jnp.bfloat16)
    mean = scatter_about(seeds[5], (IN, D), 1.0, 6.0, ((0, 8),), jnp.float32)
    hess = jnp.clip(jnp.exp(math.log(4.0) - 2.7725887 * jax.random.uniform(seeds[6], (IN, D), jnp.float32) ** levels(seeds[6], (IN, D), ((0, 8),), -0.2, 0.2)), 0.25, 4.0)
    momentum = scatter_about(seeds[7], (IN, D), 0.5, 3.0, ((0, 8),), jnp.float32)
    return {"seed_step": seed_step, "attn": attn, "resid": resid, "cotangent": cotangent, "gain": gain, "mean": mean, "hess": hess, "momentum": momentum}


ess_value = 10.0
decay_first = 0.8
decay_second = 0.8
step_size = 0.3
damping = 0.1
norm_eps = 1e-05

def noise_table(seed_step, group_id, row_start, row_count, in_width, width):
    row_index = jnp.arange(row_count, dtype=jnp.int32)[:, None] + row_start
    col_index = jnp.arange(width, dtype=jnp.int32)[None, :]
    mixing = (group_id * in_width + row_index) * width + col_index
    mixing = jnp.bitwise_xor(mixing, seed_step[0])
    mixing = mixing * 668265261 + seed_step[1] * 374761393
    mixing = jnp.bitwise_xor(mixing, jnp.right_shift(mixing, 15) & 131071)
    mixing = mixing * 739982445
    mixing = jnp.bitwise_xor(mixing, jnp.right_shift(mixing, 12) & 1048575)
    mixing = mixing * 695872825
    mixing = jnp.bitwise_xor(mixing, jnp.right_shift(mixing, 15) & 131071)
    first_unif = ((mixing & 4095).astype(jnp.float32) + 0.5) / 4096.0
    second_unif = ((jnp.right_shift(mixing, 12) & 4095).astype(jnp.float32) + 0.5) / 4096.0
    return 2.449489742783178 * (first_unif + second_unif - 1.0)

def reference(seed_step, attn, resid, cotangent, gain, mean, hess, momentum):
    scaling = IN ** (-0.5)
    sigma = 1.0 / jnp.sqrt(ess_value * (hess + damping))
    mean_low = mean.astype(jnp.bfloat16).astype(jnp.float32)
    sigma_low = sigma.astype(jnp.bfloat16).astype(jnp.float32)
    group_rows = TOK_DEV * N_FSDP
    attn_groups = attn.reshape(N_SAMPLE, group_rows, IN)
    resid_groups = resid.reshape(N_SAMPLE, group_rows, D)
    cot_groups = cotangent.reshape(N_SAMPLE, group_rows, D)
    gain_full = gain.astype(jnp.float32)

    def per_group(carry, inputs):
        grad_sum, curv_sum = carry
        group_id, attn_s, resid_s, cot_s = inputs
        epsilon = noise_table(seed_step, group_id, 0, IN, IN, D)
        sampled = (mean_low + sigma_low * epsilon).astype(jnp.bfloat16)
        total = resid_s.astype(jnp.float32) + jnp.dot(attn_s, sampled, preferred_element_type=jnp.float32) * scaling
        inverse = lax.rsqrt(lax.optimization_barrier(jnp.mean(total * total, axis=-1, keepdims=True)) + norm_eps)
        upstream = gain_full * cot_s.astype(jnp.float32)
        back = inverse * upstream - total * inverse ** 3 * lax.optimization_barrier(jnp.mean(total * upstream, axis=-1, keepdims=True))
        back_low = back.astype(jnp.bfloat16)

        def add_part(accum, pair):
            part = (jnp.dot(pair[0].T, pair[1], preferred_element_type=jnp.float32) * scaling).astype(jnp.bfloat16)
            part = lax.optimization_barrier(part)
            return (accum + part.astype(jnp.float32), None)
        grad_s, _ = lax.scan(add_part, jnp.zeros((IN, D), jnp.float32), (attn_s.reshape(N_FSDP, TOK_DEV, IN), back_low.reshape(N_FSDP, TOK_DEV, D)))
        return ((grad_sum + grad_s, curv_sum + grad_s * epsilon / sigma), None)
    start = (jnp.zeros((IN, D), jnp.float32), jnp.zeros((IN, D), jnp.float32))
    (grad_sum, curv_sum), _ = lax.scan(per_group, start, (jnp.arange(N_SAMPLE, dtype=jnp.int32), attn_groups, resid_groups, cot_groups))
    grad_mean = grad_sum / N_SAMPLE
    hess_est = curv_sum / N_SAMPLE
    new_momentum = decay_first * momentum + (1.0 - decay_first) * grad_mean
    new_hess = decay_second * hess + (1.0 - decay_second) * hess_est + 0.5 * (1.0 - decay_second) ** 2 * (hess - hess_est) ** 2 / (hess + damping)
    new_mean = mean - step_size * (new_momentum + damping * mean) / (new_hess + damping)
    return (new_mean, new_hess, new_momentum)
```

```python
import functools

import jax
import jax.numpy as jnp
from jax import lax
from jax.experimental import pallas as pl
from jax.experimental.pallas import tpu as pltpu
from jax.sharding import PartitionSpec as P

ess_value = 10.0
decay_first = 0.8
decay_second = 0.8
step_size = 0.3
damping = 0.1
norm_eps = 1e-05


noise_scale = 2.449489742783178

MESH = pl.DeviceIdType.MESH
PIECES = 8
STRIP = 32


def noise_count(mixing, seed, key):
    shift = lax.shift_right_logical
    mixing = jnp.bitwise_xor(mixing, seed)
    mixing = mixing * 668265261 + key
    mixing = jnp.bitwise_xor(mixing, shift(mixing, 15))
    mixing = mixing * 739982445
    mixing = jnp.bitwise_xor(mixing, shift(mixing, 12))
    mixing = mixing * 695872825
    mixing = jnp.bitwise_xor(mixing, shift(mixing, 15))
    return (mixing & 4095) + (shift(mixing, 12) & 4095)


def noise_block(first, dims, width, seed, key):
    index = (
        lax.broadcasted_iota(jnp.int32, dims, 0) * width
        + lax.broadcasted_iota(jnp.int32, dims, 1)
        + first
    )
    count = noise_count(index, seed, key).astype(jnp.float32)
    return count * (noise_scale / 4096.0) + (noise_scale / 4096.0 - noise_scale)


def ivon_update(mean, hess, momentum, grad_sum, curv_sum, groups):
    grad_mean = grad_sum / groups
    hess_est = curv_sum / groups
    new_momentum = decay_first * momentum + (1.0 - decay_first) * grad_mean
    new_hess = (
        decay_second * hess
        + (1.0 - decay_second) * hess_est
        + 0.5 * (1.0 - decay_second) ** 2 * (hess - hess_est) ** 2 / (hess + damping)
    )
    new_mean = mean - step_size * (new_momentum + damping * mean) / (new_hess + damping)
    return (new_mean, new_hess, new_momentum)


def exchange_kernel(
    line, groups, scaling,
    seed_step, gain, attn_in, mean, hess, resid, cotangent, out,
    attn, weights, back, total, paired, chained, settings, outbox,
    local_sem, own_sem, set_up, set_down, set_recv, peer_send, peer_recv,
    twin_send, twin_recv, free,
    pair_send, pair_recv, chain_send, chain_recv, group_send, group_recv, out_sem,
):
    group = lax.axis_index("sample")
    shard = lax.axis_index("fsdp")
    place = lax.div(shard, 2)
    core = lax.rem(shard, 2)
    twin = place * 2 + 1 - core
    rows, width = mean.shape
    tokens, in_width = attn.shape
    quarter = rows // groups
    part = width // PIECES
    strip = min(STRIP, quarter)
    last = line - 1
    above = lax.rem(place + 1, line) * 2 + core
    below = lax.rem(place + last, line) * 2 + core

    barrier = pltpu.get_barrier_semaphore()
    for other in (twin, above, below):
        pl.semaphore_signal(barrier, inc=1, device_id={"fsdp": other}, device_id_type=MESH)
    for step in range(1, groups):
        pl.semaphore_signal(
            barrier, inc=1, device_id={"sample": lax.rem(group + step, groups)}, device_id_type=MESH
        )

    def own_copy(which, k):
        rs = pl.ds(pl.multiple_of(k * quarter, quarter), quarter)
        to = pl.ds(pl.multiple_of(which * rows + k * quarter, quarter), quarter)
        return pltpu.make_async_copy(
            (mean, hess)[which].at[rs, :], total.at[to, :], own_sem.at[which, k]
        )

    def take_own(k, carry):
        own_copy(0, lax.rem(group + k, groups)).start()
        own_copy(1, lax.rem(group + k, groups)).start()
        return carry

    lax.fori_loop(0, groups, take_own, 0)
    take_attn = pltpu.make_async_copy(attn_in, attn, local_sem.at[1])
    take_attn.start()
    take_resid = pltpu.make_async_copy(resid, back, local_sem.at[0])
    take_resid.start()

    def wait_own(k, carry):
        own_copy(0, lax.rem(group + k, groups)).wait()
        own_copy(1, lax.rem(group + k, groups)).wait()
        return carry

    wait_own(0, 0)
    seed = seed_step[0]
    key = seed_step[1] * 374761393

    def low_sigma(value):
        return lax.rsqrt(ess_value * (value + damping)).astype(jnp.bfloat16)

    def piece_cols(h):
        return pl.ds(pl.multiple_of(h * part, part), part)

    def quarter_rows(which):
        return pl.ds(pl.multiple_of(core * rows + which * quarter, quarter), quarter)

    def set_copy(layer, h, send, other):
        return pltpu.make_async_remote_copy(
            src_ref=settings.at[layer, h],
            dst_ref=settings.at[layer, h],
            send_sem=send,
            recv_sem=set_recv.at[layer, h],
            device_id={"fsdp": other},
            device_id_type=MESH,
        )

    pl.semaphore_wait(barrier, groups + 2)

    def settle(h, carry):
        cs = piece_cols(h)
        at = pl.multiple_of(group * quarter, quarter)
        settings[place, h, 0] = total[pl.ds(at, quarter), cs].astype(jnp.bfloat16)
        settings[place, h, 1] = low_sigma(
            total[pl.ds(pl.multiple_of(rows + group * quarter, quarter), quarter), cs]
        )

        @pl.when(place < last)
        def _():
            set_copy(place, h, set_up.at[place], above).start()

        @pl.when(place > 0)
        def _():
            set_copy(place, h, set_down.at[place], below).start()
        return carry

    lax.fori_loop(0, PIECES, settle, 0)
    lax.fori_loop(1, groups, wait_own, 0)

    def twin_copy(layer, h):
        block = weights.at[layer, h, pl.ds(pl.multiple_of(core * rows, rows), rows)]
        return pltpu.make_async_remote_copy(
            src_ref=block,
            dst_ref=block,
            send_sem=twin_send.at[layer],
            recv_sem=twin_recv.at[layer, h],
            device_id={"fsdp": twin},
            device_id_type=MESH,
        )

    def first_index(g, layer, row, h):
        return (g * in_width + (layer * 2 + core) * rows + row) * width + h * part

    def sample_own(h):
        cs = piece_cols(h)

        def some(r, carry):
            at = r * strip
            mean_low = total[pl.ds(pl.multiple_of(at, strip), strip), cs].astype(jnp.bfloat16)
            sigma = low_sigma(total[pl.ds(pl.multiple_of(rows + at, strip), strip), cs])
            noise = noise_block(
                first_index(group, place, at, h), (strip, part), width, seed, key
            )
            weights[place, h, pl.ds(pl.multiple_of(core * rows + at, strip), strip)] = (
                mean_low.astype(jnp.float32) + sigma.astype(jnp.float32) * noise
            ).astype(jnp.bfloat16)
            return carry

        lax.fori_loop(0, rows // strip, some, 0)
        twin_copy(place, h).start()

    def box_of(layer):
        return layer - jnp.where(layer > place, 1, 0)

    def peer_copy(layer, h, k):
        return pltpu.make_async_remote_copy(
            src_ref=outbox.at[box_of(layer), h, k - 1],
            dst_ref=weights.at[layer, h, quarter_rows(group)],
            send_sem=peer_send.at[box_of(layer)],
            recv_sem=peer_recv.at[layer, h],
            device_id={"sample": lax.rem(group + k, groups)},
            device_id_type=MESH,
        )

    def produce(layer, h):
        def draw(g, r):
            rs = pl.ds(pl.multiple_of(r * strip, strip), strip)
            noise = noise_block(
                first_index(g, layer, group * quarter + r * strip, h),
                (strip, part), width, seed, key,
            )
            return (
                settings[layer, h, 0, rs].astype(jnp.float32)
                + settings[layer, h, 1, rs].astype(jnp.float32) * noise
            ).astype(jnp.bfloat16)

        def for_peer(k, carry):
            def some(r, inner):
                rs = pl.ds(pl.multiple_of(r * strip, strip), strip)
                outbox[box_of(layer), h, k - 1, rs] = draw(lax.rem(group + k, groups), r)
                return inner

            lax.fori_loop(0, quarter // strip, some, 0)
            peer_copy(layer, h, k).start()
            return carry

        lax.fori_loop(1, groups, for_peer, 0)

        def for_own(r, inner):
            at = pl.multiple_of(core * rows + group * quarter + r * strip, strip)
            weights[layer, h, pl.ds(at, strip)] = draw(group, r)
            return inner

        lax.fori_loop(0, quarter // strip, for_own, 0)

    def pass_to_twin(layer, h):
        some = pl.ds(pl.multiple_of(core * rows, rows), (groups - 1) * quarter)
        pltpu.make_async_remote_copy(
            src_ref=weights.at[layer, h, some],
            dst_ref=weights.at[layer, h, some],
            send_sem=peer_send.at[0],
            recv_sem=peer_recv.at[layer, h],
            device_id={"sample": lax.rem(group + 1, groups)},
            device_id_type=MESH,
        ).wait_recv()
        twin_copy(layer, h).start()

    def product(layer, h):
        twin_copy(layer, h).wait_recv()
        lhs = attn[:, pl.ds(pl.multiple_of(layer * 2 * rows, 2 * rows), 2 * rows)]
        return jnp.dot(lhs, weights[layer, h], preferred_element_type=jnp.float32)

    def multiply_own(h):
        cs = piece_cols(h)
        total[:, cs] = product(place, h) + back[:, cs].astype(jnp.float32) * (1.0 / scaling)

    def multiply(layer, h):
        total[:, piece_cols(h)] += product(layer, h)

    def both(i, action):
        t = lax.div(i, PIECES)
        h = lax.rem(i, PIECES)
        low = place - 1 - t
        high = place + 1 + t

        @pl.when((i >= 0) & (low >= 0))
        def _():
            action(jnp.maximum(low, 0), h, True)

        @pl.when((i >= 0) & (high <= last))
        def _():
            action(jnp.minimum(high, last), h, False)

    def arrive(layer, h, upward):
        set_copy(layer, h, set_up.at[layer], above).wait_recv()
        if upward:
            @pl.when(place < last)
            def _():
                set_copy(layer, h, set_up.at[layer], above).start()
        else:
            @pl.when(place > 0)
            def _():
                set_copy(layer, h, set_down.at[layer], below).start()
        produce(layer, h)

    steps = last * PIECES

    def gather_step(i, carry):
        @pl.when(i < steps)
        def _():
            both(i, arrive)

        @pl.when(i < PIECES)
        def _():
            sample_own(jnp.minimum(i, PIECES - 1))

        @pl.when((i >= 1) & (i <= steps))
        def _():
            both(i - 1, lambda layer, h, upward: pass_to_twin(layer, h))

        @pl.when(i == 1)
        def _():
            take_attn.wait()
            take_resid.wait()

        @pl.when((i >= 1) & (i <= PIECES))
        def _():
            multiply_own(jnp.minimum(jnp.maximum(i - 1, 0), PIECES - 1))

        @pl.when(i == PIECES + 1)
        def _():
            pltpu.make_async_copy(cotangent, back, local_sem.at[0]).start()

        @pl.when(i >= 2)
        def _():
            both(i - 2, lambda layer, h, upward: multiply(layer, h))
        return carry

    lax.fori_loop(0, steps + 2, gather_step, 0)

    def drain_twin(layer, carry):
        block = weights.at[layer, :, pl.ds(pl.multiple_of(core * rows, rows), rows)]
        pltpu.make_async_remote_copy(
            src_ref=block,
            dst_ref=block,
            send_sem=twin_send.at[layer],
            recv_sem=twin_recv.at[layer, 0],
            device_id={"fsdp": twin},
            device_id_type=MESH,
        ).wait_send()
        return carry

    lax.fori_loop(0, line, drain_twin, 0)
    for step in range(1, groups):
        pl.semaphore_signal(
            free, inc=1, device_id={"sample": lax.rem(group + step, groups)}, device_id_type=MESH
        )

    pltpu.make_async_copy(cotangent, back, local_sem.at[0]).wait()
    span = 512

    def normalise(r, carry):
        sl = pl.ds(pl.multiple_of(r * 16, 16), 16)
        square = jnp.zeros((16, span), jnp.float32)
        cross = jnp.zeros((16, span), jnp.float32)
        for c in range(width // span):
            cs = pl.ds(c * span, span)
            value = total[sl, cs] * scaling
            upstream = gain[:, cs].astype(jnp.float32) * back[sl, cs].astype(jnp.float32)
            square = square + value * value
            cross = cross + value * upstream
        inverse = lax.rsqrt(jnp.sum(square, axis=-1, keepdims=True) * (1.0 / width) + norm_eps)
        slope = inverse * inverse * inverse * (
            jnp.sum(cross, axis=-1, keepdims=True) * (1.0 / width)
        )
        for c in range(width // span):
            cs = pl.ds(c * span, span)
            value = total[sl, cs] * scaling
            upstream = gain[:, cs].astype(jnp.float32) * back[sl, cs].astype(jnp.float32)
            back[sl, cs] = (inverse * upstream - value * slope).astype(jnp.bfloat16)
        return carry

    lax.fori_loop(0, tokens // 16, normalise, 0)

    def partial(block, piece):
        lhs = attn[:, pl.ds(pl.multiple_of(block * rows, rows), rows)]
        rhs = back[:, piece_cols(piece)]
        return (
            lax.dot_general(lhs, rhs, (((0,), (0,)), ((), ())), preferred_element_type=jnp.float32)
            * scaling
        )

    def pair_copy(goal, piece):
        return pltpu.make_async_remote_copy(
            src_ref=weights.at[goal, piece, pl.ds(0, rows)],
            dst_ref=paired.at[goal, piece],
            send_sem=pair_send.at[goal, piece],
            recv_sem=pair_recv.at[goal, piece],
            device_id={"fsdp": twin},
            device_id_type=MESH,
        )

    def give_twin(i, piece):
        goal = i
        weights[goal, piece, pl.ds(0, rows)] = partial(goal * 2 + 1 - core, piece).astype(
            jnp.bfloat16
        )
        pair_copy(goal, piece).start()
        return piece

    def chain_copy(goal, slot, piece, other):
        return pltpu.make_async_remote_copy(
            src_ref=chained.at[goal, piece],
            dst_ref=chained.at[slot, piece],
            send_sem=chain_send.at[goal, piece],
            recv_sem=chain_recv.at[slot, piece],
            device_id={"fsdp": other},
            device_id_type=MESH,
        )

    def own_term(goal, piece):
        pair_copy(goal, piece).wait_recv()
        return partial(goal * 2 + core, piece) + paired[goal, piece].astype(jnp.float32)

    def forward(goal, piece, first, slot, other):
        @pl.when(first)
        def _():
            chained[goal, piece] = own_term(goal, piece).astype(jnp.bfloat16)

        @pl.when(jnp.logical_not(first))
        def _():
            term = own_term(goal, piece)
            chain_copy(goal, goal, piece, other).wait_recv()
            chained[goal, piece] = (term + chained[goal, piece].astype(jnp.float32)).astype(
                jnp.bfloat16
            )

        chain_copy(goal, slot, piece, other).start()

    inbox = pl.ds(rows, rows)

    def group_copy(piece, step):
        return pltpu.make_async_remote_copy(
            src_ref=weights.at[group, piece, inbox],
            dst_ref=weights.at[group, piece, inbox],
            send_sem=group_send.at[step, piece],
            recv_sem=group_recv.at[piece],
            device_id={"sample": lax.rem(group + step, groups)},
            device_id_type=MESH,
        )

    def out_copy(which, piece):
        rs = pl.ds(which * rows, rows)
        cs = piece_cols(piece)
        return pltpu.make_async_copy(
            total.at[rs, cs], out.at[which, :, cs], out_sem.at[which, piece]
        )

    def consume(piece):
        many = weights.at[pl.ds(0, groups - 1), piece, inbox]
        pltpu.make_async_remote_copy(
            src_ref=many,
            dst_ref=many,
            send_sem=group_send.at[1, piece],
            recv_sem=group_recv.at[piece],
            device_id={"sample": lax.rem(group + 1, groups)},
            device_id_type=MESH,
        ).wait_recv()
        cs = piece_cols(piece)

        def some(r, carry):
            at = r * strip
            grad_sum = jnp.zeros((strip, part), jnp.float32)
            curv_sum = jnp.zeros((strip, part), jnp.float32)
            for g in range(groups):
                grad = weights[
                    g, piece, pl.ds(pl.multiple_of(rows + at, strip), strip)
                ].astype(jnp.float32)
                noise = noise_block(
                    first_index(g, place, at, piece), (strip, part), width, seed, key
                )
                grad_sum = grad_sum + grad
                curv_sum = curv_sum + grad * noise
            total[pl.ds(pl.multiple_of(at, strip), strip), cs] = grad_sum
            total[pl.ds(pl.multiple_of(rows + at, strip), strip), cs] = curv_sum
            return carry

        lax.fori_loop(0, rows // strip, some, 0)
        out_copy(0, piece).start()
        out_copy(1, piece).start()

    @pl.when(place == 0)
    def _():
        chained[0] = jnp.zeros(chained.shape[1:], chained.dtype)

    @pl.when(place == last)
    def _():
        chained[line] = jnp.zeros(chained.shape[1:], chained.dtype)

    lax.fori_loop(0, line, give_twin, 0)

    def reduce_step(step, carry):
        up_at = step - place
        up_piece = lax.div(jnp.maximum(up_at, 0), last)
        up_goal = last - lax.rem(jnp.maximum(up_at, 0), last)

        @pl.when((up_at >= 0) & (up_piece < PIECES) & (up_goal > place))
        def _():
            forward(up_goal, up_piece, place == 0, up_goal, above)

        down_at = step - (last - place)
        down_piece = lax.div(jnp.maximum(down_at, 0), last)
        down_goal = lax.rem(jnp.maximum(down_at, 0), last)

        @pl.when((down_at >= 0) & (down_piece < PIECES) & (down_goal < place))
        def _():
            slot = jnp.where(down_goal == place - 1, line, down_goal)
            forward(down_goal, down_piece, place == last, slot, below)

        turn = lax.div(step, last)

        @pl.when((lax.rem(step, last) == 0) & (turn < PIECES - 1))
        def _():
            lax.fori_loop(0, line, give_twin, turn + 1)

        @pl.when((lax.rem(step, last) == 0) & (turn >= 1))
        def _():
            piece = turn - 1
            term = own_term(place, piece)

            @pl.when(place > 0)
            def _():
                chain_copy(place, place, piece, below).wait_recv()

            @pl.when(place < last)
            def _():
                chain_copy(place, line, piece, above).wait_recv()

            weights[group, piece, inbox] = (
                term
                + chained[place, piece].astype(jnp.float32)
                + chained[line, piece].astype(jnp.float32)
            ).astype(jnp.bfloat16)

            @pl.when(piece == 0)
            def _():
                pl.semaphore_wait(free, groups - 1)

            for k in range(1, groups):
                group_copy(piece, k).start()

        @pl.when((lax.rem(step, last) == 0) & (turn >= 2))
        def _():
            consume(jnp.maximum(turn - 2, 0))
        return carry

    lax.fori_loop(0, PIECES * last + 1, reduce_step, 0)

    def drain_layer(layer, carry):
        @pl.when((place < last) & (layer <= place))
        def _():
            pltpu.make_async_remote_copy(
                src_ref=settings.at[layer], dst_ref=settings.at[layer],
                send_sem=set_up.at[layer], recv_sem=set_recv.at[layer, 0],
                device_id={"fsdp": above}, device_id_type=MESH,
            ).wait_send()

        @pl.when((place > 0) & (layer >= place))
        def _():
            pltpu.make_async_remote_copy(
                src_ref=settings.at[layer], dst_ref=settings.at[layer],
                send_sem=set_down.at[layer], recv_sem=set_recv.at[layer, 0],
                device_id={"fsdp": below}, device_id_type=MESH,
            ).wait_send()

        @pl.when(layer < last)
        def _():
            box = jnp.minimum(layer, last - 1)
            pltpu.make_async_remote_copy(
                src_ref=outbox.at[box], dst_ref=outbox.at[box],
                send_sem=peer_send.at[box], recv_sem=peer_recv.at[0, 0],
                device_id={"sample": lax.rem(group + 1, groups)}, device_id_type=MESH,
            ).wait_send()
        return carry

    lax.fori_loop(0, line, drain_layer, 0)

    def finish(piece, carry):
        def goals(goal, inner):
            pair_copy(goal, piece).wait_send()

            @pl.when(goal != place)
            def _():
                chain_copy(goal, goal, piece, above).wait_send()
            return inner

        lax.fori_loop(0, line, goals, 0)
        for k in range(1, groups):
            group_copy(piece, k).wait_send()
        return carry

    lax.fori_loop(0, PIECES, finish, 0)
    consume(PIECES - 1)

    def finish_out(piece, carry):
        out_copy(0, piece).wait()
        out_copy(1, piece).wait()
        return carry

    lax.fori_loop(0, PIECES, finish_out, 0)


def exchange(seed_step, attn, resid, cotangent, gain, mean, hess, scaling):
    line = lax.axis_size("fsdp") // 2
    groups = lax.axis_size("sample")
    tokens, width = resid.shape
    in_width = attn.shape[1]
    rows = mean.shape[0]
    part = width // PIECES
    quarter = rows // groups
    vmem = pl.BlockSpec(memory_space=pltpu.VMEM)
    hbm = pl.BlockSpec(memory_space=pl.ANY)
    dma = pltpu.SemaphoreType.DMA
    return pl.pallas_call(
        functools.partial(exchange_kernel, line, groups, scaling),
        out_shape=jax.ShapeDtypeStruct((2, rows, width), jnp.float32),
        in_specs=[pl.BlockSpec(memory_space=pltpu.SMEM), vmem, hbm, hbm, hbm, hbm, hbm],
        out_specs=hbm,
        scratch_shapes=[
            pltpu.VMEM((tokens, in_width), jnp.bfloat16),
            pltpu.VMEM((line, PIECES, 2 * rows, part), jnp.bfloat16),
            pltpu.VMEM((tokens, width), jnp.bfloat16),
            pltpu.VMEM((tokens, width), jnp.float32),
            pltpu.VMEM((line, PIECES, rows, part), jnp.bfloat16),
            pltpu.VMEM((line + 1, PIECES, rows, part), jnp.bfloat16),
            pltpu.VMEM((line, PIECES, 2, quarter, part), jnp.bfloat16),
            pltpu.VMEM((line - 1, PIECES, groups - 1, quarter, part), jnp.bfloat16),
            dma((2,)),
            dma((2, groups)),
            dma((line,)),
            dma((line,)),
            dma((line, PIECES)),
            dma((line - 1,)),
            dma((line, PIECES)),
            dma((line,)),
            dma((line, PIECES)),
            pltpu.SemaphoreType.REGULAR,
            dma((line, PIECES)),
            dma((line, PIECES)),
            dma((line, PIECES)),
            dma((line + 1, PIECES)),
            dma((groups, PIECES)),
            dma((PIECES,)),
            dma((2, PIECES)),
        ],
        compiler_params=pltpu.CompilerParams(
            collective_id=0, has_side_effects=True, vmem_limit_bytes=60 * 2**20
        ),
    )(seed_step, gain[None, :], attn, mean, hess, resid, cotangent)


def per_device(seed_step, attn, resid, cotangent, gain, mean, hess, momentum):
    in_width = attn.shape[1]
    scaling = in_width ** (-0.5)
    groups = lax.axis_size("sample")
    sums = exchange(seed_step, attn, resid, cotangent, gain, mean, hess, scaling)
    curv_sum = sums[1] * jnp.sqrt(ess_value * (hess + damping))
    return ivon_update(mean, hess, momentum, sums[0], curv_sum, groups)


def solution(mesh):
    placed = (
        P(),
        P(("sample", "fsdp"), None),
        P(("sample", "fsdp"), None),
        P(("sample", "fsdp"), None),
        P(),
        P("fsdp", None),
        P("fsdp", None),
        P("fsdp", None),
    )
    return jax.shard_map(
        per_device,
        mesh=mesh,
        in_specs=placed,
        out_specs=(P("fsdp", None), P("fsdp", None), P("fsdp", None)),
        check_vma=False,
    )
```

```python
import functools

import jax
import jax.numpy as jnp
from jax import lax
from jax.experimental import pallas as pl
from jax.experimental.pallas import tpu as pltpu
from jax.sharding import PartitionSpec as P

ess_value = 10.0
decay_first = 0.8
decay_second = 0.8
step_size = 0.3
damping = 0.1
norm_eps = 1e-05


noise_scale = 2.449489742783178

MESH = pl.DeviceIdType.MESH
PIECES = 8
PLAIN = 4
STRIP = 32


def noise_count(mixing, seed, key):
    shift = lax.shift_right_logical
    mixing = jnp.bitwise_xor(mixing, seed)
    mixing = mixing * 668265261 + key
    mixing = jnp.bitwise_xor(mixing, shift(mixing, 15))
    mixing = mixing * 739982445
    mixing = jnp.bitwise_xor(mixing, shift(mixing, 12))
    mixing = mixing * 695872825
    mixing = jnp.bitwise_xor(mixing, shift(mixing, 15))
    return (mixing & 4095) + (shift(mixing, 12) & 4095)


def noise_block(first, dims, width, seed, key):
    index = (
        lax.broadcasted_iota(jnp.int32, dims, 0) * width
        + lax.broadcasted_iota(jnp.int32, dims, 1)
        + first
    )
    count = noise_count(index, seed, key).astype(jnp.float32)
    return count * (noise_scale / 4096.0) + (noise_scale / 4096.0 - noise_scale)


def ivon_update(mean, hess, momentum, grad_sum, curv_sum, groups):
    grad_mean = grad_sum / groups
    hess_est = curv_sum / groups
    new_momentum = decay_first * momentum + (1.0 - decay_first) * grad_mean
    new_hess = (
        decay_second * hess
        + (1.0 - decay_second) * hess_est
        + 0.5 * (1.0 - decay_second) ** 2 * (hess - hess_est) ** 2 / (hess + damping)
    )
    new_mean = mean - step_size * (new_momentum + damping * mean) / (new_hess + damping)
    return (new_mean, new_hess, new_momentum)


def update_kernel(groups, mean, hess, momentum, sums, new_mean, new_hess, new_momentum):
    rows, width = mean.shape

    def some(c, carry):
        cs = pl.ds(pl.multiple_of(c * 512, 512), 512)
        old_hess = hess[:, cs]
        curv_sum = sums[1, :, cs].astype(jnp.float32) * jnp.sqrt(ess_value * (old_hess + damping))
        new_mean[:, cs], new_hess[:, cs], new_momentum[:, cs] = ivon_update(
            mean[:, cs], old_hess, momentum[:, cs], sums[0, :, cs].astype(jnp.float32),
            curv_sum, groups,
        )
        return carry

    lax.fori_loop(0, width // 512, some, 0)


def update(mean, hess, momentum, sums, groups):
    rows, width = mean.shape
    block = pl.BlockSpec((32, width), lambda i: (i, 0))
    return pl.pallas_call(
        functools.partial(update_kernel, groups),
        grid=(rows // 32,),
        out_shape=(jax.ShapeDtypeStruct(mean.shape, jnp.float32),) * 3,
        in_specs=[block, block, block, pl.BlockSpec((2, 32, width), lambda i: (0, i, 0))],
        out_specs=(block, block, block),
        compiler_params=pltpu.CompilerParams(vmem_limit_bytes=60 * 2**20),
    )(mean, hess, momentum, sums)


def exchange_kernel(
    line, groups, scaling,
    seed_step, gain, attn_in, mean, hess, resid, cotangent, out,
    attn, weights, back, total, paired, chained, settings, outbox,
    local_sem, own_sem, set_up, set_down, set_recv, peer_send, peer_recv,
    twin_send, twin_recv, free,
    pair_send, pair_recv, chain_send, chain_recv, share_send, share_recv,
    out_send, out_recv, keep_sem,
):
    group = lax.axis_index("sample")
    shard = lax.axis_index("fsdp")
    place = lax.div(shard, 2)
    core = lax.rem(shard, 2)
    twin = place * 2 + 1 - core
    rows, width = mean.shape
    tokens, in_width = attn.shape
    quarter = rows // groups
    part = width // PIECES
    strip = min(STRIP, quarter)
    last = line - 1
    above = lax.rem(place + 1, line) * 2 + core
    below = lax.rem(place + last, line) * 2 + core

    barrier = pltpu.get_barrier_semaphore()
    for other in (twin, above, below):
        pl.semaphore_signal(barrier, inc=1, device_id={"fsdp": other}, device_id_type=MESH)
    for step in range(1, groups):
        pl.semaphore_signal(
            barrier, inc=1, device_id={"sample": lax.rem(group + step, groups)}, device_id_type=MESH
        )

    def own_copy(which, k):
        rs = pl.ds(pl.multiple_of(k * quarter, quarter), quarter)
        to = pl.ds(pl.multiple_of(which * rows + k * quarter, quarter), quarter)
        return pltpu.make_async_copy(
            (mean, hess)[which].at[rs, :], total.at[to, :], own_sem.at[which, k]
        )

    def take_own(k, carry):
        own_copy(0, lax.rem(group + k, groups)).start()
        own_copy(1, lax.rem(group + k, groups)).start()
        return carry

    lax.fori_loop(0, groups, take_own, 0)
    take_attn = pltpu.make_async_copy(attn_in, attn, local_sem.at[1])
    take_attn.start()
    take_resid = pltpu.make_async_copy(resid, back, local_sem.at[0])
    take_resid.start()

    def wait_own(k, carry):
        own_copy(0, lax.rem(group + k, groups)).wait()
        own_copy(1, lax.rem(group + k, groups)).wait()
        return carry

    wait_own(0, 0)
    seed = seed_step[0]
    key = seed_step[1] * 374761393

    def low_sigma(value):
        return lax.rsqrt(ess_value * (value + damping)).astype(jnp.bfloat16)

    def piece_cols(h):
        return pl.ds(pl.multiple_of(h * part, part), part)

    def quarter_rows(which):
        return pl.ds(pl.multiple_of(core * rows + which * quarter, quarter), quarter)

    def set_copy(layer, h, send, other):
        return pltpu.make_async_remote_copy(
            src_ref=settings.at[layer, h],
            dst_ref=settings.at[layer, h],
            send_sem=send,
            recv_sem=set_recv.at[layer, h],
            device_id={"fsdp": other},
            device_id_type=MESH,
        )

    pl.semaphore_wait(barrier, groups + 2)

    def settle(h, carry):
        cs = piece_cols(h)
        at = pl.multiple_of(group * quarter, quarter)
        settings[place, h, 0] = total[pl.ds(at, quarter), cs].astype(jnp.bfloat16)
        settings[place, h, 1] = low_sigma(
            total[pl.ds(pl.multiple_of(rows + group * quarter, quarter), quarter), cs]
        )

        @pl.when(place < last)
        def _():
            set_copy(place, h, set_up.at[place], above).start()

        @pl.when(place > 0)
        def _():
            set_copy(place, h, set_down.at[place], below).start()
        return carry

    lax.fori_loop(0, PIECES, settle, 0)
    lax.fori_loop(1, groups, wait_own, 0)

    def twin_copy(layer, h):
        block = weights.at[layer, h, pl.ds(pl.multiple_of(core * rows, rows), rows)]
        return pltpu.make_async_remote_copy(
            src_ref=block,
            dst_ref=block,
            send_sem=twin_send.at[layer],
            recv_sem=twin_recv.at[layer, h],
            device_id={"fsdp": twin},
            device_id_type=MESH,
        )

    def first_index(g, layer, row, h):
        return (g * in_width + (layer * 2 + core) * rows + row) * width + h * part

    def sample_own(h):
        cs = piece_cols(h)

        def some(r, carry):
            at = r * strip
            mean_low = total[pl.ds(pl.multiple_of(at, strip), strip), cs].astype(jnp.bfloat16)
            sigma = low_sigma(total[pl.ds(pl.multiple_of(rows + at, strip), strip), cs])
            noise = noise_block(
                first_index(group, place, at, h), (strip, part), width, seed, key
            )
            weights[place, h, pl.ds(pl.multiple_of(core * rows + at, strip), strip)] = (
                mean_low.astype(jnp.float32) + sigma.astype(jnp.float32) * noise
            ).astype(jnp.bfloat16)
            return carry

        lax.fori_loop(0, rows // strip, some, 0)
        twin_copy(place, h).start()

    def box_of(layer):
        return layer - jnp.where(layer > place, 1, 0)

    def peer_copy(layer, h, k):
        return pltpu.make_async_remote_copy(
            src_ref=outbox.at[box_of(layer), h, k - 1],
            dst_ref=weights.at[layer, h, quarter_rows(group)],
            send_sem=peer_send.at[box_of(layer)],
            recv_sem=peer_recv.at[layer, h],
            device_id={"sample": lax.rem(group + k, groups)},
            device_id_type=MESH,
        )

    def produce(layer, h):
        def draw(g, r):
            rs = pl.ds(pl.multiple_of(r * strip, strip), strip)
            noise = noise_block(
                first_index(g, layer, group * quarter + r * strip, h),
                (strip, part), width, seed, key,
            )
            return (
                settings[layer, h, 0, rs].astype(jnp.float32)
                + settings[layer, h, 1, rs].astype(jnp.float32) * noise
            ).astype(jnp.bfloat16)

        def for_peer(k, carry):
            def some(r, inner):
                rs = pl.ds(pl.multiple_of(r * strip, strip), strip)
                outbox[box_of(layer), h, k - 1, rs] = draw(lax.rem(group + k, groups), r)
                return inner

            lax.fori_loop(0, quarter // strip, some, 0)
            peer_copy(layer, h, k).start()
            return carry

        lax.fori_loop(1, groups, for_peer, 0)

        def for_own(r, inner):
            at = pl.multiple_of(core * rows + group * quarter + r * strip, strip)
            weights[layer, h, pl.ds(at, strip)] = draw(group, r)
            return inner

        lax.fori_loop(0, quarter // strip, for_own, 0)

    def pass_to_twin(layer, h):
        some = pl.ds(pl.multiple_of(core * rows, rows), (groups - 1) * quarter)
        pltpu.make_async_remote_copy(
            src_ref=weights.at[layer, h, some],
            dst_ref=weights.at[layer, h, some],
            send_sem=peer_send.at[0],
            recv_sem=peer_recv.at[layer, h],
            device_id={"sample": lax.rem(group + 1, groups)},
            device_id_type=MESH,
        ).wait_recv()
        twin_copy(layer, h).start()

    def product(layer, h):
        twin_copy(layer, h).wait_recv()
        lhs = attn[:, pl.ds(pl.multiple_of(layer * 2 * rows, 2 * rows), 2 * rows)]
        return jnp.dot(lhs, weights[layer, h], preferred_element_type=jnp.float32)

    def multiply_own(h):
        cs = piece_cols(h)
        total[:, cs] = product(place, h) + back[:, cs].astype(jnp.float32) * (1.0 / scaling)

    def multiply(layer, h):
        total[:, piece_cols(h)] += product(layer, h)

    def both(i, action):
        t = lax.div(i, PIECES)
        h = lax.rem(i, PIECES)
        low = place - 1 - t
        high = place + 1 + t

        @pl.when((i >= 0) & (low >= 0))
        def _():
            action(jnp.maximum(low, 0), h, True)

        @pl.when((i >= 0) & (high <= last))
        def _():
            action(jnp.minimum(high, last), h, False)

    def arrive(layer, h, upward):
        set_copy(layer, h, set_up.at[layer], above).wait_recv()
        if upward:
            @pl.when(place < last)
            def _():
                set_copy(layer, h, set_up.at[layer], above).start()
        else:
            @pl.when(place > 0)
            def _():
                set_copy(layer, h, set_down.at[layer], below).start()
        produce(layer, h)

    steps = last * PIECES

    def gather_step(i, carry):
        @pl.when(i < steps)
        def _():
            both(i, arrive)

        @pl.when(i < PIECES)
        def _():
            sample_own(jnp.minimum(i, PIECES - 1))

        @pl.when((i >= 1) & (i <= steps))
        def _():
            both(i - 1, lambda layer, h, upward: pass_to_twin(layer, h))

        @pl.when(i == 1)
        def _():
            take_attn.wait()
            take_resid.wait()

        @pl.when((i >= 1) & (i <= PIECES))
        def _():
            multiply_own(jnp.minimum(jnp.maximum(i - 1, 0), PIECES - 1))

        @pl.when(i == PIECES + 1)
        def _():
            pltpu.make_async_copy(cotangent, back, local_sem.at[0]).start()

        @pl.when(i >= 2)
        def _():
            both(i - 2, lambda layer, h, upward: multiply(layer, h))
        return carry

    lax.fori_loop(0, steps + 2, gather_step, 0)

    def drain_twin(layer, carry):
        block = weights.at[layer, :, pl.ds(pl.multiple_of(core * rows, rows), rows)]
        pltpu.make_async_remote_copy(
            src_ref=block,
            dst_ref=block,
            send_sem=twin_send.at[layer],
            recv_sem=twin_recv.at[layer, 0],
            device_id={"fsdp": twin},
            device_id_type=MESH,
        ).wait_send()
        return carry

    lax.fori_loop(0, line, drain_twin, 0)
    for step in range(1, groups):
        pl.semaphore_signal(
            free, inc=1, device_id={"sample": lax.rem(group + step, groups)}, device_id_type=MESH
        )

    pltpu.make_async_copy(cotangent, back, local_sem.at[0]).wait()
    span = 512

    def normalise(r, carry):
        sl = pl.ds(pl.multiple_of(r * 16, 16), 16)
        square = jnp.zeros((16, span), jnp.float32)
        cross = jnp.zeros((16, span), jnp.float32)
        for c in range(width // span):
            cs = pl.ds(c * span, span)
            value = total[sl, cs] * scaling
            upstream = gain[:, cs].astype(jnp.float32) * back[sl, cs].astype(jnp.float32)
            square = square + value * value
            cross = cross + value * upstream
        inverse = lax.rsqrt(jnp.sum(square, axis=-1, keepdims=True) * (1.0 / width) + norm_eps)
        slope = inverse * inverse * inverse * (
            jnp.sum(cross, axis=-1, keepdims=True) * (1.0 / width)
        )
        for c in range(width // span):
            cs = pl.ds(c * span, span)
            value = total[sl, cs] * scaling
            upstream = gain[:, cs].astype(jnp.float32) * back[sl, cs].astype(jnp.float32)
            back[sl, cs] = (inverse * upstream - value * slope).astype(jnp.bfloat16)
        return carry

    lax.fori_loop(0, tokens // 16, normalise, 0)

    def partial(block, piece):
        lhs = attn[:, pl.ds(pl.multiple_of(block * rows, rows), rows)]
        rhs = back[:, piece_cols(piece)]
        return (
            lax.dot_general(lhs, rhs, (((0,), (0,)), ((), ())), preferred_element_type=jnp.float32)
            * scaling
        )

    def pair_copy(goal, piece):
        return pltpu.make_async_remote_copy(
            src_ref=weights.at[goal, piece, pl.ds(0, rows)],
            dst_ref=paired.at[goal, piece],
            send_sem=pair_send.at[goal, piece],
            recv_sem=pair_recv.at[goal, piece],
            device_id={"fsdp": twin},
            device_id_type=MESH,
        )

    def give_twin(i, piece):
        goal = i
        weights[goal, piece, pl.ds(0, rows)] = partial(goal * 2 + 1 - core, piece).astype(
            jnp.bfloat16
        )
        pair_copy(goal, piece).start()
        return piece

    def drain_layer(layer, carry):
        @pl.when((place < last) & (layer <= place))
        def _():
            pltpu.make_async_remote_copy(
                src_ref=settings.at[layer], dst_ref=settings.at[layer],
                send_sem=set_up.at[layer], recv_sem=set_recv.at[layer, 0],
                device_id={"fsdp": above}, device_id_type=MESH,
            ).wait_send()

        @pl.when((place > 0) & (layer >= place))
        def _():
            pltpu.make_async_remote_copy(
                src_ref=settings.at[layer], dst_ref=settings.at[layer],
                send_sem=set_down.at[layer], recv_sem=set_recv.at[layer, 0],
                device_id={"fsdp": below}, device_id_type=MESH,
            ).wait_send()
        return carry

    def drain_peers(box, carry):
        pltpu.make_async_remote_copy(
            src_ref=outbox.at[box], dst_ref=outbox.at[box],
            send_sem=peer_send.at[box], recv_sem=peer_recv.at[0, 0],
            device_id={"sample": lax.rem(group + 1, groups)}, device_id_type=MESH,
        ).wait_send()
        return carry

    def chain_copy(goal, slot, piece, other):
        return pltpu.make_async_remote_copy(
            src_ref=chained.at[goal, piece],
            dst_ref=chained.at[slot, piece],
            send_sem=chain_send.at[goal, piece],
            recv_sem=chain_recv.at[slot, piece],
            device_id={"fsdp": other},
            device_id_type=MESH,
        )

    def sums_copy(goal, slot, piece, other):
        return pltpu.make_async_remote_copy(
            src_ref=chained.at[goal, piece, pl.ds(0, 2 * quarter)],
            dst_ref=chained.at[slot, piece, pl.ds(0, 2 * quarter)],
            send_sem=chain_send.at[goal, piece],
            recv_sem=chain_recv.at[slot, piece],
            device_id={"fsdp": other},
            device_id_type=MESH,
        )

    def own_term(goal, piece):
        pair_copy(goal, piece).wait_recv()
        return partial(goal * 2 + core, piece) + paired[goal, piece].astype(jnp.float32)

    def forward(goal, piece, first, slot, other):
        @pl.when(first)
        def _():
            chained[goal, piece] = own_term(goal, piece).astype(jnp.bfloat16)

        @pl.when(jnp.logical_not(first))
        def _():
            term = own_term(goal, piece)
            chain_copy(goal, goal, piece, other).wait_recv()
            chained[goal, piece] = (term + chained[goal, piece].astype(jnp.float32)).astype(
                jnp.bfloat16
            )

        chain_copy(goal, slot, piece, other).start()

    def share_rows(which):
        return pl.ds(pl.multiple_of(which * quarter, quarter), quarter)

    def inbox_rows(which):
        return pl.ds(pl.multiple_of(rows + which * quarter, quarter), quarter)

    def share_copy(layer, piece, k):
        other = lax.rem(group + k, groups)
        return pltpu.make_async_remote_copy(
            src_ref=paired.at[layer, piece, share_rows(other)],
            dst_ref=weights.at[layer, piece, inbox_rows(group)],
            send_sem=share_send.at[layer, piece],
            recv_sem=share_recv.at[layer, piece],
            device_id={"sample": other},
            device_id_type=MESH,
        )

    def share(layer, piece):
        for k in range(1, groups):
            share_copy(layer, piece, k).start()
        weights[layer, piece, inbox_rows(group)] = paired[layer, piece, share_rows(group)]

    def share_all(layer, piece):
        some = paired.at[layer, piece, pl.ds(0, (groups - 1) * quarter)]
        return pltpu.make_async_remote_copy(
            src_ref=some,
            dst_ref=some,
            send_sem=share_send.at[layer, piece],
            recv_sem=share_recv.at[layer, piece],
            device_id={"sample": lax.rem(group + 1, groups)},
            device_id_type=MESH,
        )

    def combine(layer, piece, store):
        share_all(layer, piece).wait_recv()

        def some(r, carry):
            at = r * strip
            grad_sum = jnp.zeros((strip, part), jnp.float32)
            curv_sum = jnp.zeros((strip, part), jnp.float32)
            for g in range(groups):
                grad = weights[
                    layer, piece, pl.ds(pl.multiple_of(rows + g * quarter + at, strip), strip)
                ].astype(jnp.float32)
                noise = noise_block(
                    first_index(g, layer, group * quarter + at, piece),
                    (strip, part), width, seed, key,
                )
                grad_sum = grad_sum + grad
                curv_sum = curv_sum + grad * noise
            store(at, grad_sum, curv_sum)
            return carry

        lax.fori_loop(0, quarter // strip, some, 0)

    def strip_rows(which, at):
        return pl.ds(pl.multiple_of(which * quarter + at, strip), strip)

    def forward_sums(goal, piece, first, slot, other):
        def store_first(at, grad_sum, curv_sum):
            chained[goal, piece, strip_rows(0, at)] = grad_sum.astype(jnp.bfloat16)
            chained[goal, piece, strip_rows(1, at)] = curv_sum.astype(jnp.bfloat16)

        def store_more(at, grad_sum, curv_sum):
            for which, value in ((0, grad_sum), (1, curv_sum)):
                rs = strip_rows(which, at)
                chained[goal, piece, rs] = (
                    value + chained[goal, piece, rs].astype(jnp.float32)
                ).astype(jnp.bfloat16)

        @pl.when(first)
        def _():
            combine(goal, piece, store_first)

        @pl.when(jnp.logical_not(first))
        def _():
            sums_copy(goal, goal, piece, other).wait_recv()
            combine(goal, piece, store_more)

        sums_copy(goal, slot, piece, other).start()

    def out_copy(piece, k):
        cs = piece_cols(piece)
        return pltpu.make_async_remote_copy(
            src_ref=settings.at[0, piece],
            dst_ref=out.at[:, group, :, cs],
            send_sem=out_send.at[piece],
            recv_sem=out_recv.at[piece],
            device_id={"sample": lax.rem(group + k, groups)},
            device_id_type=MESH,
        )

    def keep_copy(piece):
        return pltpu.make_async_copy(
            settings.at[0, piece], out.at[:, group, :, piece_cols(piece)], keep_sem.at[piece]
        )

    def publish(piece):
        for k in range(1, groups):
            out_copy(piece, k).start()
        keep_copy(piece).start()

    def close_plain(piece):
        term = own_term(place, piece)

        @pl.when(place > 0)
        def _():
            chain_copy(place, place, piece, below).wait_recv()

        @pl.when(place < last)
        def _():
            chain_copy(place, line, piece, above).wait_recv()

        paired[place, piece] = (
            term
            + chained[place, piece].astype(jnp.float32)
            + chained[line, piece].astype(jnp.float32)
        ).astype(jnp.bfloat16)
        share(place, piece)

    def settle_plain(piece):
        def store(at, grad_sum, curv_sum):
            rs = pl.ds(pl.multiple_of(at, strip), strip)
            settings[0, piece, 0, rs] = grad_sum.astype(jnp.bfloat16)
            settings[0, piece, 1, rs] = curv_sum.astype(jnp.bfloat16)

        combine(place, piece, store)
        publish(piece)

    def settle_sums(piece):
        @pl.when(place > 0)
        def _():
            sums_copy(place, place, piece, below).wait_recv()

        @pl.when(place < last)
        def _():
            sums_copy(place, line, piece, above).wait_recv()

        def store(at, grad_sum, curv_sum):
            for which, value in ((0, grad_sum), (1, curv_sum)):
                rs = strip_rows(which, at)
                settings[0, piece, which, pl.ds(pl.multiple_of(at, strip), strip)] = (
                    value
                    + chained[place, piece, rs].astype(jnp.float32)
                    + chained[line, piece, rs].astype(jnp.float32)
                ).astype(jnp.bfloat16)

        combine(place, piece, store)
        publish(piece)

    @pl.when(place == 0)
    def _():
        chained[0] = jnp.zeros(chained.shape[1:], chained.dtype)

    @pl.when(place == last)
    def _():
        chained[line] = jnp.zeros(chained.shape[1:], chained.dtype)

    lax.fori_loop(0, line, give_twin, 0)
    lax.fori_loop(0, line, drain_layer, 0)

    def moves(step, count, send):
        up_at = step - place
        up_piece = lax.div(jnp.maximum(up_at, 0), last)
        up_goal = last - lax.rem(jnp.maximum(up_at, 0), last)

        @pl.when((up_at >= 0) & (up_piece < count) & (up_goal > place))
        def _():
            send(up_goal, up_piece, place == 0, up_goal, above)

        down_at = step - (last - place)
        down_piece = lax.div(jnp.maximum(down_at, 0), last)
        down_goal = lax.rem(jnp.maximum(down_at, 0), last)

        @pl.when((down_at >= 0) & (down_piece < count) & (down_goal < place))
        def _():
            slot = jnp.where(down_goal == place - 1, line, down_goal)
            send(down_goal, down_piece, place == last, slot, below)

    def share_layer(layer, piece):
        paired[layer, piece] = own_term(layer, piece).astype(jnp.bfloat16)
        share(layer, piece)
        return piece

    def plain_step(step, carry):
        moves(step, PLAIN, forward)
        turn = lax.div(step, last)
        phase = lax.rem(step, last)

        @pl.when((phase == 0) & (turn < PLAIN - 1))
        def _():
            lax.fori_loop(0, line, give_twin, turn + 1)

        @pl.when((phase == 0) & (turn < PIECES - PLAIN))
        def _():
            lax.fori_loop(0, line, give_twin, PLAIN + turn)

        @pl.when((phase == 0) & (turn >= 1))
        def _():
            close_plain(jnp.maximum(turn - 1, 0))

        @pl.when((phase == 0) & (turn >= 2))
        def _():
            settle_plain(jnp.maximum(turn - 2, 0))

        @pl.when((phase == 1) & (turn < PIECES - PLAIN))
        def _():
            @pl.when(turn == 0)
            def _():
                pl.semaphore_wait(free, groups - 1)

            lax.fori_loop(0, line, share_layer, PLAIN + turn)
        return carry

    lax.fori_loop(0, PLAIN * last + 1, plain_step, 0)

    def sums_step(step, carry):
        moves(
            step,
            PIECES - PLAIN,
            lambda goal, piece, *rest: forward_sums(goal, piece + PLAIN, *rest),
        )
        turn = lax.div(step, last)
        phase = lax.rem(step, last)

        @pl.when(step == 1)
        def _():
            settle_plain(PLAIN - 1)

        @pl.when((phase == 0) & (turn >= 1))
        def _():
            settle_sums(PLAIN + jnp.maximum(turn - 1, 0))
        return carry

    lax.fori_loop(0, (PIECES - PLAIN) * last + 1, sums_step, 0)
    lax.fori_loop(0, last, drain_peers, 0)

    def finish(piece, carry):
        def goals(goal, inner):
            pair_copy(goal, piece).wait_send()

            @pl.when((goal != place) & (piece < PLAIN))
            def _():
                chain_copy(goal, goal, piece, above).wait_send()

            @pl.when((goal != place) & (piece >= PLAIN))
            def _():
                sums_copy(goal, goal, piece, above).wait_send()

            @pl.when((goal == place) | (piece >= PLAIN))
            def _():
                share_all(goal, piece).wait_send()
            return inner

        lax.fori_loop(0, line, goals, 0)
        return carry

    lax.fori_loop(0, PIECES, finish, 0)

    def finish_out(piece, carry):
        keep_copy(piece).wait()
        everything = out.at[:, pl.ds(0, groups - 1), :, piece_cols(piece)]
        arrived = pltpu.make_async_remote_copy(
            src_ref=everything,
            dst_ref=everything,
            send_sem=out_send.at[piece],
            recv_sem=out_recv.at[piece],
            device_id={"sample": lax.rem(group + 1, groups)},
            device_id_type=MESH,
        )
        arrived.wait_send()
        arrived.wait_recv()
        return carry

    lax.fori_loop(0, PIECES, finish_out, 0)


def exchange(seed_step, attn, resid, cotangent, gain, mean, hess, scaling):
    line = lax.axis_size("fsdp") // 2
    groups = lax.axis_size("sample")
    tokens, width = resid.shape
    in_width = attn.shape[1]
    rows = mean.shape[0]
    part = width // PIECES
    quarter = rows // groups
    vmem = pl.BlockSpec(memory_space=pltpu.VMEM)
    hbm = pl.BlockSpec(memory_space=pl.ANY)
    dma = pltpu.SemaphoreType.DMA
    return pl.pallas_call(
        functools.partial(exchange_kernel, line, groups, scaling),
        out_shape=jax.ShapeDtypeStruct((2, groups, quarter, width), jnp.bfloat16),
        in_specs=[pl.BlockSpec(memory_space=pltpu.SMEM), vmem, hbm, hbm, hbm, hbm, hbm],
        out_specs=hbm,
        scratch_shapes=[
            pltpu.VMEM((tokens, in_width), jnp.bfloat16),
            pltpu.VMEM((line, PIECES, 2 * rows, part), jnp.bfloat16),
            pltpu.VMEM((tokens, width), jnp.bfloat16),
            pltpu.VMEM((tokens, width), jnp.float32),
            pltpu.VMEM((line, PIECES, rows, part), jnp.bfloat16),
            pltpu.VMEM((line + 1, PIECES, rows, part), jnp.bfloat16),
            pltpu.VMEM((line, PIECES, 2, quarter, part), jnp.bfloat16),
            pltpu.VMEM((line - 1, PIECES, groups - 1, quarter, part), jnp.bfloat16),
            dma((2,)),
            dma((2, groups)),
            dma((line,)),
            dma((line,)),
            dma((line, PIECES)),
            dma((line - 1,)),
            dma((line, PIECES)),
            dma((line,)),
            dma((line, PIECES)),
            pltpu.SemaphoreType.REGULAR,
            dma((line, PIECES)),
            dma((line, PIECES)),
            dma((line, PIECES)),
            dma((line + 1, PIECES)),
            dma((line, PIECES)),
            dma((line, PIECES)),
            dma((PIECES,)),
            dma((PIECES,)),
            dma((PIECES,)),
        ],
        compiler_params=pltpu.CompilerParams(
            collective_id=0, has_side_effects=True, vmem_limit_bytes=60 * 2**20
        ),
    )(seed_step, gain[None, :], attn, mean, hess, resid, cotangent)


def per_device(seed_step, attn, resid, cotangent, gain, mean, hess, momentum):
    in_width = attn.shape[1]
    scaling = in_width ** (-0.5)
    groups = lax.axis_size("sample")
    sums = exchange(seed_step, attn, resid, cotangent, gain, mean, hess, scaling)
    return update(mean, hess, momentum, sums.reshape((2,) + mean.shape), groups)


def solution(mesh):
    placed = (
        P(),
        P(("sample", "fsdp"), None),
        P(("sample", "fsdp"), None),
        P(("sample", "fsdp"), None),
        P(),
        P("fsdp", None),
        P("fsdp", None),
        P("fsdp", None),
    )
    return jax.shard_map(
        per_device,
        mesh=mesh,
        in_specs=placed,
        out_specs=(P("fsdp", None), P("fsdp", None), P("fsdp", None)),
        check_vma=False,
    )
```

```python
import functools

import jax
import jax.numpy as jnp
from jax import lax
from jax.experimental import pallas as pl
from jax.experimental.pallas import tpu as pltpu
from jax.sharding import PartitionSpec as P

ess_value = 10.0
decay_first = 0.8
decay_second = 0.8
step_size = 0.3
damping = 0.1
norm_eps = 1e-05


noise_scale = 2.449489742783178

MESH = pl.DeviceIdType.MESH
PIECES = 8
PLAIN = 4
CLOSE_LAG = 0
SETTLE_LAG = 0
SUMS_LAG = 1
STRIP = 32


def noise_count(mixing, seed, key):
    shift = lax.shift_right_logical
    mixing = jnp.bitwise_xor(mixing, seed)
    mixing = mixing * 668265261 + key
    mixing = jnp.bitwise_xor(mixing, shift(mixing, 15))
    mixing = mixing * 739982445
    mixing = jnp.bitwise_xor(mixing, shift(mixing, 12))
    mixing = mixing * 695872825
    mixing = jnp.bitwise_xor(mixing, shift(mixing, 15))
    return (mixing & 4095) + (shift(mixing, 12) & 4095)


def noise_block(first, dims, width, seed, key):
    index = (
        lax.broadcasted_iota(jnp.int32, dims, 0) * width
        + lax.broadcasted_iota(jnp.int32, dims, 1)
        + first
    )
    count = noise_count(index, seed, key).astype(jnp.float32)
    return count * (noise_scale / 4096.0) + (noise_scale / 4096.0 - noise_scale)


def ivon_update(mean, hess, momentum, grad_sum, curv_sum, groups):
    inverse = lax.rsqrt(ess_value * (hess + damping))
    grad_mean = grad_sum * (1.0 / groups)
    hess_est = curv_sum * (1.0 / groups) * (ess_value * (hess + damping) * inverse)
    new_momentum = decay_first * momentum + (1.0 - decay_first) * grad_mean
    new_hess = (
        decay_second * hess
        + (1.0 - decay_second) * hess_est
        + 0.5 * (1.0 - decay_second) ** 2 * ess_value * ((hess - hess_est) * inverse) ** 2
    )
    new_mean = mean - step_size * (new_momentum + damping * mean) / (new_hess + damping)
    return (new_mean, new_hess, new_momentum)


def update_kernel(groups, mean, hess, momentum, sums, new_mean, new_hess, new_momentum):
    rows, width = mean.shape

    def some(c, carry):
        cs = pl.ds(pl.multiple_of(c * 512, 512), 512)
        new_mean[:, cs], new_hess[:, cs], new_momentum[:, cs] = ivon_update(
            mean[:, cs], hess[:, cs], momentum[:, cs], sums[0, :, cs].astype(jnp.float32),
            sums[1, :, cs].astype(jnp.float32), groups,
        )
        return carry

    lax.fori_loop(0, width // 512, some, 0)


def update(mean, hess, momentum, sums, groups):
    rows, width = mean.shape
    height = min(64, rows)
    block = pl.BlockSpec((height, width), lambda i: (i, 0))
    return pl.pallas_call(
        functools.partial(update_kernel, groups),
        grid=(rows // height,),
        out_shape=(jax.ShapeDtypeStruct(mean.shape, jnp.float32),) * 3,
        in_specs=[block, block, block, pl.BlockSpec((2, height, width), lambda i: (0, i, 0))],
        out_specs=(block, block, block),
        compiler_params=pltpu.CompilerParams(vmem_limit_bytes=60 * 2**20),
    )(mean, hess, momentum, sums)


def exchange_kernel(
    line, groups, scaling,
    seed_step, gain_rows, attn_in, mean, hess, resid, cotangent, out,
    gain, square, cross, attn, weights, back, total, paired, chained, settings, outbox,
    local_sem, own_sem, set_up, set_down, set_recv, peer_send, peer_recv,
    twin_send, twin_recv, free,
    pair_send, pair_recv, chain_send, chain_recv, share_send, share_recv,
    out_send, out_recv, keep_sem,
):
    group = lax.axis_index("sample")
    shard = lax.axis_index("fsdp")
    place = lax.div(shard, 2)
    core = lax.rem(shard, 2)
    twin = place * 2 + 1 - core
    rows, width = mean.shape
    tokens, in_width = attn.shape
    quarter = rows // groups
    part = width // PIECES
    strip = min(STRIP, quarter)
    last = line - 1
    above = lax.rem(place + 1, line) * 2 + core
    below = lax.rem(place + last, line) * 2 + core

    barrier = pltpu.get_barrier_semaphore()
    for other in (twin, above, below):
        pl.semaphore_signal(barrier, inc=1, device_id={"fsdp": other}, device_id_type=MESH)
    for step in range(1, groups):
        pl.semaphore_signal(
            barrier, inc=1, device_id={"sample": lax.rem(group + step, groups)}, device_id_type=MESH
        )

    def own_copy(which, k):
        rs = pl.ds(pl.multiple_of(k * quarter, quarter), quarter)
        to = pl.ds(pl.multiple_of(which * rows + k * quarter, quarter), quarter)
        return pltpu.make_async_copy(
            (mean, hess)[which].at[rs, :], total.at[to, :], own_sem.at[which, k]
        )

    def take_own(k, carry):
        own_copy(0, lax.rem(group + k, groups)).start()
        own_copy(1, lax.rem(group + k, groups)).start()
        return carry

    lax.fori_loop(0, groups, take_own, 0)
    take_attn = pltpu.make_async_copy(attn_in, attn, local_sem.at[1])
    take_attn.start()
    take_resid = pltpu.make_async_copy(resid, back, local_sem.at[0])
    take_resid.start()

    def wait_own(k, carry):
        own_copy(0, lax.rem(group + k, groups)).wait()
        own_copy(1, lax.rem(group + k, groups)).wait()
        return carry

    wait_own(0, 0)
    seed = seed_step[0]
    key = seed_step[1] * 374761393

    def low_sigma(value):
        return lax.rsqrt(ess_value * (value + damping)).astype(jnp.bfloat16)

    def piece_cols(h):
        return pl.ds(pl.multiple_of(h * part, part), part)

    def quarter_rows(which):
        return pl.ds(pl.multiple_of(core * rows + which * quarter, quarter), quarter)

    def set_copy(layer, h, send, other):
        return pltpu.make_async_remote_copy(
            src_ref=settings.at[layer, h],
            dst_ref=settings.at[layer, h],
            send_sem=send,
            recv_sem=set_recv.at[layer, h],
            device_id={"fsdp": other},
            device_id_type=MESH,
        )

    pl.semaphore_wait(barrier, groups + 2)

    def settle(h, carry):
        cs = piece_cols(h)
        at = pl.multiple_of(group * quarter, quarter)
        settings[place, h, 0] = total[pl.ds(at, quarter), cs].astype(jnp.bfloat16)
        settings[place, h, 1] = low_sigma(
            total[pl.ds(pl.multiple_of(rows + group * quarter, quarter), quarter), cs]
        )

        @pl.when(place < last)
        def _():
            set_copy(place, h, set_up.at[place], above).start()

        @pl.when(place > 0)
        def _():
            set_copy(place, h, set_down.at[place], below).start()
        return carry

    lax.fori_loop(0, PIECES, settle, 0)
    for k in range(width // 128):
        gain[:, k * 128 : (k + 1) * 128] = gain_rows[k : k + 1, :].astype(jnp.float32)
    lax.fori_loop(1, groups, wait_own, 0)
    square[...] = jnp.zeros(square.shape, square.dtype)
    cross[...] = jnp.zeros(cross.shape, cross.dtype)

    def twin_copy(layer, h):
        block = weights.at[layer, h, pl.ds(pl.multiple_of(core * rows, rows), rows)]
        return pltpu.make_async_remote_copy(
            src_ref=block,
            dst_ref=block,
            send_sem=twin_send.at[layer],
            recv_sem=twin_recv.at[layer, h],
            device_id={"fsdp": twin},
            device_id_type=MESH,
        )

    def first_index(g, layer, row, h):
        return (g * in_width + (layer * 2 + core) * rows + row) * width + h * part

    def sample_own(h):
        cs = piece_cols(h)

        def some(r, carry):
            at = r * strip
            mean_low = total[pl.ds(pl.multiple_of(at, strip), strip), cs].astype(jnp.bfloat16)
            sigma = low_sigma(total[pl.ds(pl.multiple_of(rows + at, strip), strip), cs])
            noise = noise_block(
                first_index(group, place, at, h), (strip, part), width, seed, key
            )
            weights[place, h, pl.ds(pl.multiple_of(core * rows + at, strip), strip)] = (
                mean_low.astype(jnp.float32) + sigma.astype(jnp.float32) * noise
            ).astype(jnp.bfloat16)
            return carry

        lax.fori_loop(0, rows // strip, some, 0)
        twin_copy(place, h).start()

    def box_of(layer):
        return layer - jnp.where(layer > place, 1, 0)

    def peer_copy(layer, h, k):
        return pltpu.make_async_remote_copy(
            src_ref=outbox.at[box_of(layer), h, k - 1],
            dst_ref=weights.at[layer, h, quarter_rows(group)],
            send_sem=peer_send.at[box_of(layer)],
            recv_sem=peer_recv.at[layer, h],
            device_id={"sample": lax.rem(group + k, groups)},
            device_id_type=MESH,
        )

    def produce(layer, h):
        def draw(g, r):
            rs = pl.ds(pl.multiple_of(r * strip, strip), strip)
            noise = noise_block(
                first_index(g, layer, group * quarter + r * strip, h),
                (strip, part), width, seed, key,
            )
            return (
                settings[layer, h, 0, rs].astype(jnp.float32)
                + settings[layer, h, 1, rs].astype(jnp.float32) * noise
            ).astype(jnp.bfloat16)

        def for_peer(k, carry):
            def some(r, inner):
                rs = pl.ds(pl.multiple_of(r * strip, strip), strip)
                outbox[box_of(layer), h, k - 1, rs] = draw(lax.rem(group + k, groups), r)
                return inner

            lax.fori_loop(0, quarter // strip, some, 0)
            peer_copy(layer, h, k).start()
            return carry

        lax.fori_loop(1, groups, for_peer, 0)

        def for_own(r, inner):
            at = pl.multiple_of(core * rows + group * quarter + r * strip, strip)
            weights[layer, h, pl.ds(at, strip)] = draw(group, r)
            return inner

        lax.fori_loop(0, quarter // strip, for_own, 0)

    def pass_to_twin(layer, h):
        some = pl.ds(pl.multiple_of(core * rows, rows), (groups - 1) * quarter)
        pltpu.make_async_remote_copy(
            src_ref=weights.at[layer, h, some],
            dst_ref=weights.at[layer, h, some],
            send_sem=peer_send.at[0],
            recv_sem=peer_recv.at[layer, h],
            device_id={"sample": lax.rem(group + 1, groups)},
            device_id_type=MESH,
        ).wait_recv()
        twin_copy(layer, h).start()

    def product(layer, h):
        twin_copy(layer, h).wait_recv()
        lhs = attn[:, pl.ds(pl.multiple_of(layer * 2 * rows, 2 * rows), 2 * rows)]
        return jnp.dot(lhs, weights[layer, h], preferred_element_type=jnp.float32)

    def multiply_own(h):
        cs = piece_cols(h)
        total[:, cs] = product(place, h) + back[:, cs].astype(jnp.float32) * (1.0 / scaling)

    def multiply(layer, h):
        total[:, piece_cols(h)] += product(layer, h)

    def both(i, action):
        t = lax.div(i, PIECES)
        h = lax.rem(i, PIECES)
        low = place - 1 - t
        high = place + 1 + t

        @pl.when((i >= 0) & (low >= 0))
        def _():
            action(jnp.maximum(low, 0), h, True)

        @pl.when((i >= 0) & (high <= last))
        def _():
            action(jnp.minimum(high, last), h, False)

    def arrive(layer, h, upward):
        set_copy(layer, h, set_up.at[layer], above).wait_recv()
        if upward:
            @pl.when(place < last)
            def _():
                set_copy(layer, h, set_up.at[layer], above).start()
        else:
            @pl.when(place > 0)
            def _():
                set_copy(layer, h, set_down.at[layer], below).start()
        produce(layer, h)

    @pl.when(place == 0)
    def _():
        chained[0] = jnp.zeros(chained.shape[1:], chained.dtype)

    @pl.when(place == last)
    def _():
        chained[line] = jnp.zeros(chained.shape[1:], chained.dtype)

    steps = last * PIECES
    farthest = jnp.maximum(place, last - place) - 1

    def add_stats(h):
        cs = piece_cols(h)

        def some(r, carry):
            sl = pl.ds(pl.multiple_of(r * 32, 32), 32)
            value = total[sl, cs] * scaling
            upstream = gain[:, cs] * back[sl, cs].astype(jnp.float32)
            more = value * value
            mixed = value * upstream
            square[sl] += sum(more[:, k : k + 128] for k in range(0, part, 128))
            cross[sl] += sum(mixed[:, k : k + 128] for k in range(0, part, 128))
            return carry

        lax.fori_loop(0, tokens // 32, some, 0)

    def gather_step(i, carry):
        @pl.when(i < steps)
        def _():
            both(i, arrive)

        @pl.when(i < PIECES)
        def _():
            sample_own(jnp.minimum(i, PIECES - 1))

        @pl.when((i >= 1) & (i <= steps))
        def _():
            both(i - 1, lambda layer, h, upward: pass_to_twin(layer, h))

        @pl.when(i == 1)
        def _():
            take_attn.wait()
            take_resid.wait()

        @pl.when((i >= 1) & (i <= PIECES))
        def _():
            multiply_own(jnp.minimum(jnp.maximum(i - 1, 0), PIECES - 1))

        @pl.when(i == PIECES + 1)
        def _():
            pltpu.make_async_copy(cotangent, back, local_sem.at[0]).start()

        @pl.when(i >= 2)
        def _():
            both(i - 2, lambda layer, h, upward: multiply(layer, h))

            @pl.when(i == farthest * PIECES + 2)
            def _():
                pltpu.make_async_copy(cotangent, back, local_sem.at[0]).wait()

            @pl.when(lax.div(i - 2, PIECES) == farthest)
            def _():
                add_stats(lax.rem(i - 2, PIECES))
        return carry

    lax.fori_loop(0, steps + 2, gather_step, 0)

    def drain_twin(layer, carry):
        block = weights.at[layer, :, pl.ds(pl.multiple_of(core * rows, rows), rows)]
        pltpu.make_async_remote_copy(
            src_ref=block,
            dst_ref=block,
            send_sem=twin_send.at[layer],
            recv_sem=twin_recv.at[layer, 0],
            device_id={"fsdp": twin},
            device_id_type=MESH,
        ).wait_send()
        return carry

    lax.fori_loop(0, line, drain_twin, 0)
    for step in range(1, groups):
        pl.semaphore_signal(
            free, inc=1, device_id={"sample": lax.rem(group + step, groups)}, device_id_type=MESH
        )

    def finish_stats(r, carry):
        sl = pl.ds(pl.multiple_of(r * 64, 64), 64)
        scale = 1.0 / width
        inverse = lax.rsqrt(jnp.sum(square[sl], axis=-1, keepdims=True) * scale + norm_eps)
        slope = inverse * inverse * inverse * (jnp.sum(cross[sl], axis=-1, keepdims=True) * scale)
        square[sl] = jnp.broadcast_to(inverse, (64, 128))
        cross[sl] = jnp.broadcast_to(slope, (64, 128))
        return carry

    lax.fori_loop(0, tokens // 64, finish_stats, 0)

    def normalise(piece):
        cs = piece_cols(piece)

        def some(r, carry):
            sl = pl.ds(pl.multiple_of(r * 32, 32), 32)
            inverse = square[sl, 0:1]
            slope = cross[sl, 0:1] * scaling
            upstream = gain[:, cs] * back[sl, cs].astype(jnp.float32)
            back[sl, cs] = (inverse * upstream - total[sl, cs] * slope).astype(jnp.bfloat16)
            return carry

        lax.fori_loop(0, tokens // 32, some, 0)

    def partial(block, piece):
        lhs = attn[:, pl.ds(pl.multiple_of(block * rows, rows), rows)]
        rhs = back[:, piece_cols(piece)]
        return (
            lax.dot_general(lhs, rhs, (((0,), (0,)), ((), ())), preferred_element_type=jnp.float32)
            * scaling
        )

    def pair_copy(goal, piece):
        return pltpu.make_async_remote_copy(
            src_ref=weights.at[goal, piece, pl.ds(0, rows)],
            dst_ref=paired.at[goal, piece],
            send_sem=pair_send.at[goal, piece],
            recv_sem=pair_recv.at[goal, piece],
            device_id={"fsdp": twin},
            device_id_type=MESH,
        )

    def give_twin(i, piece):
        goal = jnp.where(place * 2 < line, last - i, i)
        weights[goal, piece, pl.ds(0, rows)] = partial(goal * 2 + 1 - core, piece).astype(
            jnp.bfloat16
        )
        pair_copy(goal, piece).start()
        return piece

    def drain_layer(layer, carry):
        @pl.when((place < last) & (layer <= place))
        def _():
            pltpu.make_async_remote_copy(
                src_ref=settings.at[layer], dst_ref=settings.at[layer],
                send_sem=set_up.at[layer], recv_sem=set_recv.at[layer, 0],
                device_id={"fsdp": above}, device_id_type=MESH,
            ).wait_send()

        @pl.when((place > 0) & (layer >= place))
        def _():
            pltpu.make_async_remote_copy(
                src_ref=settings.at[layer], dst_ref=settings.at[layer],
                send_sem=set_down.at[layer], recv_sem=set_recv.at[layer, 0],
                device_id={"fsdp": below}, device_id_type=MESH,
            ).wait_send()
        return carry

    def drain_peers(box, carry):
        pltpu.make_async_remote_copy(
            src_ref=outbox.at[box], dst_ref=outbox.at[box],
            send_sem=peer_send.at[box], recv_sem=peer_recv.at[0, 0],
            device_id={"sample": lax.rem(group + 1, groups)}, device_id_type=MESH,
        ).wait_send()
        return carry

    def chain_copy(goal, slot, piece, other):
        return pltpu.make_async_remote_copy(
            src_ref=chained.at[goal, piece],
            dst_ref=chained.at[slot, piece],
            send_sem=chain_send.at[goal, piece],
            recv_sem=chain_recv.at[slot, piece],
            device_id={"fsdp": other},
            device_id_type=MESH,
        )

    def sums_copy(goal, slot, piece, other):
        return pltpu.make_async_remote_copy(
            src_ref=chained.at[goal, piece, pl.ds(0, 2 * quarter)],
            dst_ref=chained.at[slot, piece, pl.ds(0, 2 * quarter)],
            send_sem=chain_send.at[goal, piece],
            recv_sem=chain_recv.at[slot, piece],
            device_id={"fsdp": other},
            device_id_type=MESH,
        )

    def own_term(goal, piece):
        pair_copy(goal, piece).wait_recv()
        return partial(goal * 2 + core, piece) + paired[goal, piece].astype(jnp.float32)

    def forward(goal, piece, first, slot, other):
        @pl.when(first)
        def _():
            chained[goal, piece] = own_term(goal, piece).astype(jnp.bfloat16)

        @pl.when(jnp.logical_not(first))
        def _():
            term = own_term(goal, piece)
            chain_copy(goal, goal, piece, other).wait_recv()
            chained[goal, piece] = (term + chained[goal, piece].astype(jnp.float32)).astype(
                jnp.bfloat16
            )

        chain_copy(goal, slot, piece, other).start()

    def share_rows(which):
        return pl.ds(pl.multiple_of(which * quarter, quarter), quarter)

    def inbox_rows(which):
        return pl.ds(pl.multiple_of(rows + which * quarter, quarter), quarter)

    def share_copy(layer, piece, k):
        other = lax.rem(group + k, groups)
        return pltpu.make_async_remote_copy(
            src_ref=paired.at[layer, piece, share_rows(other)],
            dst_ref=weights.at[layer, piece, inbox_rows(group)],
            send_sem=share_send.at[layer, piece],
            recv_sem=share_recv.at[layer, piece],
            device_id={"sample": other},
            device_id_type=MESH,
        )

    def share(layer, piece):
        for k in range(1, groups):
            share_copy(layer, piece, k).start()
        weights[layer, piece, inbox_rows(group)] = paired[layer, piece, share_rows(group)]

    def share_all(layer, piece):
        some = paired.at[layer, piece, pl.ds(0, (groups - 1) * quarter)]
        return pltpu.make_async_remote_copy(
            src_ref=some,
            dst_ref=some,
            send_sem=share_send.at[layer, piece],
            recv_sem=share_recv.at[layer, piece],
            device_id={"sample": lax.rem(group + 1, groups)},
            device_id_type=MESH,
        )

    def combine(layer, piece, store):
        share_all(layer, piece).wait_recv()

        def some(r, carry):
            at = r * strip
            grad_sum = jnp.zeros((strip, part), jnp.float32)
            curv_sum = jnp.zeros((strip, part), jnp.float32)
            for g in range(groups):
                grad = weights[
                    layer, piece, pl.ds(pl.multiple_of(rows + g * quarter + at, strip), strip)
                ].astype(jnp.float32)
                noise = noise_block(
                    first_index(g, layer, group * quarter + at, piece),
                    (strip, part), width, seed, key,
                )
                grad_sum = grad_sum + grad
                curv_sum = curv_sum + grad * noise
            store(at, grad_sum, curv_sum)
            return carry

        lax.fori_loop(0, quarter // strip, some, 0)

    def strip_rows(which, at):
        return pl.ds(pl.multiple_of(which * quarter + at, strip), strip)

    def forward_sums(goal, piece, first, slot, other):
        def store_first(at, grad_sum, curv_sum):
            chained[goal, piece, strip_rows(0, at)] = grad_sum.astype(jnp.bfloat16)
            chained[goal, piece, strip_rows(1, at)] = curv_sum.astype(jnp.bfloat16)

        def store_more(at, grad_sum, curv_sum):
            for which, value in ((0, grad_sum), (1, curv_sum)):
                rs = strip_rows(which, at)
                chained[goal, piece, rs] = (
                    value + chained[goal, piece, rs].astype(jnp.float32)
                ).astype(jnp.bfloat16)

        @pl.when(first)
        def _():
            combine(goal, piece, store_first)

        @pl.when(jnp.logical_not(first))
        def _():
            sums_copy(goal, goal, piece, other).wait_recv()
            combine(goal, piece, store_more)

        sums_copy(goal, slot, piece, other).start()

    def out_copy(piece, k):
        cs = piece_cols(piece)
        return pltpu.make_async_remote_copy(
            src_ref=settings.at[0, piece],
            dst_ref=out.at[:, group, :, cs],
            send_sem=out_send.at[piece],
            recv_sem=out_recv.at[piece],
            device_id={"sample": lax.rem(group + k, groups)},
            device_id_type=MESH,
        )

    def keep_copy(piece):
        return pltpu.make_async_copy(
            settings.at[0, piece], out.at[:, group, :, piece_cols(piece)], keep_sem.at[piece]
        )

    def publish(piece):
        for k in range(1, groups):
            out_copy(piece, k).start()
        keep_copy(piece).start()

    def close_plain(piece):
        term = own_term(place, piece)

        @pl.when(place > 0)
        def _():
            chain_copy(place, place, piece, below).wait_recv()

        @pl.when(place < last)
        def _():
            chain_copy(place, line, piece, above).wait_recv()

        paired[place, piece] = (
            term
            + chained[place, piece].astype(jnp.float32)
            + chained[line, piece].astype(jnp.float32)
        ).astype(jnp.bfloat16)
        share(place, piece)

    def settle_plain(piece):
        def store(at, grad_sum, curv_sum):
            rs = pl.ds(pl.multiple_of(at, strip), strip)
            settings[0, piece, 0, rs] = grad_sum.astype(jnp.bfloat16)
            settings[0, piece, 1, rs] = curv_sum.astype(jnp.bfloat16)

        combine(place, piece, store)
        publish(piece)

    def settle_sums(piece):
        @pl.when(place > 0)
        def _():
            sums_copy(place, place, piece, below).wait_recv()

        @pl.when(place < last)
        def _():
            sums_copy(place, line, piece, above).wait_recv()

        def store(at, grad_sum, curv_sum):
            for which, value in ((0, grad_sum), (1, curv_sum)):
                rs = strip_rows(which, at)
                settings[0, piece, which, pl.ds(pl.multiple_of(at, strip), strip)] = (
                    value
                    + chained[place, piece, rs].astype(jnp.float32)
                    + chained[line, piece, rs].astype(jnp.float32)
                ).astype(jnp.bfloat16)

        combine(place, piece, store)
        publish(piece)

    def give_piece(piece):
        normalise(piece)
        lax.fori_loop(0, line, give_twin, piece)

    give_piece(0)
    lax.fori_loop(0, line, drain_layer, 0)

    def send_on(goal, piece, first, slot, other):
        @pl.when(piece < PLAIN)
        def _():
            forward(goal, jnp.minimum(piece, PLAIN - 1), first, slot, other)

        @pl.when(piece >= PLAIN)
        def _():
            forward_sums(goal, jnp.maximum(piece, PLAIN), first, slot, other)

    def share_layer(layer, piece):
        paired[layer, piece] = own_term(layer, piece).astype(jnp.bfloat16)
        share(layer, piece)
        return piece

    def at_turn(step, lag, first, stop, action):
        turn = lax.div(jnp.maximum(step - lag, 0), last)
        phase = lax.rem(jnp.maximum(step - lag, 0), last)

        @pl.when((step >= lag) & (phase == 0) & (turn >= first) & (turn < stop))
        def _():
            action(turn)

    def reduce_step(step, carry):
        up_at = step - place
        up_piece = lax.div(jnp.maximum(up_at, 0), last)
        up_goal = last - lax.rem(jnp.maximum(up_at, 0), last)

        @pl.when((up_at >= 0) & (up_piece < PIECES) & (up_goal > place))
        def _():
            send_on(up_goal, up_piece, place == 0, up_goal, above)

        down_at = step - (last - place)
        down_piece = lax.div(jnp.maximum(down_at, 0), last)
        down_goal = lax.rem(jnp.maximum(down_at, 0), last)

        @pl.when((down_at >= 0) & (down_piece < PIECES) & (down_goal < place))
        def _():
            slot = jnp.where(down_goal == place - 1, line, down_goal)
            send_on(down_goal, down_piece, place == last, slot, below)

        @pl.when(step == 1)
        def _():
            pl.semaphore_wait(free, groups - 1)

        at_turn(step, 0, 0, PLAIN - 1, lambda turn: give_piece(turn + 1))
        at_turn(
            step, 0, 0, PIECES - PLAIN,
            lambda turn: give_piece(PLAIN + turn),
        )
        at_turn(
            step, 1, 0, PIECES - PLAIN,
            lambda turn: lax.fori_loop(0, line, share_layer, PLAIN + turn),
        )
        at_turn(step, CLOSE_LAG, 1, PLAIN + 1, lambda turn: close_plain(turn - 1))
        at_turn(step, SETTLE_LAG, 2, PLAIN + 2, lambda turn: settle_plain(turn - 2))
        at_turn(step, SUMS_LAG, PLAIN + 1, PIECES, lambda turn: settle_sums(turn - 1))
        return carry

    lax.fori_loop(0, PIECES * last, reduce_step, 0)
    settle_sums(PIECES - 1)
    lax.fori_loop(0, last, drain_peers, 0)

    def finish(piece, carry):
        def goals(goal, inner):
            pair_copy(goal, piece).wait_send()

            @pl.when((goal != place) & (piece < PLAIN))
            def _():
                chain_copy(goal, goal, piece, above).wait_send()

            @pl.when((goal != place) & (piece >= PLAIN))
            def _():
                sums_copy(goal, goal, piece, above).wait_send()

            @pl.when((goal == place) | (piece >= PLAIN))
            def _():
                share_all(goal, piece).wait_send()
            return inner

        lax.fori_loop(0, line, goals, 0)
        return carry

    lax.fori_loop(0, PIECES, finish, 0)

    def finish_out(piece, carry):
        keep_copy(piece).wait()
        everything = out.at[:, pl.ds(0, groups - 1), :, piece_cols(piece)]
        arrived = pltpu.make_async_remote_copy(
            src_ref=everything,
            dst_ref=everything,
            send_sem=out_send.at[piece],
            recv_sem=out_recv.at[piece],
            device_id={"sample": lax.rem(group + 1, groups)},
            device_id_type=MESH,
        )
        arrived.wait_send()
        arrived.wait_recv()
        return carry

    lax.fori_loop(0, PIECES, finish_out, 0)


def exchange(seed_step, attn, resid, cotangent, gain, mean, hess, scaling):
    line = lax.axis_size("fsdp") // 2
    groups = lax.axis_size("sample")
    tokens, width = resid.shape
    in_width = attn.shape[1]
    rows = mean.shape[0]
    part = width // PIECES
    quarter = rows // groups
    vmem = pl.BlockSpec(memory_space=pltpu.VMEM)
    hbm = pl.BlockSpec(memory_space=pl.ANY)
    dma = pltpu.SemaphoreType.DMA
    return pl.pallas_call(
        functools.partial(exchange_kernel, line, groups, scaling),
        out_shape=jax.ShapeDtypeStruct((2, groups, quarter, width), jnp.bfloat16),
        in_specs=[pl.BlockSpec(memory_space=pltpu.SMEM), vmem, hbm, hbm, hbm, hbm, hbm],
        out_specs=hbm,
        scratch_shapes=[
            pltpu.VMEM((1, width), jnp.float32),
            pltpu.VMEM((tokens, 128), jnp.float32),
            pltpu.VMEM((tokens, 128), jnp.float32),
            pltpu.VMEM((tokens, in_width), jnp.bfloat16),
            pltpu.VMEM((line, PIECES, 2 * rows, part), jnp.bfloat16),
            pltpu.VMEM((tokens, width), jnp.bfloat16),
            pltpu.VMEM((tokens, width), jnp.float32),
            pltpu.VMEM((line, PIECES, rows, part), jnp.bfloat16),
            pltpu.VMEM((line + 1, PIECES, rows, part), jnp.bfloat16),
            pltpu.VMEM((line, PIECES, 2, quarter, part), jnp.bfloat16),
            pltpu.VMEM((line - 1, PIECES, groups - 1, quarter, part), jnp.bfloat16),
            dma((2,)),
            dma((2, groups)),
            dma((line,)),
            dma((line,)),
            dma((line, PIECES)),
            dma((line - 1,)),
            dma((line, PIECES)),
            dma((line,)),
            dma((line, PIECES)),
            pltpu.SemaphoreType.REGULAR,
            dma((line, PIECES)),
            dma((line, PIECES)),
            dma((line, PIECES)),
            dma((line + 1, PIECES)),
            dma((line, PIECES)),
            dma((line, PIECES)),
            dma((PIECES,)),
            dma((PIECES,)),
            dma((PIECES,)),
        ],
        compiler_params=pltpu.CompilerParams(
            collective_id=0, has_side_effects=True, vmem_limit_bytes=60 * 2**20
        ),
    )(seed_step, gain.reshape(width // 128, 128), attn, mean, hess, resid, cotangent)


def per_device(seed_step, attn, resid, cotangent, gain, mean, hess, momentum):
    in_width = attn.shape[1]
    scaling = in_width ** (-0.5)
    groups = lax.axis_size("sample")
    sums = exchange(seed_step, attn, resid, cotangent, gain, mean, hess, scaling)
    return update(mean, hess, momentum, sums.reshape((2,) + mean.shape), groups)


def solution(mesh):
    placed = (
        P(),
        P(("sample", "fsdp"), None),
        P(("sample", "fsdp"), None),
        P(("sample", "fsdp"), None),
        P(),
        P("fsdp", None),
        P("fsdp", None),
        P("fsdp", None),
    )
    return jax.shard_map(
        per_device,
        mesh=mesh,
        in_specs=placed,
        out_specs=(P("fsdp", None), P("fsdp", None), P("fsdp", None)),
        check_vma=False,
    )
```

```python
import functools

import jax
import jax.numpy as jnp
from jax import lax
from jax.experimental import pallas as pl
from jax.experimental.pallas import tpu as pltpu
from jax.sharding import PartitionSpec as P

ess_value = 10.0
decay_first = 0.8
decay_second = 0.8
step_size = 0.3
damping = 0.1
norm_eps = 1e-05


noise_scale = 2.449489742783178

MESH = pl.DeviceIdType.MESH
PIECES = 8
PLAIN = 4
READY = 1
CLOSE_LAG = 0
SETTLE_LAG = 3
SUMS_LAG = 1
STRIP = 32


def noise_count(mixing, seed, key):
    shift = lax.shift_right_logical
    mixing = jnp.bitwise_xor(mixing, seed)
    mixing = mixing * 668265261 + key
    mixing = jnp.bitwise_xor(mixing, shift(mixing, 15))
    mixing = mixing * 739982445
    mixing = jnp.bitwise_xor(mixing, shift(mixing, 12))
    mixing = mixing * 695872825
    mixing = jnp.bitwise_xor(mixing, shift(mixing, 15))
    return (mixing & 4095) + (shift(mixing, 12) & 4095)


def noise_block(first, dims, width, seed, key):
    index = (
        lax.broadcasted_iota(jnp.int32, dims, 0) * width
        + lax.broadcasted_iota(jnp.int32, dims, 1)
        + first
    )
    count = noise_count(index, seed, key).astype(jnp.float32)
    return count * (noise_scale / 4096.0) + (noise_scale / 4096.0 - noise_scale)


def ivon_update(mean, hess, momentum, grad_sum, curv_sum, groups):
    inverse = lax.rsqrt(ess_value * (hess + damping))
    grad_mean = grad_sum * (1.0 / groups)
    hess_est = curv_sum * (1.0 / groups) * (ess_value * (hess + damping) * inverse)
    new_momentum = decay_first * momentum + (1.0 - decay_first) * grad_mean
    new_hess = (
        decay_second * hess
        + (1.0 - decay_second) * hess_est
        + 0.5 * (1.0 - decay_second) ** 2 * ess_value * ((hess - hess_est) * inverse) ** 2
    )
    new_mean = mean - step_size * (new_momentum + damping * mean) / (new_hess + damping)
    return (new_mean, new_hess, new_momentum)


def update_kernel(groups, mean, hess, momentum, sums, new_mean, new_hess, new_momentum):
    rows, width = mean.shape

    def some(c, carry):
        cs = pl.ds(pl.multiple_of(c * 512, 512), 512)
        new_mean[:, cs], new_hess[:, cs], new_momentum[:, cs] = ivon_update(
            mean[:, cs], hess[:, cs], momentum[:, cs], sums[0, :, cs].astype(jnp.float32),
            sums[1, :, cs].astype(jnp.float32), groups,
        )
        return carry

    lax.fori_loop(0, width // 512, some, 0)


def update(mean, hess, momentum, sums, groups):
    rows, width = mean.shape
    height = min(64, rows)
    block = pl.BlockSpec((height, width), lambda i: (i, 0))
    return pl.pallas_call(
        functools.partial(update_kernel, groups),
        grid=(rows // height,),
        out_shape=(jax.ShapeDtypeStruct(mean.shape, jnp.float32),) * 3,
        in_specs=[block, block, block, pl.BlockSpec((2, height, width), lambda i: (0, i, 0))],
        out_specs=(block, block, block),
        compiler_params=pltpu.CompilerParams(vmem_limit_bytes=60 * 2**20),
    )(mean, hess, momentum, sums)


def exchange_kernel(
    line, groups, scaling,
    seed_step, gain_rows, attn_in, mean, hess, resid, cotangent, out,
    gain, square, cross, attn, weights, back, total, paired, chained, settings, outbox,
    local_sem, own_sem, set_up, set_down, ready_up, ready_down, set_recv, peer_send, peer_recv,
    twin_send, twin_recv, free,
    pair_send, pair_recv, chain_send, chain_recv, share_send, share_recv,
    out_send, out_recv, keep_sem,
):
    group = lax.axis_index("sample")
    shard = lax.axis_index("fsdp")
    place = lax.div(shard, 2)
    core = lax.rem(shard, 2)
    twin = place * 2 + 1 - core
    rows, width = mean.shape
    tokens, in_width = attn.shape
    quarter = rows // groups
    part = width // PIECES
    strip = min(STRIP, quarter)
    last = line - 1
    above = lax.rem(place + 1, line) * 2 + core
    below = lax.rem(place + last, line) * 2 + core

    barrier = pltpu.get_barrier_semaphore()
    for other in (twin, above, below):
        pl.semaphore_signal(barrier, inc=1, device_id={"fsdp": other}, device_id_type=MESH)
    for step in range(1, groups):
        pl.semaphore_signal(
            barrier, inc=1, device_id={"sample": lax.rem(group + step, groups)}, device_id_type=MESH
        )

    def own_copy(which, k):
        rs = pl.ds(pl.multiple_of(k * quarter, quarter), quarter)
        to = pl.ds(pl.multiple_of(which * rows + k * quarter, quarter), quarter)
        return pltpu.make_async_copy(
            (mean, hess)[which].at[rs, :], total.at[to, :], own_sem.at[which, k]
        )

    def take_own(k, carry):
        own_copy(0, lax.rem(group + k, groups)).start()
        own_copy(1, lax.rem(group + k, groups)).start()
        return carry

    lax.fori_loop(0, groups, take_own, 0)
    take_attn = pltpu.make_async_copy(attn_in, attn, local_sem.at[1])
    take_attn.start()
    take_resid = pltpu.make_async_copy(resid, back, local_sem.at[0])
    take_resid.start()

    def wait_own(k, carry):
        own_copy(0, lax.rem(group + k, groups)).wait()
        own_copy(1, lax.rem(group + k, groups)).wait()
        return carry

    wait_own(0, 0)
    seed = seed_step[0]
    key = seed_step[1] * 374761393

    def low_sigma(value):
        return lax.rsqrt(ess_value * (value + damping)).astype(jnp.bfloat16)

    def piece_cols(h):
        return pl.ds(pl.multiple_of(h * part, part), part)

    def quarter_rows(which):
        return pl.ds(pl.multiple_of(core * rows + which * quarter, quarter), quarter)

    def set_copy(layer, h, send, other):
        return pltpu.make_async_remote_copy(
            src_ref=settings.at[layer, h],
            dst_ref=settings.at[layer, h],
            send_sem=send,
            recv_sem=set_recv.at[layer, h],
            device_id={"fsdp": other},
            device_id_type=MESH,
        )

    pl.semaphore_wait(barrier, groups + 2)

    def at_end(layer):
        return (layer == 0) | (layer == last)

    def is_ready(layer, h):
        return at_end(layer) & (h >= PIECES - READY)

    def ready_copy(layer, h, send, other):
        block = weights.at[layer, h, pl.ds(pl.multiple_of(core * rows, rows), rows)]
        return pltpu.make_async_remote_copy(
            src_ref=block,
            dst_ref=block,
            send_sem=send,
            recv_sem=set_recv.at[layer, h],
            device_id={"fsdp": other},
            device_id_type=MESH,
        )

    def settle(h, carry):
        cs = piece_cols(h)
        at = pl.multiple_of(group * quarter, quarter)
        settings[place, h, 0] = total[pl.ds(at, quarter), cs].astype(jnp.bfloat16)
        settings[place, h, 1] = low_sigma(
            total[pl.ds(pl.multiple_of(rows + group * quarter, quarter), quarter), cs]
        )

        @pl.when(place < last)
        def _():
            set_copy(place, h, set_up.at[place], above).start()

        @pl.when(place > 0)
        def _():
            set_copy(place, h, set_down.at[place], below).start()
        return carry

    lax.fori_loop(0, jnp.where(at_end(place), PIECES - READY, PIECES), settle, 0)
    for k in range(width // 128):
        gain[:, k * 128 : (k + 1) * 128] = gain_rows[k : k + 1, :].astype(jnp.float32)
    lax.fori_loop(1, groups, wait_own, 0)
    square[...] = jnp.zeros(square.shape, square.dtype)
    cross[...] = jnp.zeros(cross.shape, cross.dtype)

    def twin_copy(layer, h):
        block = weights.at[layer, h, pl.ds(pl.multiple_of(core * rows, rows), rows)]
        return pltpu.make_async_remote_copy(
            src_ref=block,
            dst_ref=block,
            send_sem=twin_send.at[layer],
            recv_sem=twin_recv.at[layer, h],
            device_id={"fsdp": twin},
            device_id_type=MESH,
        )

    def first_index(g, layer, row, h):
        return (g * in_width + (layer * 2 + core) * rows + row) * width + h * part

    def sample_own(h):
        cs = piece_cols(h)

        def some(r, carry):
            at = r * strip
            mean_low = total[pl.ds(pl.multiple_of(at, strip), strip), cs].astype(jnp.bfloat16)
            sigma = low_sigma(total[pl.ds(pl.multiple_of(rows + at, strip), strip), cs])
            noise = noise_block(
                first_index(group, place, at, h), (strip, part), width, seed, key
            )
            weights[place, h, pl.ds(pl.multiple_of(core * rows + at, strip), strip)] = (
                mean_low.astype(jnp.float32) + sigma.astype(jnp.float32) * noise
            ).astype(jnp.bfloat16)
            return carry

        lax.fori_loop(0, rows // strip, some, 0)
        twin_copy(place, h).start()

        @pl.when((place == 0) & is_ready(place, h))
        def _():
            ready_copy(place, h, ready_up.at[place], above).start()

        @pl.when((place == last) & is_ready(place, h))
        def _():
            ready_copy(place, h, ready_down.at[place], below).start()

    def box_of(layer):
        return layer - jnp.where(layer > place, 1, 0)

    def peer_copy(layer, h, k):
        return pltpu.make_async_remote_copy(
            src_ref=outbox.at[box_of(layer), h, k - 1],
            dst_ref=weights.at[layer, h, quarter_rows(group)],
            send_sem=peer_send.at[box_of(layer)],
            recv_sem=peer_recv.at[layer, h],
            device_id={"sample": lax.rem(group + k, groups)},
            device_id_type=MESH,
        )

    def produce(layer, h):
        def draw(g, r):
            rs = pl.ds(pl.multiple_of(r * strip, strip), strip)
            noise = noise_block(
                first_index(g, layer, group * quarter + r * strip, h),
                (strip, part), width, seed, key,
            )
            return (
                settings[layer, h, 0, rs].astype(jnp.float32)
                + settings[layer, h, 1, rs].astype(jnp.float32) * noise
            ).astype(jnp.bfloat16)

        def for_peer(k, carry):
            def some(r, inner):
                rs = pl.ds(pl.multiple_of(r * strip, strip), strip)
                outbox[box_of(layer), h, k - 1, rs] = draw(lax.rem(group + k, groups), r)
                return inner

            lax.fori_loop(0, quarter // strip, some, 0)
            peer_copy(layer, h, k).start()
            return carry

        lax.fori_loop(1, groups, for_peer, 0)

        def for_own(r, inner):
            at = pl.multiple_of(core * rows + group * quarter + r * strip, strip)
            weights[layer, h, pl.ds(at, strip)] = draw(group, r)
            return inner

        lax.fori_loop(0, quarter // strip, for_own, 0)

    def pass_to_twin(layer, h):
        some = pl.ds(pl.multiple_of(core * rows, rows), (groups - 1) * quarter)

        @pl.when(jnp.logical_not(is_ready(layer, h)))
        def _():
            pltpu.make_async_remote_copy(
                src_ref=weights.at[layer, h, some],
                dst_ref=weights.at[layer, h, some],
                send_sem=peer_send.at[0],
                recv_sem=peer_recv.at[layer, h],
                device_id={"sample": lax.rem(group + 1, groups)},
                device_id_type=MESH,
            ).wait_recv()

        twin_copy(layer, h).start()

    def product(layer, h):
        twin_copy(layer, h).wait_recv()
        lhs = attn[:, pl.ds(pl.multiple_of(layer * 2 * rows, 2 * rows), 2 * rows)]
        return jnp.dot(lhs, weights[layer, h], preferred_element_type=jnp.float32)

    def multiply_own(h):
        cs = piece_cols(h)
        total[:, cs] = product(place, h) + back[:, cs].astype(jnp.float32) * (1.0 / scaling)

    def multiply(layer, h):
        total[:, piece_cols(h)] += product(layer, h)

    def both(i, action):
        t = lax.div(i, PIECES)
        h = lax.rem(i, PIECES)
        low = place - 1 - t
        high = place + 1 + t

        @pl.when((i >= 0) & (low >= 0))
        def _():
            action(jnp.maximum(low, 0), h, True)

        @pl.when((i >= 0) & (high <= last))
        def _():
            action(jnp.minimum(high, last), h, False)

    def arrive(layer, h, upward):
        def take(copy, up, down):
            copy(layer, h, up.at[layer], above).wait_recv()
            if upward:
                @pl.when(place < last)
                def _():
                    copy(layer, h, up.at[layer], above).start()
            else:
                @pl.when(place > 0)
                def _():
                    copy(layer, h, down.at[layer], below).start()

        @pl.when(is_ready(layer, h))
        def _():
            take(ready_copy, ready_up, ready_down)

        @pl.when(jnp.logical_not(is_ready(layer, h)))
        def _():
            take(set_copy, set_up, set_down)
            produce(layer, h)

    @pl.when(place == 0)
    def _():
        chained[0] = jnp.zeros(chained.shape[1:], chained.dtype)

    @pl.when(place == last)
    def _():
        chained[line] = jnp.zeros(chained.shape[1:], chained.dtype)

    steps = last * PIECES
    farthest = jnp.maximum(place, last - place) - 1

    def add_stats(h):
        cs = piece_cols(h)

        def some(r, carry):
            sl = pl.ds(pl.multiple_of(r * 32, 32), 32)
            value = total[sl, cs] * scaling
            upstream = gain[:, cs] * back[sl, cs].astype(jnp.float32)
            more = value * value
            mixed = value * upstream
            square[sl] += sum(more[:, k : k + 128] for k in range(0, part, 128))
            cross[sl] += sum(mixed[:, k : k + 128] for k in range(0, part, 128))
            return carry

        lax.fori_loop(0, tokens // 32, some, 0)

    def gather_step(i, carry):
        @pl.when(i < steps)
        def _():
            both(i, arrive)

        @pl.when(i < PIECES)
        def _():
            sample_own(lax.rem(i + PIECES - READY, PIECES))

        @pl.when((i >= 1) & (i <= steps))
        def _():
            both(i - 1, lambda layer, h, upward: pass_to_twin(layer, h))

        @pl.when(i == 1)
        def _():
            take_attn.wait()
            take_resid.wait()

        @pl.when((i >= 1) & (i <= PIECES))
        def _():
            multiply_own(lax.rem(i - 1 + PIECES - READY, PIECES))

        @pl.when(i == PIECES + 1)
        def _():
            pltpu.make_async_copy(cotangent, back, local_sem.at[0]).start()

        @pl.when(i >= 2)
        def _():
            both(i - 2, lambda layer, h, upward: multiply(layer, h))

            @pl.when(i == farthest * PIECES + 2)
            def _():
                pltpu.make_async_copy(cotangent, back, local_sem.at[0]).wait()

            @pl.when(lax.div(i - 2, PIECES) == farthest)
            def _():
                add_stats(lax.rem(i - 2, PIECES))
        return carry

    lax.fori_loop(0, steps + 2, gather_step, 0)

    def drain_twin(layer, carry):
        block = weights.at[layer, :, pl.ds(pl.multiple_of(core * rows, rows), rows)]
        pltpu.make_async_remote_copy(
            src_ref=block,
            dst_ref=block,
            send_sem=twin_send.at[layer],
            recv_sem=twin_recv.at[layer, 0],
            device_id={"fsdp": twin},
            device_id_type=MESH,
        ).wait_send()
        return carry

    lax.fori_loop(0, line, drain_twin, 0)

    def drain_ready(layer, send, other):
        block = weights.at[
            layer, pl.ds(PIECES - READY, READY), pl.ds(pl.multiple_of(core * rows, rows), rows)
        ]
        pltpu.make_async_remote_copy(
            src_ref=block, dst_ref=block, send_sem=send, recv_sem=set_recv.at[layer, 0],
            device_id={"fsdp": other}, device_id_type=MESH,
        ).wait_send()

    @pl.when(place < last)
    def _():
        drain_ready(0, ready_up.at[0], above)

    @pl.when(place > 0)
    def _():
        drain_ready(last, ready_down.at[last], below)
    for step in range(1, groups):
        pl.semaphore_signal(
            free, inc=1, device_id={"sample": lax.rem(group + step, groups)}, device_id_type=MESH
        )

    def finish_stats(r, carry):
        sl = pl.ds(pl.multiple_of(r * 64, 64), 64)
        scale = 1.0 / width
        inverse = lax.rsqrt(jnp.sum(square[sl], axis=-1, keepdims=True) * scale + norm_eps)
        slope = inverse * inverse * inverse * (jnp.sum(cross[sl], axis=-1, keepdims=True) * scale)
        square[sl] = jnp.broadcast_to(inverse, (64, 128))
        cross[sl] = jnp.broadcast_to(slope, (64, 128))
        return carry

    lax.fori_loop(0, tokens // 64, finish_stats, 0)

    def normalise(piece):
        cs = piece_cols(piece)

        def some(r, carry):
            sl = pl.ds(pl.multiple_of(r * 32, 32), 32)
            inverse = square[sl, 0:1]
            slope = cross[sl, 0:1] * scaling
            upstream = gain[:, cs] * back[sl, cs].astype(jnp.float32)
            back[sl, cs] = (inverse * upstream - total[sl, cs] * slope).astype(jnp.bfloat16)
            return carry

        lax.fori_loop(0, tokens // 32, some, 0)

    def partial(block, piece):
        lhs = attn[:, pl.ds(pl.multiple_of(block * rows, rows), rows)]
        rhs = back[:, piece_cols(piece)]
        return (
            lax.dot_general(lhs, rhs, (((0,), (0,)), ((), ())), preferred_element_type=jnp.float32)
            * scaling
        )

    def pair_copy(goal, piece):
        return pltpu.make_async_remote_copy(
            src_ref=weights.at[goal, piece, pl.ds(0, rows)],
            dst_ref=paired.at[goal, piece],
            send_sem=pair_send.at[goal, piece],
            recv_sem=pair_recv.at[goal, piece],
            device_id={"fsdp": twin},
            device_id_type=MESH,
        )

    def give_twin(i, piece):
        goal = jnp.where(place * 2 < line, last - i, i)
        weights[goal, piece, pl.ds(0, rows)] = partial(goal * 2 + 1 - core, piece).astype(
            jnp.bfloat16
        )
        pair_copy(goal, piece).start()
        return piece

    def drain_sets(layer, send, other):
        def some(count):
            block = settings.at[layer, pl.ds(0, count)]
            pltpu.make_async_remote_copy(
                src_ref=block, dst_ref=block, send_sem=send, recv_sem=set_recv.at[layer, 0],
                device_id={"fsdp": other}, device_id_type=MESH,
            ).wait_send()

        @pl.when(at_end(layer))
        def _():
            some(PIECES - READY)

        @pl.when(jnp.logical_not(at_end(layer)))
        def _():
            some(PIECES)

    def drain_layer(layer, carry):
        @pl.when((place < last) & (layer <= place))
        def _():
            drain_sets(layer, set_up.at[layer], above)

        @pl.when((place > 0) & (layer >= place))
        def _():
            drain_sets(layer, set_down.at[layer], below)
        return carry

    def drain_peers(layer, carry):
        box = box_of(layer)

        def some(count):
            block = outbox.at[box, pl.ds(0, count)]
            pltpu.make_async_remote_copy(
                src_ref=block, dst_ref=block,
                send_sem=peer_send.at[box], recv_sem=peer_recv.at[0, 0],
                device_id={"sample": lax.rem(group + 1, groups)}, device_id_type=MESH,
            ).wait_send()

        @pl.when((layer != place) & at_end(layer))
        def _():
            some(PIECES - READY)

        @pl.when((layer != place) & jnp.logical_not(at_end(layer)))
        def _():
            some(PIECES)
        return carry

    def chain_copy(goal, slot, piece, other):
        return pltpu.make_async_remote_copy(
            src_ref=chained.at[goal, piece],
            dst_ref=chained.at[slot, piece],
            send_sem=chain_send.at[goal, piece],
            recv_sem=chain_recv.at[slot, piece],
            device_id={"fsdp": other},
            device_id_type=MESH,
        )

    def sums_copy(goal, slot, piece, other):
        return pltpu.make_async_remote_copy(
            src_ref=chained.at[goal, piece, pl.ds(0, 2 * quarter)],
            dst_ref=chained.at[slot, piece, pl.ds(0, 2 * quarter)],
            send_sem=chain_send.at[goal, piece],
            recv_sem=chain_recv.at[slot, piece],
            device_id={"fsdp": other},
            device_id_type=MESH,
        )

    def own_term(goal, piece):
        pair_copy(goal, piece).wait_recv()
        return partial(goal * 2 + core, piece) + paired[goal, piece].astype(jnp.float32)

    def forward(goal, piece, first, slot, other):
        @pl.when(first)
        def _():
            chained[goal, piece] = own_term(goal, piece).astype(jnp.bfloat16)

        @pl.when(jnp.logical_not(first))
        def _():
            term = own_term(goal, piece)
            chain_copy(goal, goal, piece, other).wait_recv()
            chained[goal, piece] = (term + chained[goal, piece].astype(jnp.float32)).astype(
                jnp.bfloat16
            )

        chain_copy(goal, slot, piece, other).start()

    def share_rows(which):
        return pl.ds(pl.multiple_of(which * quarter, quarter), quarter)

    def inbox_rows(which):
        return pl.ds(pl.multiple_of(rows + which * quarter, quarter), quarter)

    def share_copy(layer, piece, k):
        other = lax.rem(group + k, groups)
        return pltpu.make_async_remote_copy(
            src_ref=paired.at[layer, piece, share_rows(other)],
            dst_ref=weights.at[layer, piece, inbox_rows(group)],
            send_sem=share_send.at[layer, piece],
            recv_sem=share_recv.at[layer, piece],
            device_id={"sample": other},
            device_id_type=MESH,
        )

    def share(layer, piece):
        for k in range(1, groups):
            share_copy(layer, piece, k).start()
        weights[layer, piece, inbox_rows(group)] = paired[layer, piece, share_rows(group)]

    def share_all(layer, piece):
        some = paired.at[layer, piece, pl.ds(0, (groups - 1) * quarter)]
        return pltpu.make_async_remote_copy(
            src_ref=some,
            dst_ref=some,
            send_sem=share_send.at[layer, piece],
            recv_sem=share_recv.at[layer, piece],
            device_id={"sample": lax.rem(group + 1, groups)},
            device_id_type=MESH,
        )

    def combine(layer, piece, store):
        share_all(layer, piece).wait_recv()

        def some(r, carry):
            at = r * strip
            grad_sum = jnp.zeros((strip, part), jnp.float32)
            curv_sum = jnp.zeros((strip, part), jnp.float32)
            for g in range(groups):
                grad = weights[
                    layer, piece, pl.ds(pl.multiple_of(rows + g * quarter + at, strip), strip)
                ].astype(jnp.float32)
                noise = noise_block(
                    first_index(g, layer, group * quarter + at, piece),
                    (strip, part), width, seed, key,
                )
                grad_sum = grad_sum + grad
                curv_sum = curv_sum + grad * noise
            store(at, grad_sum, curv_sum)
            return carry

        lax.fori_loop(0, quarter // strip, some, 0)

    def strip_rows(which, at):
        return pl.ds(pl.multiple_of(which * quarter + at, strip), strip)

    def forward_sums(goal, piece, first, slot, other):
        def store_first(at, grad_sum, curv_sum):
            chained[goal, piece, strip_rows(0, at)] = grad_sum.astype(jnp.bfloat16)
            chained[goal, piece, strip_rows(1, at)] = curv_sum.astype(jnp.bfloat16)

        def store_more(at, grad_sum, curv_sum):
            for which, value in ((0, grad_sum), (1, curv_sum)):
                rs = strip_rows(which, at)
                chained[goal, piece, rs] = (
                    value + chained[goal, piece, rs].astype(jnp.float32)
                ).astype(jnp.bfloat16)

        @pl.when(first)
        def _():
            combine(goal, piece, store_first)

        @pl.when(jnp.logical_not(first))
        def _():
            sums_copy(goal, goal, piece, other).wait_recv()
            combine(goal, piece, store_more)

        sums_copy(goal, slot, piece, other).start()

    def out_copy(piece, k):
        cs = piece_cols(piece)
        return pltpu.make_async_remote_copy(
            src_ref=settings.at[0, piece],
            dst_ref=out.at[:, group, :, cs],
            send_sem=out_send.at[piece],
            recv_sem=out_recv.at[piece],
            device_id={"sample": lax.rem(group + k, groups)},
            device_id_type=MESH,
        )

    def keep_copy(piece):
        return pltpu.make_async_copy(
            settings.at[0, piece], out.at[:, group, :, piece_cols(piece)], keep_sem.at[piece]
        )

    def publish(piece):
        for k in range(1, groups):
            out_copy(piece, k).start()
        keep_copy(piece).start()

    def close_plain(piece):
        term = own_term(place, piece)

        @pl.when(place > 0)
        def _():
            chain_copy(place, place, piece, below).wait_recv()

        @pl.when(place < last)
        def _():
            chain_copy(place, line, piece, above).wait_recv()

        paired[place, piece] = (
            term
            + chained[place, piece].astype(jnp.float32)
            + chained[line, piece].astype(jnp.float32)
        ).astype(jnp.bfloat16)
        share(place, piece)

    def settle_plain(piece):
        def store(at, grad_sum, curv_sum):
            rs = pl.ds(pl.multiple_of(at, strip), strip)
            settings[0, piece, 0, rs] = grad_sum.astype(jnp.bfloat16)
            settings[0, piece, 1, rs] = curv_sum.astype(jnp.bfloat16)

        combine(place, piece, store)
        publish(piece)

    def settle_sums(piece):
        @pl.when(place > 0)
        def _():
            sums_copy(place, place, piece, below).wait_recv()

        @pl.when(place < last)
        def _():
            sums_copy(place, line, piece, above).wait_recv()

        def store(at, grad_sum, curv_sum):
            for which, value in ((0, grad_sum), (1, curv_sum)):
                rs = strip_rows(which, at)
                settings[0, piece, which, pl.ds(pl.multiple_of(at, strip), strip)] = (
                    value
                    + chained[place, piece, rs].astype(jnp.float32)
                    + chained[line, piece, rs].astype(jnp.float32)
                ).astype(jnp.bfloat16)

        combine(place, piece, store)
        publish(piece)

    def give_piece(piece):
        normalise(piece)
        lax.fori_loop(0, line, give_twin, piece)

    give_piece(0)
    lax.fori_loop(0, line, drain_layer, 0)

    def send_on(goal, piece, first, slot, other):
        @pl.when(piece < PLAIN)
        def _():
            forward(goal, jnp.minimum(piece, PLAIN - 1), first, slot, other)

        @pl.when(piece >= PLAIN)
        def _():
            forward_sums(goal, jnp.maximum(piece, PLAIN), first, slot, other)

    def share_layer(layer, piece):
        paired[layer, piece] = own_term(layer, piece).astype(jnp.bfloat16)
        share(layer, piece)
        return piece

    def at_piece(step, lag, first, stop, action):
        since = jnp.maximum(step - lag, 0)
        piece = lax.div(since, last) - 1

        @pl.when((lax.rem(since, last) == 0) & (piece >= first) & (piece < stop))
        def _():
            action(piece)

    def reduce_step(step, carry):
        up_at = step - place
        up_piece = lax.div(jnp.maximum(up_at, 0), last)
        up_goal = last - lax.rem(jnp.maximum(up_at, 0), last)

        @pl.when((up_at >= 0) & (up_piece < PIECES) & (up_goal > place))
        def _():
            send_on(up_goal, up_piece, place == 0, up_goal, above)

        down_at = step - (last - place)
        down_piece = lax.div(jnp.maximum(down_at, 0), last)
        down_goal = lax.rem(jnp.maximum(down_at, 0), last)

        @pl.when((down_at >= 0) & (down_piece < PIECES) & (down_goal < place))
        def _():
            slot = jnp.where(down_goal == place - 1, line, down_goal)
            send_on(down_goal, down_piece, place == last, slot, below)

        @pl.when(step == 1)
        def _():
            pl.semaphore_wait(free, groups - 1)

        @pl.when((lax.rem(step, last) == 0) & (step < (PLAIN - 1) * last))
        def _():
            give_piece(lax.div(step, last) + 1)

        early = lax.div(step, 2)

        @pl.when((lax.rem(step, 2) == 0) & (early < PIECES - PLAIN))
        def _():
            give_piece(PLAIN + early)

        @pl.when((lax.rem(step, 2) == 1) & (early < PIECES - PLAIN))
        def _():
            lax.fori_loop(0, line, share_layer, PLAIN + early)

        at_piece(step, CLOSE_LAG, 0, PLAIN, close_plain)
        at_piece(step, SETTLE_LAG, 0, PLAIN, settle_plain)
        at_piece(step, SUMS_LAG, PLAIN, PIECES, settle_sums)
        return carry

    lax.fori_loop(0, PIECES * last + SUMS_LAG + 1, reduce_step, 0)
    lax.fori_loop(0, line, drain_peers, 0)

    def finish(piece, carry):
        def goals(goal, inner):
            pair_copy(goal, piece).wait_send()

            @pl.when((goal != place) & (piece < PLAIN))
            def _():
                chain_copy(goal, goal, piece, above).wait_send()

            @pl.when((goal != place) & (piece >= PLAIN))
            def _():
                sums_copy(goal, goal, piece, above).wait_send()

            @pl.when((goal == place) | (piece >= PLAIN))
            def _():
                share_all(goal, piece).wait_send()
            return inner

        lax.fori_loop(0, line, goals, 0)
        return carry

    lax.fori_loop(0, PIECES, finish, 0)

    def finish_out(piece, carry):
        keep_copy(piece).wait()
        everything = out.at[:, pl.ds(0, groups - 1), :, piece_cols(piece)]
        arrived = pltpu.make_async_remote_copy(
            src_ref=everything,
            dst_ref=everything,
            send_sem=out_send.at[piece],
            recv_sem=out_recv.at[piece],
            device_id={"sample": lax.rem(group + 1, groups)},
            device_id_type=MESH,
        )
        arrived.wait_send()
        arrived.wait_recv()
        return carry

    lax.fori_loop(0, PIECES, finish_out, 0)


def exchange(seed_step, attn, resid, cotangent, gain, mean, hess, scaling):
    line = lax.axis_size("fsdp") // 2
    groups = lax.axis_size("sample")
    tokens, width = resid.shape
    in_width = attn.shape[1]
    rows = mean.shape[0]
    part = width // PIECES
    quarter = rows // groups
    vmem = pl.BlockSpec(memory_space=pltpu.VMEM)
    hbm = pl.BlockSpec(memory_space=pl.ANY)
    dma = pltpu.SemaphoreType.DMA
    return pl.pallas_call(
        functools.partial(exchange_kernel, line, groups, scaling),
        out_shape=jax.ShapeDtypeStruct((2, groups, quarter, width), jnp.bfloat16),
        in_specs=[pl.BlockSpec(memory_space=pltpu.SMEM), vmem, hbm, hbm, hbm, hbm, hbm],
        out_specs=hbm,
        scratch_shapes=[
            pltpu.VMEM((1, width), jnp.float32),
            pltpu.VMEM((tokens, 128), jnp.float32),
            pltpu.VMEM((tokens, 128), jnp.float32),
            pltpu.VMEM((tokens, in_width), jnp.bfloat16),
            pltpu.VMEM((line, PIECES, 2 * rows, part), jnp.bfloat16),
            pltpu.VMEM((tokens, width), jnp.bfloat16),
            pltpu.VMEM((tokens, width), jnp.float32),
            pltpu.VMEM((line, PIECES, rows, part), jnp.bfloat16),
            pltpu.VMEM((line + 1, PIECES, rows, part), jnp.bfloat16),
            pltpu.VMEM((line, PIECES, 2, quarter, part), jnp.bfloat16),
            pltpu.VMEM((line - 1, PIECES, groups - 1, quarter, part), jnp.bfloat16),
            dma((2,)),
            dma((2, groups)),
            dma((line,)),
            dma((line,)),
            dma((line,)),
            dma((line,)),
            dma((line, PIECES)),
            dma((line - 1,)),
            dma((line, PIECES)),
            dma((line,)),
            dma((line, PIECES)),
            pltpu.SemaphoreType.REGULAR,
            dma((line, PIECES)),
            dma((line, PIECES)),
            dma((line, PIECES)),
            dma((line + 1, PIECES)),
            dma((line, PIECES)),
            dma((line, PIECES)),
            dma((PIECES,)),
            dma((PIECES,)),
            dma((PIECES,)),
        ],
        compiler_params=pltpu.CompilerParams(
            collective_id=0, has_side_effects=True, vmem_limit_bytes=60 * 2**20
        ),
    )(seed_step, gain.reshape(width // 128, 128), attn, mean, hess, resid, cotangent)


def per_device(seed_step, attn, resid, cotangent, gain, mean, hess, momentum):
    in_width = attn.shape[1]
    scaling = in_width ** (-0.5)
    groups = lax.axis_size("sample")
    sums = exchange(seed_step, attn, resid, cotangent, gain, mean, hess, scaling)
    return update(mean, hess, momentum, sums.reshape((2,) + mean.shape), groups)


def solution(mesh):
    placed = (
        P(),
        P(("sample", "fsdp"), None),
        P(("sample", "fsdp"), None),
        P(("sample", "fsdp"), None),
        P(),
        P("fsdp", None),
        P("fsdp", None),
        P("fsdp", None),
    )
    return jax.shard_map(
        per_device,
        mesh=mesh,
        in_specs=placed,
        out_specs=(P("fsdp", None), P("fsdp", None), P("fsdp", None)),
        check_vma=False,
    )
```

```python
import functools

import jax
import jax.numpy as jnp
from jax import lax
from jax.experimental import pallas as pl
from jax.experimental.pallas import tpu as pltpu
from jax.sharding import PartitionSpec as P

ess_value = 10.0
decay_first = 0.8
decay_second = 0.8
step_size = 0.3
damping = 0.1
norm_eps = 1e-05


noise_scale = 2.449489742783178

MESH = pl.DeviceIdType.MESH
PIECES = 8
PLAIN = (0, 1, 2, 3)
SUMMED = tuple(k for k in range(PIECES) if k not in PLAIN)
PACE = 2
READY = 1
CLOSE_LAG = 1
SETTLE_LAG = 5
SUMS_LAG = 3
STRIP = 32


def noise_count(mixing, seed, key):
    shift = lax.shift_right_logical
    mixing = jnp.bitwise_xor(mixing, seed)
    mixing = mixing * 668265261 + key
    mixing = jnp.bitwise_xor(mixing, shift(mixing, 15))
    mixing = mixing * 739982445
    mixing = jnp.bitwise_xor(mixing, shift(mixing, 12))
    mixing = mixing * 695872825
    mixing = jnp.bitwise_xor(mixing, shift(mixing, 15))
    return (mixing & 4095) + (shift(mixing, 12) & 4095)


def noise_block(first, dims, width, seed, key):
    index = (
        lax.broadcasted_iota(jnp.int32, dims, 0) * width
        + lax.broadcasted_iota(jnp.int32, dims, 1)
        + first
    )
    count = noise_count(index, seed, key).astype(jnp.float32)
    return count * (noise_scale / 4096.0) + (noise_scale / 4096.0 - noise_scale)


def ivon_update(mean, hess, momentum, grad_sum, curv_sum, groups):
    inverse = lax.rsqrt(ess_value * (hess + damping))
    grad_mean = grad_sum * (1.0 / groups)
    hess_est = curv_sum * (1.0 / groups) * (ess_value * (hess + damping) * inverse)
    new_momentum = decay_first * momentum + (1.0 - decay_first) * grad_mean
    new_hess = (
        decay_second * hess
        + (1.0 - decay_second) * hess_est
        + 0.5 * (1.0 - decay_second) ** 2 * ess_value * ((hess - hess_est) * inverse) ** 2
    )
    new_mean = mean - step_size * (new_momentum + damping * mean) / (new_hess + damping)
    return (new_mean, new_hess, new_momentum)


def update_kernel(groups, mean, hess, momentum, sums, new_mean, new_hess, new_momentum):
    rows, width = mean.shape

    def some(c, carry):
        cs = pl.ds(pl.multiple_of(c * 512, 512), 512)
        new_mean[:, cs], new_hess[:, cs], new_momentum[:, cs] = ivon_update(
            mean[:, cs], hess[:, cs], momentum[:, cs], sums[0, :, cs].astype(jnp.float32),
            sums[1, :, cs].astype(jnp.float32), groups,
        )
        return carry

    lax.fori_loop(0, width // 512, some, 0)


def update(mean, hess, momentum, sums, groups):
    rows, width = mean.shape
    height = min(64, rows)
    block = pl.BlockSpec((height, width), lambda i: (i, 0))
    return pl.pallas_call(
        functools.partial(update_kernel, groups),
        grid=(rows // height,),
        out_shape=(jax.ShapeDtypeStruct(mean.shape, jnp.float32),) * 3,
        in_specs=[block, block, block, pl.BlockSpec((2, height, width), lambda i: (0, i, 0))],
        out_specs=(block, block, block),
        compiler_params=pltpu.CompilerParams(vmem_limit_bytes=60 * 2**20),
    )(mean, hess, momentum, sums)


def exchange_kernel(
    line, groups, scaling,
    seed_step, gain_rows, attn_in, mean, hess, resid, cotangent, out,
    gain, square, cross, attn, weights, back, total, paired, chained, settings, outbox,
    local_sem, own_sem, set_up, set_down, ready_up, ready_down, set_recv, peer_send, peer_recv,
    twin_send, twin_recv, free,
    pair_send, pair_recv, chain_send, chain_recv, share_send, share_recv,
    out_send, out_recv, keep_sem,
):
    group = lax.axis_index("sample")
    shard = lax.axis_index("fsdp")
    place = lax.div(shard, 2)
    core = lax.rem(shard, 2)
    twin = place * 2 + 1 - core
    rows, width = mean.shape
    tokens, in_width = attn.shape
    quarter = rows // groups
    part = width // PIECES
    strip = min(STRIP, quarter)
    last = line - 1
    above = lax.rem(place + 1, line) * 2 + core
    below = lax.rem(place + last, line) * 2 + core

    barrier = pltpu.get_barrier_semaphore()
    for other in (twin, above, below):
        pl.semaphore_signal(barrier, inc=1, device_id={"fsdp": other}, device_id_type=MESH)
    for step in range(1, groups):
        pl.semaphore_signal(
            barrier, inc=1, device_id={"sample": lax.rem(group + step, groups)}, device_id_type=MESH
        )

    def own_copy(which, k):
        rs = pl.ds(pl.multiple_of(k * quarter, quarter), quarter)
        to = pl.ds(pl.multiple_of(which * rows + k * quarter, quarter), quarter)
        return pltpu.make_async_copy(
            (mean, hess)[which].at[rs, :], total.at[to, :], own_sem.at[which, k]
        )

    def take_own(k, carry):
        own_copy(0, lax.rem(group + k, groups)).start()
        own_copy(1, lax.rem(group + k, groups)).start()
        return carry

    lax.fori_loop(0, groups, take_own, 0)
    take_attn = pltpu.make_async_copy(attn_in, attn, local_sem.at[1])
    take_attn.start()
    take_resid = pltpu.make_async_copy(resid, back, local_sem.at[0])
    take_resid.start()

    def wait_own(k, carry):
        own_copy(0, lax.rem(group + k, groups)).wait()
        own_copy(1, lax.rem(group + k, groups)).wait()
        return carry

    wait_own(0, 0)
    seed = seed_step[0]
    key = seed_step[1] * 374761393

    def low_sigma(value):
        return lax.rsqrt(ess_value * (value + damping)).astype(jnp.bfloat16)

    def piece_cols(h):
        return pl.ds(pl.multiple_of(h * part, part), part)

    def quarter_rows(which):
        return pl.ds(pl.multiple_of(core * rows + which * quarter, quarter), quarter)

    def set_copy(layer, h, send, other):
        return pltpu.make_async_remote_copy(
            src_ref=settings.at[layer, h],
            dst_ref=settings.at[layer, h],
            send_sem=send,
            recv_sem=set_recv.at[layer, h],
            device_id={"fsdp": other},
            device_id_type=MESH,
        )

    pl.semaphore_wait(barrier, groups + 2)

    def at_end(layer):
        return (layer == 0) | (layer == last)

    def is_ready(layer, h):
        return at_end(layer) & (h >= PIECES - READY)

    def ready_copy(layer, h, send, other):
        block = weights.at[layer, h, pl.ds(pl.multiple_of(core * rows, rows), rows)]
        return pltpu.make_async_remote_copy(
            src_ref=block,
            dst_ref=block,
            send_sem=send,
            recv_sem=set_recv.at[layer, h],
            device_id={"fsdp": other},
            device_id_type=MESH,
        )

    def settle(h, carry):
        cs = piece_cols(h)
        at = pl.multiple_of(group * quarter, quarter)
        settings[place, h, 0] = total[pl.ds(at, quarter), cs].astype(jnp.bfloat16)
        settings[place, h, 1] = low_sigma(
            total[pl.ds(pl.multiple_of(rows + group * quarter, quarter), quarter), cs]
        )

        @pl.when(place < last)
        def _():
            set_copy(place, h, set_up.at[place], above).start()

        @pl.when(place > 0)
        def _():
            set_copy(place, h, set_down.at[place], below).start()
        return carry

    lax.fori_loop(0, jnp.where(at_end(place), PIECES - READY, PIECES), settle, 0)
    for k in range(width // 128):
        gain[:, k * 128 : (k + 1) * 128] = gain_rows[k : k + 1, :].astype(jnp.float32)
    lax.fori_loop(1, groups, wait_own, 0)
    square[...] = jnp.zeros(square.shape, square.dtype)
    cross[...] = jnp.zeros(cross.shape, cross.dtype)

    def twin_copy(layer, h):
        block = weights.at[layer, h, pl.ds(pl.multiple_of(core * rows, rows), rows)]
        return pltpu.make_async_remote_copy(
            src_ref=block,
            dst_ref=block,
            send_sem=twin_send.at[layer],
            recv_sem=twin_recv.at[layer, h],
            device_id={"fsdp": twin},
            device_id_type=MESH,
        )

    def first_index(g, layer, row, h):
        return (g * in_width + (layer * 2 + core) * rows + row) * width + h * part

    def sample_own(h):
        cs = piece_cols(h)

        def some(r, carry):
            at = r * strip
            mean_low = total[pl.ds(pl.multiple_of(at, strip), strip), cs].astype(jnp.bfloat16)
            sigma = low_sigma(total[pl.ds(pl.multiple_of(rows + at, strip), strip), cs])
            noise = noise_block(
                first_index(group, place, at, h), (strip, part), width, seed, key
            )
            weights[place, h, pl.ds(pl.multiple_of(core * rows + at, strip), strip)] = (
                mean_low.astype(jnp.float32) + sigma.astype(jnp.float32) * noise
            ).astype(jnp.bfloat16)
            return carry

        lax.fori_loop(0, rows // strip, some, 0)
        twin_copy(place, h).start()

        @pl.when((place == 0) & is_ready(place, h))
        def _():
            ready_copy(place, h, ready_up.at[place], above).start()

        @pl.when((place == last) & is_ready(place, h))
        def _():
            ready_copy(place, h, ready_down.at[place], below).start()

    def box_of(layer):
        return layer - jnp.where(layer > place, 1, 0)

    def peer_copy(layer, h, k):
        return pltpu.make_async_remote_copy(
            src_ref=outbox.at[box_of(layer), h, k - 1],
            dst_ref=weights.at[layer, h, quarter_rows(group)],
            send_sem=peer_send.at[box_of(layer)],
            recv_sem=peer_recv.at[layer, h],
            device_id={"sample": lax.rem(group + k, groups)},
            device_id_type=MESH,
        )

    def produce(layer, h):
        def draw(g, r):
            rs = pl.ds(pl.multiple_of(r * strip, strip), strip)
            noise = noise_block(
                first_index(g, layer, group * quarter + r * strip, h),
                (strip, part), width, seed, key,
            )
            return (
                settings[layer, h, 0, rs].astype(jnp.float32)
                + settings[layer, h, 1, rs].astype(jnp.float32) * noise
            ).astype(jnp.bfloat16)

        def for_peer(k, carry):
            def some(r, inner):
                rs = pl.ds(pl.multiple_of(r * strip, strip), strip)
                outbox[box_of(layer), h, k - 1, rs] = draw(lax.rem(group + k, groups), r)
                return inner

            lax.fori_loop(0, quarter // strip, some, 0)
            peer_copy(layer, h, k).start()
            return carry

        lax.fori_loop(1, groups, for_peer, 0)

        def for_own(r, inner):
            at = pl.multiple_of(core * rows + group * quarter + r * strip, strip)
            weights[layer, h, pl.ds(at, strip)] = draw(group, r)
            return inner

        lax.fori_loop(0, quarter // strip, for_own, 0)

    def pass_to_twin(layer, h):
        some = pl.ds(pl.multiple_of(core * rows, rows), (groups - 1) * quarter)

        @pl.when(jnp.logical_not(is_ready(layer, h)))
        def _():
            pltpu.make_async_remote_copy(
                src_ref=weights.at[layer, h, some],
                dst_ref=weights.at[layer, h, some],
                send_sem=peer_send.at[0],
                recv_sem=peer_recv.at[layer, h],
                device_id={"sample": lax.rem(group + 1, groups)},
                device_id_type=MESH,
            ).wait_recv()

        twin_copy(layer, h).start()

    def product(layer, h):
        twin_copy(layer, h).wait_recv()
        lhs = attn[:, pl.ds(pl.multiple_of(layer * 2 * rows, 2 * rows), 2 * rows)]
        return jnp.dot(lhs, weights[layer, h], preferred_element_type=jnp.float32)

    def multiply_own(h):
        cs = piece_cols(h)
        total[:, cs] = product(place, h) + back[:, cs].astype(jnp.float32) * (1.0 / scaling)

    def multiply(layer, h):
        total[:, piece_cols(h)] += product(layer, h)

    def both(i, action):
        t = lax.div(i, PIECES)
        h = lax.rem(i, PIECES)
        low = place - 1 - t
        high = place + 1 + t

        @pl.when((i >= 0) & (low >= 0))
        def _():
            action(jnp.maximum(low, 0), h, True)

        @pl.when((i >= 0) & (high <= last))
        def _():
            action(jnp.minimum(high, last), h, False)

    def arrive(layer, h, upward):
        def take(copy, up, down):
            copy(layer, h, up.at[layer], above).wait_recv()
            if upward:
                @pl.when(place < last)
                def _():
                    copy(layer, h, up.at[layer], above).start()
            else:
                @pl.when(place > 0)
                def _():
                    copy(layer, h, down.at[layer], below).start()

        @pl.when(is_ready(layer, h))
        def _():
            take(ready_copy, ready_up, ready_down)

        @pl.when(jnp.logical_not(is_ready(layer, h)))
        def _():
            take(set_copy, set_up, set_down)
            produce(layer, h)

    @pl.when(place == 0)
    def _():
        chained[0] = jnp.zeros(chained.shape[1:], chained.dtype)

    @pl.when(place == last)
    def _():
        chained[line] = jnp.zeros(chained.shape[1:], chained.dtype)

    steps = last * PIECES
    farthest = jnp.maximum(place, last - place) - 1

    def add_stats(h):
        cs = piece_cols(h)

        def some(r, carry):
            sl = pl.ds(pl.multiple_of(r * 32, 32), 32)
            value = total[sl, cs] * scaling
            upstream = gain[:, cs] * back[sl, cs].astype(jnp.float32)
            more = value * value
            mixed = value * upstream
            square[sl] += sum(more[:, k : k + 128] for k in range(0, part, 128))
            cross[sl] += sum(mixed[:, k : k + 128] for k in range(0, part, 128))
            return carry

        lax.fori_loop(0, tokens // 32, some, 0)

    def gather_step(i, carry):
        @pl.when(i < steps)
        def _():
            both(i, arrive)

        @pl.when(i < PIECES)
        def _():
            sample_own(lax.rem(i + PIECES - READY, PIECES))

        @pl.when((i >= 1) & (i <= steps))
        def _():
            both(i - 1, lambda layer, h, upward: pass_to_twin(layer, h))

        @pl.when(i == 1)
        def _():
            take_attn.wait()
            take_resid.wait()

        @pl.when((i >= 1) & (i <= PIECES))
        def _():
            multiply_own(lax.rem(i - 1 + PIECES - READY, PIECES))

        @pl.when(i == PIECES + 1)
        def _():
            pltpu.make_async_copy(cotangent, back, local_sem.at[0]).start()

        @pl.when(i >= 2)
        def _():
            both(i - 2, lambda layer, h, upward: multiply(layer, h))

            @pl.when(i == farthest * PIECES + 2)
            def _():
                pltpu.make_async_copy(cotangent, back, local_sem.at[0]).wait()

            @pl.when(lax.div(i - 2, PIECES) == farthest)
            def _():
                add_stats(lax.rem(i - 2, PIECES))
        return carry

    lax.fori_loop(0, steps + 2, gather_step, 0)

    def drain_twin(layer, carry):
        block = weights.at[layer, :, pl.ds(pl.multiple_of(core * rows, rows), rows)]
        pltpu.make_async_remote_copy(
            src_ref=block,
            dst_ref=block,
            send_sem=twin_send.at[layer],
            recv_sem=twin_recv.at[layer, 0],
            device_id={"fsdp": twin},
            device_id_type=MESH,
        ).wait_send()
        return carry

    lax.fori_loop(0, line, drain_twin, 0)

    def drain_ready(layer, send, other):
        block = weights.at[
            layer, pl.ds(PIECES - READY, READY), pl.ds(pl.multiple_of(core * rows, rows), rows)
        ]
        pltpu.make_async_remote_copy(
            src_ref=block, dst_ref=block, send_sem=send, recv_sem=set_recv.at[layer, 0],
            device_id={"fsdp": other}, device_id_type=MESH,
        ).wait_send()

    @pl.when(place < last)
    def _():
        drain_ready(0, ready_up.at[0], above)

    @pl.when(place > 0)
    def _():
        drain_ready(last, ready_down.at[last], below)
    for step in range(1, groups):
        pl.semaphore_signal(
            free, inc=1, device_id={"sample": lax.rem(group + step, groups)}, device_id_type=MESH
        )

    def finish_stats(r, carry):
        sl = pl.ds(pl.multiple_of(r * 64, 64), 64)
        scale = 1.0 / width
        inverse = lax.rsqrt(jnp.sum(square[sl], axis=-1, keepdims=True) * scale + norm_eps)
        slope = inverse * inverse * inverse * (jnp.sum(cross[sl], axis=-1, keepdims=True) * scale)
        square[sl] = jnp.broadcast_to(inverse, (64, 128))
        cross[sl] = jnp.broadcast_to(slope, (64, 128))
        return carry

    lax.fori_loop(0, tokens // 64, finish_stats, 0)

    def one_of(piece, which):
        found = piece == which[0]
        for k in which[1:]:
            found = found | (piece == k)
        return found

    def normalise(piece):
        cs = piece_cols(piece)

        def some(r, carry):
            sl = pl.ds(pl.multiple_of(r * 32, 32), 32)
            inverse = square[sl, 0:1]
            slope = cross[sl, 0:1] * scaling
            upstream = gain[:, cs] * back[sl, cs].astype(jnp.float32)
            back[sl, cs] = (inverse * upstream - total[sl, cs] * slope).astype(jnp.bfloat16)
            return carry

        lax.fori_loop(0, tokens // 32, some, 0)

    def partial(block, piece):
        lhs = attn[:, pl.ds(pl.multiple_of(block * rows, rows), rows)]
        rhs = back[:, piece_cols(piece)]
        return (
            lax.dot_general(lhs, rhs, (((0,), (0,)), ((), ())), preferred_element_type=jnp.float32)
            * scaling
        )

    def pair_copy(goal, piece):
        return pltpu.make_async_remote_copy(
            src_ref=weights.at[goal, piece, pl.ds(0, rows)],
            dst_ref=paired.at[goal, piece],
            send_sem=pair_send.at[goal, piece],
            recv_sem=pair_recv.at[goal, piece],
            device_id={"fsdp": twin},
            device_id_type=MESH,
        )

    def give_twin(i, piece):
        goal = jnp.where(place * 2 < line, last - i, i)
        weights[goal, piece, pl.ds(0, rows)] = partial(goal * 2 + 1 - core, piece).astype(
            jnp.bfloat16
        )
        pair_copy(goal, piece).start()
        return piece

    def drain_sets(layer, send, other):
        def some(count):
            block = settings.at[layer, pl.ds(0, count)]
            pltpu.make_async_remote_copy(
                src_ref=block, dst_ref=block, send_sem=send, recv_sem=set_recv.at[layer, 0],
                device_id={"fsdp": other}, device_id_type=MESH,
            ).wait_send()

        @pl.when(at_end(layer))
        def _():
            some(PIECES - READY)

        @pl.when(jnp.logical_not(at_end(layer)))
        def _():
            some(PIECES)

    def drain_layer(layer, carry):
        @pl.when((place < last) & (layer <= place))
        def _():
            drain_sets(layer, set_up.at[layer], above)

        @pl.when((place > 0) & (layer >= place))
        def _():
            drain_sets(layer, set_down.at[layer], below)
        return carry

    def drain_peers(layer, carry):
        box = box_of(layer)

        def some(count):
            block = outbox.at[box, pl.ds(0, count)]
            pltpu.make_async_remote_copy(
                src_ref=block, dst_ref=block,
                send_sem=peer_send.at[box], recv_sem=peer_recv.at[0, 0],
                device_id={"sample": lax.rem(group + 1, groups)}, device_id_type=MESH,
            ).wait_send()

        @pl.when((layer != place) & at_end(layer))
        def _():
            some(PIECES - READY)

        @pl.when((layer != place) & jnp.logical_not(at_end(layer)))
        def _():
            some(PIECES)
        return carry

    def chain_copy(goal, slot, piece, other):
        return pltpu.make_async_remote_copy(
            src_ref=chained.at[goal, piece],
            dst_ref=chained.at[slot, piece],
            send_sem=chain_send.at[goal, piece],
            recv_sem=chain_recv.at[slot, piece],
            device_id={"fsdp": other},
            device_id_type=MESH,
        )

    def sums_copy(goal, slot, piece, other):
        return pltpu.make_async_remote_copy(
            src_ref=chained.at[goal, piece, pl.ds(0, 2 * quarter)],
            dst_ref=chained.at[slot, piece, pl.ds(0, 2 * quarter)],
            send_sem=chain_send.at[goal, piece],
            recv_sem=chain_recv.at[slot, piece],
            device_id={"fsdp": other},
            device_id_type=MESH,
        )

    def own_term(goal, piece):
        pair_copy(goal, piece).wait_recv()
        return partial(goal * 2 + core, piece) + paired[goal, piece].astype(jnp.float32)

    def forward(goal, piece, first, slot, other):
        @pl.when(first)
        def _():
            chained[goal, piece] = own_term(goal, piece).astype(jnp.bfloat16)

        @pl.when(jnp.logical_not(first))
        def _():
            term = own_term(goal, piece)
            chain_copy(goal, goal, piece, other).wait_recv()
            chained[goal, piece] = (term + chained[goal, piece].astype(jnp.float32)).astype(
                jnp.bfloat16
            )

        chain_copy(goal, slot, piece, other).start()

    def share_rows(which):
        return pl.ds(pl.multiple_of(which * quarter, quarter), quarter)

    def inbox_rows(which):
        return pl.ds(pl.multiple_of(rows + which * quarter, quarter), quarter)

    def share_copy(layer, piece, k):
        other = lax.rem(group + k, groups)
        return pltpu.make_async_remote_copy(
            src_ref=paired.at[layer, piece, share_rows(other)],
            dst_ref=weights.at[layer, piece, inbox_rows(group)],
            send_sem=share_send.at[layer, piece],
            recv_sem=share_recv.at[layer, piece],
            device_id={"sample": other},
            device_id_type=MESH,
        )

    def share(layer, piece):
        for k in range(1, groups):
            share_copy(layer, piece, k).start()
        weights[layer, piece, inbox_rows(group)] = paired[layer, piece, share_rows(group)]

    def share_all(layer, piece):
        some = paired.at[layer, piece, pl.ds(0, (groups - 1) * quarter)]
        return pltpu.make_async_remote_copy(
            src_ref=some,
            dst_ref=some,
            send_sem=share_send.at[layer, piece],
            recv_sem=share_recv.at[layer, piece],
            device_id={"sample": lax.rem(group + 1, groups)},
            device_id_type=MESH,
        )

    def combine(layer, piece, store):
        share_all(layer, piece).wait_recv()

        def some(r, carry):
            at = r * strip
            grad_sum = jnp.zeros((strip, part), jnp.float32)
            curv_sum = jnp.zeros((strip, part), jnp.float32)
            for g in range(groups):
                grad = weights[
                    layer, piece, pl.ds(pl.multiple_of(rows + g * quarter + at, strip), strip)
                ].astype(jnp.float32)
                noise = noise_block(
                    first_index(g, layer, group * quarter + at, piece),
                    (strip, part), width, seed, key,
                )
                grad_sum = grad_sum + grad
                curv_sum = curv_sum + grad * noise
            store(at, grad_sum, curv_sum)
            return carry

        lax.fori_loop(0, quarter // strip, some, 0)

    def strip_rows(which, at):
        return pl.ds(pl.multiple_of(which * quarter + at, strip), strip)

    def hold(piece):
        def store(at, grad_sum, curv_sum):
            total[strip_rows(0, at), piece_cols(piece)] = grad_sum
            total[strip_rows(1, at), piece_cols(piece)] = curv_sum

        return store

    def forward_sums(goal, piece, first, slot, other):
        def store_first(at, grad_sum, curv_sum):
            chained[goal, piece, strip_rows(0, at)] = grad_sum.astype(jnp.bfloat16)
            chained[goal, piece, strip_rows(1, at)] = curv_sum.astype(jnp.bfloat16)

        @pl.when(first)
        def _():
            combine(goal, piece, store_first)

        @pl.when(jnp.logical_not(first))
        def _():
            combine(goal, piece, hold(piece))
            sums_copy(goal, goal, piece, other).wait_recv()
            both_sums = pl.ds(0, 2 * quarter)
            chained[goal, piece, both_sums] = (
                total[both_sums, piece_cols(piece)]
                + chained[goal, piece, both_sums].astype(jnp.float32)
            ).astype(jnp.bfloat16)

        sums_copy(goal, slot, piece, other).start()

    def out_copy(piece, k):
        cs = piece_cols(piece)
        return pltpu.make_async_remote_copy(
            src_ref=settings.at[0, piece],
            dst_ref=out.at[:, group, :, cs],
            send_sem=out_send.at[piece],
            recv_sem=out_recv.at[piece],
            device_id={"sample": lax.rem(group + k, groups)},
            device_id_type=MESH,
        )

    def keep_copy(piece):
        return pltpu.make_async_copy(
            settings.at[0, piece], out.at[:, group, :, piece_cols(piece)], keep_sem.at[piece]
        )

    def publish(piece):
        for k in range(1, groups):
            out_copy(piece, k).start()
        keep_copy(piece).start()

    def close_plain(piece):
        term = own_term(place, piece)

        @pl.when(place > 0)
        def _():
            chain_copy(place, place, piece, below).wait_recv()

        @pl.when(place < last)
        def _():
            chain_copy(place, line, piece, above).wait_recv()

        paired[place, piece] = (
            term
            + chained[place, piece].astype(jnp.float32)
            + chained[line, piece].astype(jnp.float32)
        ).astype(jnp.bfloat16)
        share(place, piece)

    def settle_plain(piece):
        def store(at, grad_sum, curv_sum):
            rs = pl.ds(pl.multiple_of(at, strip), strip)
            settings[0, piece, 0, rs] = grad_sum.astype(jnp.bfloat16)
            settings[0, piece, 1, rs] = curv_sum.astype(jnp.bfloat16)

        combine(place, piece, store)
        publish(piece)

    def settle_sums(piece):
        combine(place, piece, hold(piece))

        @pl.when(place > 0)
        def _():
            sums_copy(place, place, piece, below).wait_recv()

        @pl.when(place < last)
        def _():
            sums_copy(place, line, piece, above).wait_recv()

        for which in range(2):
            rs = pl.ds(which * quarter, quarter)
            settings[0, piece, which] = (
                total[rs, piece_cols(piece)]
                + chained[place, piece, rs].astype(jnp.float32)
                + chained[line, piece, rs].astype(jnp.float32)
            ).astype(jnp.bfloat16)
        publish(piece)

    def give_piece(piece):
        normalise(piece)
        lax.fori_loop(0, line, give_twin, piece)

    give_piece(0)
    lax.fori_loop(0, line, drain_layer, 0)

    def send_on(goal, piece, first, slot, other):
        @pl.when(one_of(piece, PLAIN))
        def _():
            forward(goal, piece, first, slot, other)

        @pl.when(one_of(piece, SUMMED))
        def _():
            forward_sums(goal, piece, first, slot, other)

    def share_layer(layer, piece):
        paired[layer, piece] = own_term(layer, piece).astype(jnp.bfloat16)
        share(layer, piece)
        return piece

    def at_piece(step, lag, which, action):
        since = jnp.maximum(step - lag, 0)
        piece = lax.div(since, last) - 1

        @pl.when((lax.rem(since, last) == 0) & one_of(piece, which))
        def _():
            action(piece)

    def reduce_step(step, carry):
        up_at = step - place
        up_piece = lax.div(jnp.maximum(up_at, 0), last)
        up_goal = last - lax.rem(jnp.maximum(up_at, 0), last)

        @pl.when((up_at >= 0) & (up_piece < PIECES) & (up_goal > place))
        def _():
            send_on(up_goal, up_piece, place == 0, up_goal, above)

        down_at = step - (last - place)
        down_piece = lax.div(jnp.maximum(down_at, 0), last)
        down_goal = lax.rem(jnp.maximum(down_at, 0), last)

        @pl.when((down_at >= 0) & (down_piece < PIECES) & (down_goal < place))
        def _():
            slot = jnp.where(down_goal == place - 1, line, down_goal)
            send_on(down_goal, down_piece, place == last, slot, below)

        @pl.when(step == 1)
        def _():
            pl.semaphore_wait(free, groups - 1)

        @pl.when((lax.rem(step, last) == 0) & one_of(lax.div(step, last) + 1, PLAIN))
        def _():
            give_piece(lax.div(step, last) + 1)

        early = lax.div(step, PACE)
        summed = SUMMED[-1]
        for k in range(len(SUMMED) - 1):
            summed = jnp.where(early == k, SUMMED[k], summed)

        @pl.when((lax.rem(step, PACE) == 0) & (early < len(SUMMED)))
        def _():
            give_piece(summed)

        @pl.when((lax.rem(step, PACE) == 1) & (early < len(SUMMED)))
        def _():
            lax.fori_loop(0, line, share_layer, summed)

        at_piece(step, CLOSE_LAG, PLAIN, close_plain)
        at_piece(step, SETTLE_LAG, PLAIN, settle_plain)
        at_piece(step, SUMS_LAG, SUMMED, settle_sums)
        return carry

    lax.fori_loop(0, PIECES * last + SUMS_LAG + 1, reduce_step, 0)
    lax.fori_loop(0, line, drain_peers, 0)

    def finish(piece, carry):
        def goals(goal, inner):
            pair_copy(goal, piece).wait_send()

            @pl.when((goal != place) & one_of(piece, PLAIN))
            def _():
                chain_copy(goal, goal, piece, above).wait_send()

            @pl.when((goal != place) & one_of(piece, SUMMED))
            def _():
                sums_copy(goal, goal, piece, above).wait_send()

            @pl.when((goal == place) | one_of(piece, SUMMED))
            def _():
                share_all(goal, piece).wait_send()
            return inner

        lax.fori_loop(0, line, goals, 0)
        return carry

    lax.fori_loop(0, PIECES, finish, 0)

    def finish_out(piece, carry):
        keep_copy(piece).wait()
        everything = out.at[:, pl.ds(0, groups - 1), :, piece_cols(piece)]
        arrived = pltpu.make_async_remote_copy(
            src_ref=everything,
            dst_ref=everything,
            send_sem=out_send.at[piece],
            recv_sem=out_recv.at[piece],
            device_id={"sample": lax.rem(group + 1, groups)},
            device_id_type=MESH,
        )
        arrived.wait_send()
        arrived.wait_recv()
        return carry

    lax.fori_loop(0, PIECES, finish_out, 0)


def exchange(seed_step, attn, resid, cotangent, gain, mean, hess, scaling):
    line = lax.axis_size("fsdp") // 2
    groups = lax.axis_size("sample")
    tokens, width = resid.shape
    in_width = attn.shape[1]
    rows = mean.shape[0]
    part = width // PIECES
    quarter = rows // groups
    vmem = pl.BlockSpec(memory_space=pltpu.VMEM)
    hbm = pl.BlockSpec(memory_space=pl.ANY)
    dma = pltpu.SemaphoreType.DMA
    return pl.pallas_call(
        functools.partial(exchange_kernel, line, groups, scaling),
        out_shape=jax.ShapeDtypeStruct((2, groups, quarter, width), jnp.bfloat16),
        in_specs=[pl.BlockSpec(memory_space=pltpu.SMEM), vmem, hbm, hbm, hbm, hbm, hbm],
        out_specs=hbm,
        scratch_shapes=[
            pltpu.VMEM((1, width), jnp.float32),
            pltpu.VMEM((tokens, 128), jnp.float32),
            pltpu.VMEM((tokens, 128), jnp.float32),
            pltpu.VMEM((tokens, in_width), jnp.bfloat16),
            pltpu.VMEM((line, PIECES, 2 * rows, part), jnp.bfloat16),
            pltpu.VMEM((tokens, width), jnp.bfloat16),
            pltpu.VMEM((tokens, width), jnp.float32),
            pltpu.VMEM((line, PIECES, rows, part), jnp.bfloat16),
            pltpu.VMEM((line + 1, PIECES, rows, part), jnp.bfloat16),
            pltpu.VMEM((line, PIECES, 2, quarter, part), jnp.bfloat16),
            pltpu.VMEM((line - 1, PIECES, groups - 1, quarter, part), jnp.bfloat16),
            dma((2,)),
            dma((2, groups)),
            dma((line,)),
            dma((line,)),
            dma((line,)),
            dma((line,)),
            dma((line, PIECES)),
            dma((line - 1,)),
            dma((line, PIECES)),
            dma((line,)),
            dma((line, PIECES)),
            pltpu.SemaphoreType.REGULAR,
            dma((line, PIECES)),
            dma((line, PIECES)),
            dma((line, PIECES)),
            dma((line + 1, PIECES)),
            dma((line, PIECES)),
            dma((line, PIECES)),
            dma((PIECES,)),
            dma((PIECES,)),
            dma((PIECES,)),
        ],
        compiler_params=pltpu.CompilerParams(
            collective_id=0, has_side_effects=True, vmem_limit_bytes=60 * 2**20
        ),
    )(seed_step, gain.reshape(width // 128, 128), attn, mean, hess, resid, cotangent)


def per_device(seed_step, attn, resid, cotangent, gain, mean, hess, momentum):
    in_width = attn.shape[1]
    scaling = in_width ** (-0.5)
    groups = lax.axis_size("sample")
    sums = exchange(seed_step, attn, resid, cotangent, gain, mean, hess, scaling)
    return update(mean, hess, momentum, sums.reshape((2,) + mean.shape), groups)


def solution(mesh):
    placed = (
        P(),
        P(("sample", "fsdp"), None),
        P(("sample", "fsdp"), None),
        P(("sample", "fsdp"), None),
        P(),
        P("fsdp", None),
        P("fsdp", None),
        P("fsdp", None),
    )
    return jax.shard_map(
        per_device,
        mesh=mesh,
        in_specs=placed,
        out_specs=(P("fsdp", None), P("fsdp", None), P("fsdp", None)),
        check_vma=False,
    )
```

```python
import functools

import jax
import jax.numpy as jnp
from jax import lax
from jax.experimental import pallas as pl
from jax.experimental.pallas import tpu as pltpu
from jax.sharding import PartitionSpec as P

ess_value = 10.0
decay_first = 0.8
decay_second = 0.8
step_size = 0.3
damping = 0.1
norm_eps = 1e-05


noise_scale = 2.449489742783178

MESH = pl.DeviceIdType.MESH
PIECES = 8
PLAIN = (0, 1, 2, 3)
SUMMED = tuple(k for k in range(PIECES) if k not in PLAIN)
PACE = 2
READY = 1
CLOSE_LAG = 1
SETTLE_LAG = 5
SUMS_LAG = 3
STRIP = 32


def noise_count(mixing, seed, key):
    shift = lax.shift_right_logical
    mixing = jnp.bitwise_xor(mixing, seed)
    mixing = mixing * 668265261 + key
    mixing = jnp.bitwise_xor(mixing, shift(mixing, 15))
    mixing = mixing * 739982445
    mixing = jnp.bitwise_xor(mixing, shift(mixing, 12))
    mixing = mixing * 695872825
    mixing = jnp.bitwise_xor(mixing, shift(mixing, 15))
    return (mixing & 4095) + (shift(mixing, 12) & 4095)


def noise_block(first, dims, width, seed, key):
    index = (
        lax.broadcasted_iota(jnp.int32, dims, 0) * width
        + lax.broadcasted_iota(jnp.int32, dims, 1)
        + first
    )
    count = noise_count(index, seed, key).astype(jnp.float32)
    return count * (noise_scale / 4096.0) + (noise_scale / 4096.0 - noise_scale)


def ivon_update(mean, hess, momentum, grad_sum, curv_sum, groups):
    inverse = lax.rsqrt(ess_value * (hess + damping))
    grad_mean = grad_sum * (1.0 / groups)
    hess_est = curv_sum * (1.0 / groups) * (ess_value * (hess + damping) * inverse)
    new_momentum = decay_first * momentum + (1.0 - decay_first) * grad_mean
    new_hess = (
        decay_second * hess
        + (1.0 - decay_second) * hess_est
        + 0.5 * (1.0 - decay_second) ** 2 * ess_value * ((hess - hess_est) * inverse) ** 2
    )
    new_mean = mean - step_size * (new_momentum + damping * mean) / (new_hess + damping)
    return (new_mean, new_hess, new_momentum)


def update_kernel(groups, mean, hess, momentum, sums, new_mean, new_hess, new_momentum):
    rows, width = mean.shape

    def some(c, carry):
        cs = pl.ds(pl.multiple_of(c * 512, 512), 512)
        new_mean[:, cs], new_hess[:, cs], new_momentum[:, cs] = ivon_update(
            mean[:, cs], hess[:, cs], momentum[:, cs], sums[0, :, cs].astype(jnp.float32),
            sums[1, :, cs].astype(jnp.float32), groups,
        )
        return carry

    lax.fori_loop(0, width // 512, some, 0)


def update(mean, hess, momentum, sums, groups):
    rows, width = mean.shape
    height = min(128, rows)
    block = pl.BlockSpec((height, width), lambda i: (i, 0))
    return pl.pallas_call(
        functools.partial(update_kernel, groups),
        grid=(rows // height,),
        out_shape=(jax.ShapeDtypeStruct(mean.shape, jnp.float32),) * 3,
        in_specs=[block, block, block, pl.BlockSpec((2, height, width), lambda i: (0, i, 0))],
        out_specs=(block, block, block),
        compiler_params=pltpu.CompilerParams(vmem_limit_bytes=60 * 2**20),
    )(mean, hess, momentum, sums)


def exchange_kernel(
    line, groups, scaling,
    seed_step, gain_rows, attn_in, mean, hess, resid, cotangent, out,
    gain, square, cross, attn, weights, back, total, paired, chained, settings, outbox,
    local_sem, own_sem, set_up, set_down, ready_up, ready_down, set_recv, peer_send, peer_recv,
    twin_send, twin_recv, free,
    pair_send, pair_recv, chain_send, chain_recv, share_send, share_recv,
    out_send, out_recv, keep_sem,
):
    group = lax.axis_index("sample")
    shard = lax.axis_index("fsdp")
    place = lax.div(shard, 2)
    core = lax.rem(shard, 2)
    twin = place * 2 + 1 - core
    rows, width = mean.shape
    tokens, in_width = attn.shape
    quarter = rows // groups
    part = width // PIECES
    strip = min(STRIP, quarter)
    last = line - 1
    above = lax.rem(place + 1, line) * 2 + core
    below = lax.rem(place + last, line) * 2 + core

    def peer(k):
        if groups != 4:
            return lax.rem(group + k, groups)
        beside = group + 1 - 2 * lax.rem(group, 2)
        return jnp.where(k == 1, 3 - group, jnp.where(k == 2, lax.rem(group + 2, 4), beside))

    barrier = pltpu.get_barrier_semaphore()
    for other in (twin, above, below):
        pl.semaphore_signal(barrier, inc=1, device_id={"fsdp": other}, device_id_type=MESH)
    for step in range(1, groups):
        pl.semaphore_signal(
            barrier, inc=1, device_id={"sample": lax.rem(group + step, groups)}, device_id_type=MESH
        )

    def own_copy(which, k):
        rs = pl.ds(pl.multiple_of(k * quarter, quarter), quarter)
        to = pl.ds(pl.multiple_of(which * rows + k * quarter, quarter), quarter)
        return pltpu.make_async_copy(
            (mean, hess)[which].at[rs, :], total.at[to, :], own_sem.at[which, k]
        )

    def take_own(k, carry):
        own_copy(0, lax.rem(group + k, groups)).start()
        own_copy(1, lax.rem(group + k, groups)).start()
        return carry

    lax.fori_loop(0, groups, take_own, 0)
    take_attn = pltpu.make_async_copy(attn_in, attn, local_sem.at[1])
    take_attn.start()
    take_resid = pltpu.make_async_copy(resid, back, local_sem.at[0])
    take_resid.start()

    def wait_own(k, carry):
        own_copy(0, lax.rem(group + k, groups)).wait()
        own_copy(1, lax.rem(group + k, groups)).wait()
        return carry

    wait_own(0, 0)
    seed = seed_step[0]
    key = seed_step[1] * 374761393

    def low_sigma(value):
        return lax.rsqrt(ess_value * (value + damping)).astype(jnp.bfloat16)

    def piece_cols(h):
        return pl.ds(pl.multiple_of(h * part, part), part)

    def quarter_rows(which):
        return pl.ds(pl.multiple_of(core * rows + which * quarter, quarter), quarter)

    def set_copy(layer, h, send, other):
        return pltpu.make_async_remote_copy(
            src_ref=settings.at[layer, h],
            dst_ref=settings.at[layer, h],
            send_sem=send,
            recv_sem=set_recv.at[layer, h],
            device_id={"fsdp": other},
            device_id_type=MESH,
        )

    pl.semaphore_wait(barrier, groups + 2)

    def at_end(layer):
        return (layer == 0) | (layer == last)

    def is_ready(layer, h):
        return at_end(layer) & (h >= PIECES - READY)

    def ready_copy(layer, h, send, other):
        block = weights.at[layer, h, pl.ds(pl.multiple_of(core * rows, rows), rows)]
        return pltpu.make_async_remote_copy(
            src_ref=block,
            dst_ref=block,
            send_sem=send,
            recv_sem=set_recv.at[layer, h],
            device_id={"fsdp": other},
            device_id_type=MESH,
        )

    def settle(h, carry):
        cs = piece_cols(h)
        at = pl.multiple_of(group * quarter, quarter)
        settings[place, h, 0] = total[pl.ds(at, quarter), cs].astype(jnp.bfloat16)
        settings[place, h, 1] = low_sigma(
            total[pl.ds(pl.multiple_of(rows + group * quarter, quarter), quarter), cs]
        )

        @pl.when(place < last)
        def _():
            set_copy(place, h, set_up.at[place], above).start()

        @pl.when(place > 0)
        def _():
            set_copy(place, h, set_down.at[place], below).start()
        return carry

    lax.fori_loop(0, jnp.where(at_end(place), PIECES - READY, PIECES), settle, 0)
    for k in range(width // 128):
        gain[:, k * 128 : (k + 1) * 128] = gain_rows[k : k + 1, :].astype(jnp.float32)
    lax.fori_loop(1, groups, wait_own, 0)
    square[...] = jnp.zeros(square.shape, square.dtype)
    cross[...] = jnp.zeros(cross.shape, cross.dtype)

    def twin_copy(layer, h):
        block = weights.at[layer, h, pl.ds(pl.multiple_of(core * rows, rows), rows)]
        return pltpu.make_async_remote_copy(
            src_ref=block,
            dst_ref=block,
            send_sem=twin_send.at[layer],
            recv_sem=twin_recv.at[layer, h],
            device_id={"fsdp": twin},
            device_id_type=MESH,
        )

    def first_index(g, layer, row, h):
        return (g * in_width + (layer * 2 + core) * rows + row) * width + h * part

    def sample_own(h):
        cs = piece_cols(h)

        def some(r, carry):
            at = r * strip
            mean_low = total[pl.ds(pl.multiple_of(at, strip), strip), cs].astype(jnp.bfloat16)
            sigma = low_sigma(total[pl.ds(pl.multiple_of(rows + at, strip), strip), cs])
            noise = noise_block(
                first_index(group, place, at, h), (strip, part), width, seed, key
            )
            weights[place, h, pl.ds(pl.multiple_of(core * rows + at, strip), strip)] = (
                mean_low.astype(jnp.float32) + sigma.astype(jnp.float32) * noise
            ).astype(jnp.bfloat16)
            return carry

        lax.fori_loop(0, rows // strip, some, 0)
        twin_copy(place, h).start()

        @pl.when((place == 0) & is_ready(place, h))
        def _():
            ready_copy(place, h, ready_up.at[place], above).start()

        @pl.when((place == last) & is_ready(place, h))
        def _():
            ready_copy(place, h, ready_down.at[place], below).start()

    def box_of(layer):
        return layer - jnp.where(layer > place, 1, 0)

    def peer_copy(layer, h, k):
        return pltpu.make_async_remote_copy(
            src_ref=outbox.at[box_of(layer), h, k - 1],
            dst_ref=weights.at[layer, h, quarter_rows(group)],
            send_sem=peer_send.at[box_of(layer)],
            recv_sem=peer_recv.at[layer, h],
            device_id={"sample": peer(k)},
            device_id_type=MESH,
        )

    def produce(layer, h):
        def draw(g, r):
            rs = pl.ds(pl.multiple_of(r * strip, strip), strip)
            noise = noise_block(
                first_index(g, layer, group * quarter + r * strip, h),
                (strip, part), width, seed, key,
            )
            return (
                settings[layer, h, 0, rs].astype(jnp.float32)
                + settings[layer, h, 1, rs].astype(jnp.float32) * noise
            ).astype(jnp.bfloat16)

        def for_peer(k, carry):
            def some(r, inner):
                rs = pl.ds(pl.multiple_of(r * strip, strip), strip)
                outbox[box_of(layer), h, k - 1, rs] = draw(peer(k), r)
                return inner

            lax.fori_loop(0, quarter // strip, some, 0)
            peer_copy(layer, h, k).start()
            return carry

        lax.fori_loop(1, groups, for_peer, 0)

        def for_own(r, inner):
            at = pl.multiple_of(core * rows + group * quarter + r * strip, strip)
            weights[layer, h, pl.ds(at, strip)] = draw(group, r)
            return inner

        lax.fori_loop(0, quarter // strip, for_own, 0)

    def pass_to_twin(layer, h):
        some = pl.ds(pl.multiple_of(core * rows, rows), (groups - 1) * quarter)

        @pl.when(jnp.logical_not(is_ready(layer, h)))
        def _():
            pltpu.make_async_remote_copy(
                src_ref=weights.at[layer, h, some],
                dst_ref=weights.at[layer, h, some],
                send_sem=peer_send.at[0],
                recv_sem=peer_recv.at[layer, h],
                device_id={"sample": lax.rem(group + 1, groups)},
                device_id_type=MESH,
            ).wait_recv()

        twin_copy(layer, h).start()

    def product(layer, h):
        twin_copy(layer, h).wait_recv()
        lhs = attn[:, pl.ds(pl.multiple_of(layer * 2 * rows, 2 * rows), 2 * rows)]
        return jnp.dot(lhs, weights[layer, h], preferred_element_type=jnp.float32)

    def multiply_own(h):
        cs = piece_cols(h)
        total[:, cs] = product(place, h) + back[:, cs].astype(jnp.float32) * (1.0 / scaling)

    def multiply(layer, h):
        total[:, piece_cols(h)] += product(layer, h)

    def both(i, action):
        t = lax.div(i, PIECES)
        h = lax.rem(i, PIECES)
        low = place - 1 - t
        high = place + 1 + t

        @pl.when((i >= 0) & (low >= 0))
        def _():
            action(jnp.maximum(low, 0), h, True)

        @pl.when((i >= 0) & (high <= last))
        def _():
            action(jnp.minimum(high, last), h, False)

    def arrive(layer, h, upward):
        def take(copy, up, down):
            copy(layer, h, up.at[layer], above).wait_recv()
            if upward:
                @pl.when(place < last)
                def _():
                    copy(layer, h, up.at[layer], above).start()
            else:
                @pl.when(place > 0)
                def _():
                    copy(layer, h, down.at[layer], below).start()

        @pl.when(is_ready(layer, h))
        def _():
            take(ready_copy, ready_up, ready_down)

        @pl.when(jnp.logical_not(is_ready(layer, h)))
        def _():
            take(set_copy, set_up, set_down)
            produce(layer, h)

    @pl.when(place == 0)
    def _():
        chained[0] = jnp.zeros(chained.shape[1:], chained.dtype)

    @pl.when(place == last)
    def _():
        chained[line] = jnp.zeros(chained.shape[1:], chained.dtype)

    steps = last * PIECES
    farthest = jnp.maximum(place, last - place) - 1

    def add_stats(h):
        cs = piece_cols(h)

        def some(r, carry):
            sl = pl.ds(pl.multiple_of(r * 32, 32), 32)
            value = total[sl, cs] * scaling
            upstream = gain[:, cs] * back[sl, cs].astype(jnp.float32)
            more = value * value
            mixed = value * upstream
            square[sl] += sum(more[:, k : k + 128] for k in range(0, part, 128))
            cross[sl] += sum(mixed[:, k : k + 128] for k in range(0, part, 128))
            return carry

        lax.fori_loop(0, tokens // 32, some, 0)

    def gather_step(i, carry):
        @pl.when(i < steps)
        def _():
            both(i, arrive)

        @pl.when(i < PIECES)
        def _():
            sample_own(lax.rem(i + PIECES - READY, PIECES))

        @pl.when((i >= 1) & (i <= steps))
        def _():
            both(i - 1, lambda layer, h, upward: pass_to_twin(layer, h))

        @pl.when(i == 1)
        def _():
            take_attn.wait()
            take_resid.wait()

        @pl.when((i >= 1) & (i <= PIECES))
        def _():
            multiply_own(lax.rem(i - 1 + PIECES - READY, PIECES))

        @pl.when(i == PIECES + 1)
        def _():
            pltpu.make_async_copy(cotangent, back, local_sem.at[0]).start()

        @pl.when(i >= 2)
        def _():
            both(i - 2, lambda layer, h, upward: multiply(layer, h))

            @pl.when(i == farthest * PIECES + 2)
            def _():
                pltpu.make_async_copy(cotangent, back, local_sem.at[0]).wait()

            @pl.when(lax.div(i - 2, PIECES) == farthest)
            def _():
                add_stats(lax.rem(i - 2, PIECES))
        return carry

    lax.fori_loop(0, steps + 2, gather_step, 0)

    def drain_twin(layer, carry):
        block = weights.at[layer, :, pl.ds(pl.multiple_of(core * rows, rows), rows)]
        pltpu.make_async_remote_copy(
            src_ref=block,
            dst_ref=block,
            send_sem=twin_send.at[layer],
            recv_sem=twin_recv.at[layer, 0],
            device_id={"fsdp": twin},
            device_id_type=MESH,
        ).wait_send()
        return carry

    lax.fori_loop(0, line, drain_twin, 0)

    def drain_ready(layer, send, other):
        block = weights.at[
            layer, pl.ds(PIECES - READY, READY), pl.ds(pl.multiple_of(core * rows, rows), rows)
        ]
        pltpu.make_async_remote_copy(
            src_ref=block, dst_ref=block, send_sem=send, recv_sem=set_recv.at[layer, 0],
            device_id={"fsdp": other}, device_id_type=MESH,
        ).wait_send()

    @pl.when(place < last)
    def _():
        drain_ready(0, ready_up.at[0], above)

    @pl.when(place > 0)
    def _():
        drain_ready(last, ready_down.at[last], below)
    for step in range(1, groups):
        pl.semaphore_signal(
            free, inc=1, device_id={"sample": lax.rem(group + step, groups)}, device_id_type=MESH
        )

    def finish_stats(r, carry):
        sl = pl.ds(pl.multiple_of(r * 64, 64), 64)
        scale = 1.0 / width
        inverse = lax.rsqrt(jnp.sum(square[sl], axis=-1, keepdims=True) * scale + norm_eps)
        slope = inverse * inverse * inverse * (jnp.sum(cross[sl], axis=-1, keepdims=True) * scale)
        square[sl] = jnp.broadcast_to(inverse, (64, 128))
        cross[sl] = jnp.broadcast_to(slope, (64, 128))
        return carry

    lax.fori_loop(0, tokens // 64, finish_stats, 0)

    def one_of(piece, which):
        found = piece == which[0]
        for k in which[1:]:
            found = found | (piece == k)
        return found

    def normalise(piece):
        cs = piece_cols(piece)

        def some(r, carry):
            sl = pl.ds(pl.multiple_of(r * 32, 32), 32)
            inverse = square[sl, 0:1]
            slope = cross[sl, 0:1] * scaling
            upstream = gain[:, cs] * back[sl, cs].astype(jnp.float32)
            back[sl, cs] = (inverse * upstream - total[sl, cs] * slope).astype(jnp.bfloat16)
            return carry

        lax.fori_loop(0, tokens // 32, some, 0)

    def partial(block, piece):
        lhs = attn[:, pl.ds(pl.multiple_of(block * rows, rows), rows)]
        rhs = back[:, piece_cols(piece)]
        return (
            lax.dot_general(lhs, rhs, (((0,), (0,)), ((), ())), preferred_element_type=jnp.float32)
            * scaling
        )

    def pair_copy(goal, piece):
        return pltpu.make_async_remote_copy(
            src_ref=weights.at[goal, piece, pl.ds(0, rows)],
            dst_ref=paired.at[goal, piece],
            send_sem=pair_send.at[goal, piece],
            recv_sem=pair_recv.at[goal, piece],
            device_id={"fsdp": twin},
            device_id_type=MESH,
        )

    def give_twin(i, piece):
        goal = jnp.where(place * 2 < line, last - i, i)
        weights[goal, piece, pl.ds(0, rows)] = partial(goal * 2 + 1 - core, piece).astype(
            jnp.bfloat16
        )
        pair_copy(goal, piece).start()
        return piece

    def drain_sets(layer, send, other):
        def some(count):
            block = settings.at[layer, pl.ds(0, count)]
            pltpu.make_async_remote_copy(
                src_ref=block, dst_ref=block, send_sem=send, recv_sem=set_recv.at[layer, 0],
                device_id={"fsdp": other}, device_id_type=MESH,
            ).wait_send()

        @pl.when(at_end(layer))
        def _():
            some(PIECES - READY)

        @pl.when(jnp.logical_not(at_end(layer)))
        def _():
            some(PIECES)

    def drain_layer(layer, carry):
        @pl.when((place < last) & (layer <= place))
        def _():
            drain_sets(layer, set_up.at[layer], above)

        @pl.when((place > 0) & (layer >= place))
        def _():
            drain_sets(layer, set_down.at[layer], below)
        return carry

    def drain_peers(layer, carry):
        box = box_of(layer)

        def some(count):
            block = outbox.at[box, pl.ds(0, count)]
            pltpu.make_async_remote_copy(
                src_ref=block, dst_ref=block,
                send_sem=peer_send.at[box], recv_sem=peer_recv.at[0, 0],
                device_id={"sample": lax.rem(group + 1, groups)}, device_id_type=MESH,
            ).wait_send()

        @pl.when((layer != place) & at_end(layer))
        def _():
            some(PIECES - READY)

        @pl.when((layer != place) & jnp.logical_not(at_end(layer)))
        def _():
            some(PIECES)
        return carry

    def chain_copy(goal, slot, piece, other):
        return pltpu.make_async_remote_copy(
            src_ref=chained.at[goal, piece],
            dst_ref=chained.at[slot, piece],
            send_sem=chain_send.at[goal, piece],
            recv_sem=chain_recv.at[slot, piece],
            device_id={"fsdp": other},
            device_id_type=MESH,
        )

    def sums_copy(goal, slot, piece, other):
        return pltpu.make_async_remote_copy(
            src_ref=chained.at[goal, piece, pl.ds(0, 2 * quarter)],
            dst_ref=chained.at[slot, piece, pl.ds(0, 2 * quarter)],
            send_sem=chain_send.at[goal, piece],
            recv_sem=chain_recv.at[slot, piece],
            device_id={"fsdp": other},
            device_id_type=MESH,
        )

    def own_term(goal, piece):
        pair_copy(goal, piece).wait_recv()
        return partial(goal * 2 + core, piece) + paired[goal, piece].astype(jnp.float32)

    def forward(goal, piece, first, slot, other):
        @pl.when(first)
        def _():
            chained[goal, piece] = own_term(goal, piece).astype(jnp.bfloat16)

        @pl.when(jnp.logical_not(first))
        def _():
            term = own_term(goal, piece)
            chain_copy(goal, goal, piece, other).wait_recv()
            chained[goal, piece] = (term + chained[goal, piece].astype(jnp.float32)).astype(
                jnp.bfloat16
            )

        chain_copy(goal, slot, piece, other).start()

    def share_rows(which):
        return pl.ds(pl.multiple_of(which * quarter, quarter), quarter)

    def inbox_rows(which):
        return pl.ds(pl.multiple_of(rows + which * quarter, quarter), quarter)

    def share_copy(layer, piece, k):
        other = peer(k)
        return pltpu.make_async_remote_copy(
            src_ref=paired.at[layer, piece, share_rows(other)],
            dst_ref=weights.at[layer, piece, inbox_rows(group)],
            send_sem=share_send.at[layer, piece],
            recv_sem=share_recv.at[layer, piece],
            device_id={"sample": other},
            device_id_type=MESH,
        )

    def share(layer, piece):
        for k in range(1, groups):
            share_copy(layer, piece, k).start()
        weights[layer, piece, inbox_rows(group)] = paired[layer, piece, share_rows(group)]

    def share_all(layer, piece):
        some = paired.at[layer, piece, pl.ds(0, (groups - 1) * quarter)]
        return pltpu.make_async_remote_copy(
            src_ref=some,
            dst_ref=some,
            send_sem=share_send.at[layer, piece],
            recv_sem=share_recv.at[layer, piece],
            device_id={"sample": lax.rem(group + 1, groups)},
            device_id_type=MESH,
        )

    def combine(layer, piece, store):
        share_all(layer, piece).wait_recv()

        def some(r, carry):
            at = r * strip
            grad_sum = jnp.zeros((strip, part), jnp.float32)
            curv_sum = jnp.zeros((strip, part), jnp.float32)
            for g in range(groups):
                grad = weights[
                    layer, piece, pl.ds(pl.multiple_of(rows + g * quarter + at, strip), strip)
                ].astype(jnp.float32)
                noise = noise_block(
                    first_index(g, layer, group * quarter + at, piece),
                    (strip, part), width, seed, key,
                )
                grad_sum = grad_sum + grad
                curv_sum = curv_sum + grad * noise
            store(at, grad_sum, curv_sum)
            return carry

        lax.fori_loop(0, quarter // strip, some, 0)

    def strip_rows(which, at):
        return pl.ds(pl.multiple_of(which * quarter + at, strip), strip)

    def hold(piece):
        def store(at, grad_sum, curv_sum):
            total[strip_rows(0, at), piece_cols(piece)] = grad_sum
            total[strip_rows(1, at), piece_cols(piece)] = curv_sum

        return store

    def forward_sums(goal, piece, first, slot, other):
        def store_first(at, grad_sum, curv_sum):
            chained[goal, piece, strip_rows(0, at)] = grad_sum.astype(jnp.bfloat16)
            chained[goal, piece, strip_rows(1, at)] = curv_sum.astype(jnp.bfloat16)

        @pl.when(first)
        def _():
            combine(goal, piece, store_first)

        @pl.when(jnp.logical_not(first))
        def _():
            combine(goal, piece, hold(piece))
            sums_copy(goal, goal, piece, other).wait_recv()
            both_sums = pl.ds(0, 2 * quarter)
            chained[goal, piece, both_sums] = (
                total[both_sums, piece_cols(piece)]
                + chained[goal, piece, both_sums].astype(jnp.float32)
            ).astype(jnp.bfloat16)

        sums_copy(goal, slot, piece, other).start()

    def out_copy(piece, k):
        cs = piece_cols(piece)
        return pltpu.make_async_remote_copy(
            src_ref=settings.at[0, piece],
            dst_ref=out.at[:, group, :, cs],
            send_sem=out_send.at[piece],
            recv_sem=out_recv.at[piece],
            device_id={"sample": peer(k)},
            device_id_type=MESH,
        )

    def keep_copy(piece):
        return pltpu.make_async_copy(
            settings.at[0, piece], out.at[:, group, :, piece_cols(piece)], keep_sem.at[piece]
        )

    def publish(piece):
        for k in range(1, groups):
            out_copy(piece, k).start()
        keep_copy(piece).start()

    def close_plain(piece):
        term = own_term(place, piece)

        @pl.when(place > 0)
        def _():
            chain_copy(place, place, piece, below).wait_recv()

        @pl.when(place < last)
        def _():
            chain_copy(place, line, piece, above).wait_recv()

        paired[place, piece] = (
            term
            + chained[place, piece].astype(jnp.float32)
            + chained[line, piece].astype(jnp.float32)
        ).astype(jnp.bfloat16)
        share(place, piece)

    def settle_plain(piece):
        def store(at, grad_sum, curv_sum):
            rs = pl.ds(pl.multiple_of(at, strip), strip)
            settings[0, piece, 0, rs] = grad_sum.astype(jnp.bfloat16)
            settings[0, piece, 1, rs] = curv_sum.astype(jnp.bfloat16)

        combine(place, piece, store)
        publish(piece)

    def settle_sums(piece):
        combine(place, piece, hold(piece))

        @pl.when(place > 0)
        def _():
            sums_copy(place, place, piece, below).wait_recv()

        @pl.when(place < last)
        def _():
            sums_copy(place, line, piece, above).wait_recv()

        for which in range(2):
            rs = pl.ds(which * quarter, quarter)
            settings[0, piece, which] = (
                total[rs, piece_cols(piece)]
                + chained[place, piece, rs].astype(jnp.float32)
                + chained[line, piece, rs].astype(jnp.float32)
            ).astype(jnp.bfloat16)
        publish(piece)

    def give_piece(piece):
        normalise(piece)
        lax.fori_loop(0, line, give_twin, piece)

    give_piece(0)
    lax.fori_loop(0, line, drain_layer, 0)

    def send_on(goal, piece, first, slot, other):
        @pl.when(one_of(piece, PLAIN))
        def _():
            forward(goal, piece, first, slot, other)

        @pl.when(one_of(piece, SUMMED))
        def _():
            forward_sums(goal, piece, first, slot, other)

    def share_layer(i, piece):
        layer = jnp.where(place * 2 < line, last - i, i)
        paired[layer, piece] = own_term(layer, piece).astype(jnp.bfloat16)
        share(layer, piece)
        return piece

    def at_piece(step, lag, which, action):
        since = jnp.maximum(step - lag, 0)
        piece = lax.div(since, last) - 1

        @pl.when((lax.rem(since, last) == 0) & one_of(piece, which))
        def _():
            action(piece)

    def reduce_step(step, carry):
        up_at = step - place
        up_piece = lax.div(jnp.maximum(up_at, 0), last)
        up_goal = last - lax.rem(jnp.maximum(up_at, 0), last)

        @pl.when((up_at >= 0) & (up_piece < PIECES) & (up_goal > place))
        def _():
            send_on(up_goal, up_piece, place == 0, up_goal, above)

        down_at = step - (last - place)
        down_piece = lax.div(jnp.maximum(down_at, 0), last)
        down_goal = lax.rem(jnp.maximum(down_at, 0), last)

        @pl.when((down_at >= 0) & (down_piece < PIECES) & (down_goal < place))
        def _():
            slot = jnp.where(down_goal == place - 1, line, down_goal)
            send_on(down_goal, down_piece, place == last, slot, below)

        @pl.when(step == 1)
        def _():
            pl.semaphore_wait(free, groups - 1)

        @pl.when((lax.rem(step, last) == 0) & one_of(lax.div(step, last) + 1, PLAIN))
        def _():
            give_piece(lax.div(step, last) + 1)

        early = lax.div(step, PACE)
        summed = SUMMED[-1]
        for k in range(len(SUMMED) - 1):
            summed = jnp.where(early == k, SUMMED[k], summed)

        @pl.when((lax.rem(step, PACE) == 0) & (early < len(SUMMED)))
        def _():
            give_piece(summed)

        @pl.when((lax.rem(step, PACE) == 1) & (early < len(SUMMED)))
        def _():
            lax.fori_loop(0, line, share_layer, summed)

        at_piece(step, CLOSE_LAG, PLAIN, close_plain)
        at_piece(step, SETTLE_LAG, PLAIN, settle_plain)
        at_piece(step, SUMS_LAG, SUMMED, settle_sums)
        return carry

    lax.fori_loop(0, PIECES * last + SUMS_LAG + 1, reduce_step, 0)
    lax.fori_loop(0, line, drain_peers, 0)

    def finish(piece, carry):
        def goals(goal, inner):
            pair_copy(goal, piece).wait_send()

            @pl.when((goal != place) & one_of(piece, PLAIN))
            def _():
                chain_copy(goal, goal, piece, above).wait_send()

            @pl.when((goal != place) & one_of(piece, SUMMED))
            def _():
                sums_copy(goal, goal, piece, above).wait_send()

            @pl.when((goal == place) | one_of(piece, SUMMED))
            def _():
                share_all(goal, piece).wait_send()
            return inner

        lax.fori_loop(0, line, goals, 0)
        return carry

    lax.fori_loop(0, PIECES, finish, 0)

    def finish_out(piece, carry):
        keep_copy(piece).wait()
        everything = out.at[:, pl.ds(0, groups - 1), :, piece_cols(piece)]
        arrived = pltpu.make_async_remote_copy(
            src_ref=everything,
            dst_ref=everything,
            send_sem=out_send.at[piece],
            recv_sem=out_recv.at[piece],
            device_id={"sample": lax.rem(group + 1, groups)},
            device_id_type=MESH,
        )
        arrived.wait_send()
        arrived.wait_recv()
        return carry

    lax.fori_loop(0, PIECES, finish_out, 0)


def exchange(seed_step, attn, resid, cotangent, gain, mean, hess, scaling):
    line = lax.axis_size("fsdp") // 2
    groups = lax.axis_size("sample")
    tokens, width = resid.shape
    in_width = attn.shape[1]
    rows = mean.shape[0]
    part = width // PIECES
    quarter = rows // groups
    vmem = pl.BlockSpec(memory_space=pltpu.VMEM)
    hbm = pl.BlockSpec(memory_space=pl.ANY)
    dma = pltpu.SemaphoreType.DMA
    return pl.pallas_call(
        functools.partial(exchange_kernel, line, groups, scaling),
        out_shape=jax.ShapeDtypeStruct((2, groups, quarter, width), jnp.bfloat16),
        in_specs=[pl.BlockSpec(memory_space=pltpu.SMEM), vmem, hbm, hbm, hbm, hbm, hbm],
        out_specs=hbm,
        scratch_shapes=[
            pltpu.VMEM((1, width), jnp.float32),
            pltpu.VMEM((tokens, 128), jnp.float32),
            pltpu.VMEM((tokens, 128), jnp.float32),
            pltpu.VMEM((tokens, in_width), jnp.bfloat16),
            pltpu.VMEM((line, PIECES, 2 * rows, part), jnp.bfloat16),
            pltpu.VMEM((tokens, width), jnp.bfloat16),
            pltpu.VMEM((tokens, width), jnp.float32),
            pltpu.VMEM((line, PIECES, rows, part), jnp.bfloat16),
            pltpu.VMEM((line + 1, PIECES, rows, part), jnp.bfloat16),
            pltpu.VMEM((line, PIECES, 2, quarter, part), jnp.bfloat16),
            pltpu.VMEM((line - 1, PIECES, groups - 1, quarter, part), jnp.bfloat16),
            dma((2,)),
            dma((2, groups)),
            dma((line,)),
            dma((line,)),
            dma((line,)),
            dma((line,)),
            dma((line, PIECES)),
            dma((line - 1,)),
            dma((line, PIECES)),
            dma((line,)),
            dma((line, PIECES)),
            pltpu.SemaphoreType.REGULAR,
            dma((line, PIECES)),
            dma((line, PIECES)),
            dma((line, PIECES)),
            dma((line + 1, PIECES)),
            dma((line, PIECES)),
            dma((line, PIECES)),
            dma((PIECES,)),
            dma((PIECES,)),
            dma((PIECES,)),
        ],
        compiler_params=pltpu.CompilerParams(
            collective_id=0, has_side_effects=True, vmem_limit_bytes=60 * 2**20
        ),
    )(seed_step, gain.reshape(width // 128, 128), attn, mean, hess, resid, cotangent)


def per_device(seed_step, attn, resid, cotangent, gain, mean, hess, momentum):
    in_width = attn.shape[1]
    scaling = in_width ** (-0.5)
    groups = lax.axis_size("sample")
    sums = exchange(seed_step, attn, resid, cotangent, gain, mean, hess, scaling)
    return update(mean, hess, momentum, sums.reshape((2,) + mean.shape), groups)


def solution(mesh):
    placed = (
        P(),
        P(("sample", "fsdp"), None),
        P(("sample", "fsdp"), None),
        P(("sample", "fsdp"), None),
        P(),
        P("fsdp", None),
        P("fsdp", None),
        P("fsdp", None),
    )
    return jax.shard_map(
        per_device,
        mesh=mesh,
        in_specs=placed,
        out_specs=(P("fsdp", None), P("fsdp", None), P("fsdp", None)),
        check_vma=False,
    )
```

```python
import functools

import jax
import jax.numpy as jnp
from jax import lax
from jax.experimental import pallas as pl
from jax.experimental.pallas import tpu as pltpu
from jax.sharding import PartitionSpec as P

ess_value = 10.0
decay_first = 0.8
decay_second = 0.8
step_size = 0.3
damping = 0.1
norm_eps = 1e-05


noise_scale = 2.449489742783178

MESH = pl.DeviceIdType.MESH
PIECES = 8
PLAIN = (0, 1, 2, 3)
SUMMED = tuple(k for k in range(PIECES) if k not in PLAIN)
PACE = 2
READY = 1
CLOSE_LAG = 1
SETTLE_LAG = 5
SUMS_LAG = 3
STRIP = 32


def noise_count(mixing, seed, key):
    shift = lax.shift_right_logical
    mixing = jnp.bitwise_xor(mixing, seed)
    mixing = mixing * 668265261 + key
    mixing = jnp.bitwise_xor(mixing, shift(mixing, 15))
    mixing = mixing * 739982445
    mixing = jnp.bitwise_xor(mixing, shift(mixing, 12))
    mixing = mixing * 695872825
    mixing = jnp.bitwise_xor(mixing, shift(mixing, 15))
    return (mixing & 4095) + (shift(mixing, 12) & 4095)


def noise_block(first, dims, width, seed, key):
    index = (
        lax.broadcasted_iota(jnp.int32, dims, 0) * width
        + lax.broadcasted_iota(jnp.int32, dims, 1)
        + first
    )
    count = noise_count(index, seed, key).astype(jnp.float32)
    return count * (noise_scale / 4096.0) + (noise_scale / 4096.0 - noise_scale)


def ivon_update(mean, hess, momentum, grad_sum, curv_sum, groups):
    inverse = lax.rsqrt(ess_value * (hess + damping))
    grad_mean = grad_sum * (1.0 / groups)
    hess_est = curv_sum * (1.0 / groups) * (ess_value * (hess + damping) * inverse)
    new_momentum = decay_first * momentum + (1.0 - decay_first) * grad_mean
    new_hess = (
        decay_second * hess
        + (1.0 - decay_second) * hess_est
        + 0.5 * (1.0 - decay_second) ** 2 * ess_value * ((hess - hess_est) * inverse) ** 2
    )
    new_mean = mean - step_size * (new_momentum + damping * mean) / (new_hess + damping)
    return (new_mean, new_hess, new_momentum)


def update_kernel(groups, mean, hess, momentum, sums, new_mean, new_hess, new_momentum):
    rows, width = mean.shape

    def some(c, carry):
        cs = pl.ds(pl.multiple_of(c * 512, 512), 512)
        new_mean[:, cs], new_hess[:, cs], new_momentum[:, cs] = ivon_update(
            mean[:, cs], hess[:, cs], momentum[:, cs], sums[0, :, cs].astype(jnp.float32),
            sums[1, :, cs].astype(jnp.float32), groups,
        )
        return carry

    lax.fori_loop(0, width // 512, some, 0)


def update(mean, hess, momentum, sums, groups):
    rows, width = mean.shape
    height = min(128, rows)
    block = pl.BlockSpec((height, width), lambda i: (i, 0))
    return pl.pallas_call(
        functools.partial(update_kernel, groups),
        grid=(rows // height,),
        out_shape=(jax.ShapeDtypeStruct(mean.shape, jnp.float32),) * 3,
        in_specs=[block, block, block, pl.BlockSpec((2, height, width), lambda i: (0, i, 0))],
        out_specs=(block, block, block),
        compiler_params=pltpu.CompilerParams(vmem_limit_bytes=60 * 2**20),
    )(mean, hess, momentum, sums)


def exchange_kernel(
    line, groups, scaling,
    seed_step, gain_rows, attn_in, mean, hess, resid, cotangent, out,
    gain, square, cross, attn, weights, back, total, paired, chained, settings, outbox,
    local_sem, own_sem, set_up, set_down, ready_up, ready_down, set_recv, peer_send, peer_recv,
    twin_send, twin_recv, free,
    pair_send, pair_recv, chain_send, chain_recv, share_send, share_recv,
    out_send, out_recv, keep_sem,
):
    group = lax.axis_index("sample")
    shard = lax.axis_index("fsdp")
    place = lax.div(shard, 2)
    core = lax.rem(shard, 2)
    twin = place * 2 + 1 - core
    rows, width = mean.shape
    tokens, in_width = attn.shape
    quarter = rows // groups
    part = width // PIECES
    strip = min(STRIP, quarter)
    last = line - 1
    above = lax.rem(place + 1, line) * 2 + core
    below = lax.rem(place + last, line) * 2 + core

    def peer(k):
        if groups != 4:
            return lax.rem(group + k, groups)
        beside = group + 1 - 2 * lax.rem(group, 2)
        return jnp.where(k == 1, 3 - group, jnp.where(k == 2, lax.rem(group + 2, 4), beside))

    barrier = pltpu.get_barrier_semaphore()
    for other in (twin, above, below):
        pl.semaphore_signal(barrier, inc=1, device_id={"fsdp": other}, device_id_type=MESH)
    for step in range(1, groups):
        pl.semaphore_signal(
            barrier, inc=1, device_id={"sample": lax.rem(group + step, groups)}, device_id_type=MESH
        )

    def own_copy(which, k):
        rs = pl.ds(pl.multiple_of(k * quarter, quarter), quarter)
        to = pl.ds(pl.multiple_of(which * rows + k * quarter, quarter), quarter)
        return pltpu.make_async_copy(
            (mean, hess)[which].at[rs, :], total.at[to, :], own_sem.at[which, k]
        )

    def take_own(k, carry):
        own_copy(0, lax.rem(group + k, groups)).start()
        own_copy(1, lax.rem(group + k, groups)).start()
        return carry

    lax.fori_loop(0, groups, take_own, 0)
    take_attn = pltpu.make_async_copy(attn_in, attn, local_sem.at[1])
    take_attn.start()
    take_resid = pltpu.make_async_copy(resid, back, local_sem.at[0])
    take_resid.start()

    def wait_own(k, carry):
        own_copy(0, lax.rem(group + k, groups)).wait()
        own_copy(1, lax.rem(group + k, groups)).wait()
        return carry

    wait_own(0, 0)
    seed = seed_step[0]
    key = seed_step[1] * 374761393

    def low_sigma(value):
        return lax.rsqrt(ess_value * (value + damping)).astype(jnp.bfloat16)

    def piece_cols(h):
        return pl.ds(pl.multiple_of(h * part, part), part)

    def quarter_rows(which):
        return pl.ds(pl.multiple_of(core * rows + which * quarter, quarter), quarter)

    def set_copy(layer, h, send, other):
        return pltpu.make_async_remote_copy(
            src_ref=settings.at[layer, h],
            dst_ref=settings.at[layer, h],
            send_sem=send,
            recv_sem=set_recv.at[layer, h],
            device_id={"fsdp": other},
            device_id_type=MESH,
        )

    pl.semaphore_wait(barrier, groups + 2)

    def at_end(layer):
        return (layer == 0) | (layer == last)

    def is_ready(layer, h):
        return at_end(layer) & (h >= PIECES - READY)

    def ready_copy(layer, h, send, other):
        block = weights.at[layer, h, pl.ds(pl.multiple_of(core * rows, rows), rows)]
        return pltpu.make_async_remote_copy(
            src_ref=block,
            dst_ref=block,
            send_sem=send,
            recv_sem=set_recv.at[layer, h],
            device_id={"fsdp": other},
            device_id_type=MESH,
        )

    def settle(h, carry):
        cs = piece_cols(h)
        at = pl.multiple_of(group * quarter, quarter)
        settings[place, h, 0] = total[pl.ds(at, quarter), cs].astype(jnp.bfloat16)
        settings[place, h, 1] = low_sigma(
            total[pl.ds(pl.multiple_of(rows + group * quarter, quarter), quarter), cs]
        )

        @pl.when(place < last)
        def _():
            set_copy(place, h, set_up.at[place], above).start()

        @pl.when(place > 0)
        def _():
            set_copy(place, h, set_down.at[place], below).start()
        return carry

    lax.fori_loop(0, jnp.where(at_end(place), PIECES - READY, PIECES), settle, 0)
    for k in range(width // 128):
        gain[:, k * 128 : (k + 1) * 128] = gain_rows[k : k + 1, :].astype(jnp.float32)
    lax.fori_loop(1, groups, wait_own, 0)
    square[...] = jnp.zeros(square.shape, square.dtype)
    cross[...] = jnp.zeros(cross.shape, cross.dtype)

    def twin_copy(layer, h):
        block = weights.at[layer, h, pl.ds(pl.multiple_of(core * rows, rows), rows)]
        return pltpu.make_async_remote_copy(
            src_ref=block,
            dst_ref=block,
            send_sem=twin_send.at[layer],
            recv_sem=twin_recv.at[layer, h],
            device_id={"fsdp": twin},
            device_id_type=MESH,
        )

    def first_index(g, layer, row, h):
        return (g * in_width + (layer * 2 + core) * rows + row) * width + h * part

    def sample_own(h):
        cs = piece_cols(h)

        def some(r, carry):
            at = r * strip
            mean_low = total[pl.ds(pl.multiple_of(at, strip), strip), cs].astype(jnp.bfloat16)
            sigma = low_sigma(total[pl.ds(pl.multiple_of(rows + at, strip), strip), cs])
            noise = noise_block(
                first_index(group, place, at, h), (strip, part), width, seed, key
            )
            weights[place, h, pl.ds(pl.multiple_of(core * rows + at, strip), strip)] = (
                mean_low.astype(jnp.float32) + sigma.astype(jnp.float32) * noise
            ).astype(jnp.bfloat16)
            return carry

        lax.fori_loop(0, rows // strip, some, 0)
        twin_copy(place, h).start()

        @pl.when((place == 0) & is_ready(place, h))
        def _():
            ready_copy(place, h, ready_up.at[place], above).start()

        @pl.when((place == last) & is_ready(place, h))
        def _():
            ready_copy(place, h, ready_down.at[place], below).start()

    def box_of(layer):
        return layer - jnp.where(layer > place, 1, 0)

    def peer_copy(layer, h, k):
        return pltpu.make_async_remote_copy(
            src_ref=outbox.at[box_of(layer), h, k - 1],
            dst_ref=weights.at[layer, h, quarter_rows(group)],
            send_sem=peer_send.at[box_of(layer)],
            recv_sem=peer_recv.at[layer, h],
            device_id={"sample": peer(k)},
            device_id_type=MESH,
        )

    def produce(layer, h):
        def draw(g, r):
            rs = pl.ds(pl.multiple_of(r * strip, strip), strip)
            noise = noise_block(
                first_index(g, layer, group * quarter + r * strip, h),
                (strip, part), width, seed, key,
            )
            return (
                settings[layer, h, 0, rs].astype(jnp.float32)
                + settings[layer, h, 1, rs].astype(jnp.float32) * noise
            ).astype(jnp.bfloat16)

        def for_peer(k, carry):
            def some(r, inner):
                rs = pl.ds(pl.multiple_of(r * strip, strip), strip)
                outbox[box_of(layer), h, k - 1, rs] = draw(peer(k), r)
                return inner

            lax.fori_loop(0, quarter // strip, some, 0)
            peer_copy(layer, h, k).start()
            return carry

        lax.fori_loop(1, groups, for_peer, 0)

        def for_own(r, inner):
            at = pl.multiple_of(core * rows + group * quarter + r * strip, strip)
            weights[layer, h, pl.ds(at, strip)] = draw(group, r)
            return inner

        lax.fori_loop(0, quarter // strip, for_own, 0)

    def pass_to_twin(layer, h):
        some = pl.ds(pl.multiple_of(core * rows, rows), (groups - 1) * quarter)

        @pl.when(jnp.logical_not(is_ready(layer, h)))
        def _():
            pltpu.make_async_remote_copy(
                src_ref=weights.at[layer, h, some],
                dst_ref=weights.at[layer, h, some],
                send_sem=peer_send.at[0],
                recv_sem=peer_recv.at[layer, h],
                device_id={"sample": lax.rem(group + 1, groups)},
                device_id_type=MESH,
            ).wait_recv()

        twin_copy(layer, h).start()

    def product(layer, h):
        twin_copy(layer, h).wait_recv()
        lhs = attn[:, pl.ds(pl.multiple_of(layer * 2 * rows, 2 * rows), 2 * rows)]
        return jnp.dot(lhs, weights[layer, h], preferred_element_type=jnp.float32)

    def multiply_own(h):
        cs = piece_cols(h)
        total[:, cs] = product(place, h) + back[:, cs].astype(jnp.float32) * (1.0 / scaling)

    def multiply(layer, h):
        total[:, piece_cols(h)] += product(layer, h)

    def both(i, action):
        t = lax.div(i, PIECES)
        h = lax.rem(i, PIECES)
        low = place - 1 - t
        high = place + 1 + t

        @pl.when((i >= 0) & (low >= 0))
        def _():
            action(jnp.maximum(low, 0), h, True)

        @pl.when((i >= 0) & (high <= last))
        def _():
            action(jnp.minimum(high, last), h, False)

    def arrive(layer, h, upward):
        def take(copy, up, down):
            copy(layer, h, up.at[layer], above).wait_recv()
            if upward:
                @pl.when(place < last)
                def _():
                    copy(layer, h, up.at[layer], above).start()
            else:
                @pl.when(place > 0)
                def _():
                    copy(layer, h, down.at[layer], below).start()

        @pl.when(is_ready(layer, h))
        def _():
            take(ready_copy, ready_up, ready_down)

        @pl.when(jnp.logical_not(is_ready(layer, h)))
        def _():
            take(set_copy, set_up, set_down)
            produce(layer, h)

    @pl.when(place == 0)
    def _():
        chained[0] = jnp.zeros(chained.shape[1:], chained.dtype)

    @pl.when(place == last)
    def _():
        chained[line] = jnp.zeros(chained.shape[1:], chained.dtype)

    steps = last * PIECES
    farthest = jnp.maximum(place, last - place) - 1

    def add_stats(h):
        cs = piece_cols(h)

        def some(r, carry):
            sl = pl.ds(pl.multiple_of(r * 32, 32), 32)
            value = total[sl, cs] * scaling
            upstream = gain[:, cs] * back[sl, cs].astype(jnp.float32)
            more = value * value
            mixed = value * upstream
            square[sl] += sum(more[:, k : k + 128] for k in range(0, part, 128))
            cross[sl] += sum(mixed[:, k : k + 128] for k in range(0, part, 128))
            return carry

        lax.fori_loop(0, tokens // 32, some, 0)

    def gather_step(i, carry):
        @pl.when(i < steps)
        def _():
            both(i, arrive)

        @pl.when(i < PIECES)
        def _():
            sample_own(lax.rem(i + PIECES - READY, PIECES))

        @pl.when((i >= 1) & (i <= steps))
        def _():
            both(i - 1, lambda layer, h, upward: pass_to_twin(layer, h))

        @pl.when(i == 1)
        def _():
            take_attn.wait()
            take_resid.wait()

        @pl.when((i >= 1) & (i <= PIECES))
        def _():
            multiply_own(lax.rem(i - 1 + PIECES - READY, PIECES))

        @pl.when(i == PIECES + 1)
        def _():
            pltpu.make_async_copy(cotangent, back, local_sem.at[0]).start()

        @pl.when(i >= 2)
        def _():
            both(i - 2, lambda layer, h, upward: multiply(layer, h))

            @pl.when(i == farthest * PIECES + 2)
            def _():
                pltpu.make_async_copy(cotangent, back, local_sem.at[0]).wait()

            @pl.when(lax.div(i - 2, PIECES) == farthest)
            def _():
                add_stats(lax.rem(i - 2, PIECES))
        return carry

    lax.fori_loop(0, steps + 2, gather_step, 0)

    def drain_twin(layer, carry):
        block = weights.at[layer, :, pl.ds(pl.multiple_of(core * rows, rows), rows)]
        pltpu.make_async_remote_copy(
            src_ref=block,
            dst_ref=block,
            send_sem=twin_send.at[layer],
            recv_sem=twin_recv.at[layer, 0],
            device_id={"fsdp": twin},
            device_id_type=MESH,
        ).wait_send()
        return carry

    lax.fori_loop(0, line, drain_twin, 0)

    def drain_ready(layer, send, other):
        block = weights.at[
            layer, pl.ds(PIECES - READY, READY), pl.ds(pl.multiple_of(core * rows, rows), rows)
        ]
        pltpu.make_async_remote_copy(
            src_ref=block, dst_ref=block, send_sem=send, recv_sem=set_recv.at[layer, 0],
            device_id={"fsdp": other}, device_id_type=MESH,
        ).wait_send()

    @pl.when(place < last)
    def _():
        drain_ready(0, ready_up.at[0], above)

    @pl.when(place > 0)
    def _():
        drain_ready(last, ready_down.at[last], below)
    for step in range(1, groups):
        pl.semaphore_signal(
            free, inc=1, device_id={"sample": lax.rem(group + step, groups)}, device_id_type=MESH
        )

    def finish_stats(r, carry):
        sl = pl.ds(pl.multiple_of(r * 64, 64), 64)
        scale = 1.0 / width
        inverse = lax.rsqrt(jnp.sum(square[sl], axis=-1, keepdims=True) * scale + norm_eps)
        slope = inverse * inverse * inverse * (jnp.sum(cross[sl], axis=-1, keepdims=True) * scale)
        square[sl] = jnp.broadcast_to(inverse, (64, 128))
        cross[sl] = jnp.broadcast_to(slope, (64, 128))
        return carry

    lax.fori_loop(0, tokens // 64, finish_stats, 0)

    def one_of(piece, which):
        found = piece == which[0]
        for k in which[1:]:
            found = found | (piece == k)
        return found

    def normalise(piece):
        cs = piece_cols(piece)

        def some(r, carry):
            sl = pl.ds(pl.multiple_of(r * 32, 32), 32)
            inverse = square[sl, 0:1]
            slope = cross[sl, 0:1] * scaling
            upstream = gain[:, cs] * back[sl, cs].astype(jnp.float32)
            back[sl, cs] = (inverse * upstream - total[sl, cs] * slope).astype(jnp.bfloat16)
            return carry

        lax.fori_loop(0, tokens // 32, some, 0)

    def partial(block, piece):
        lhs = attn[:, pl.ds(pl.multiple_of(block * rows, rows), rows)]
        rhs = back[:, piece_cols(piece)]
        return (
            lax.dot_general(lhs, rhs, (((0,), (0,)), ((), ())), preferred_element_type=jnp.float32)
            * scaling
        )

    def pair_copy(goal, piece):
        return pltpu.make_async_remote_copy(
            src_ref=weights.at[goal, piece, pl.ds(0, rows)],
            dst_ref=paired.at[goal, piece],
            send_sem=pair_send.at[goal, piece],
            recv_sem=pair_recv.at[goal, piece],
            device_id={"fsdp": twin},
            device_id_type=MESH,
        )

    def give_twin(i, piece):
        goal = jnp.where(place * 2 < line, last - i, i)
        weights[goal, piece, pl.ds(0, rows)] = partial(goal * 2 + 1 - core, piece).astype(
            jnp.bfloat16
        )
        pair_copy(goal, piece).start()
        return piece

    def drain_sets(layer, send, other):
        def some(count):
            block = settings.at[layer, pl.ds(0, count)]
            pltpu.make_async_remote_copy(
                src_ref=block, dst_ref=block, send_sem=send, recv_sem=set_recv.at[layer, 0],
                device_id={"fsdp": other}, device_id_type=MESH,
            ).wait_send()

        @pl.when(at_end(layer))
        def _():
            some(PIECES - READY)

        @pl.when(jnp.logical_not(at_end(layer)))
        def _():
            some(PIECES)

    def drain_layer(layer, carry):
        @pl.when((place < last) & (layer <= place))
        def _():
            drain_sets(layer, set_up.at[layer], above)

        @pl.when((place > 0) & (layer >= place))
        def _():
            drain_sets(layer, set_down.at[layer], below)
        return carry

    def drain_peers(layer, carry):
        box = box_of(layer)

        def some(count):
            block = outbox.at[box, pl.ds(0, count)]
            pltpu.make_async_remote_copy(
                src_ref=block, dst_ref=block,
                send_sem=peer_send.at[box], recv_sem=peer_recv.at[0, 0],
                device_id={"sample": lax.rem(group + 1, groups)}, device_id_type=MESH,
            ).wait_send()

        @pl.when((layer != place) & at_end(layer))
        def _():
            some(PIECES - READY)

        @pl.when((layer != place) & jnp.logical_not(at_end(layer)))
        def _():
            some(PIECES)
        return carry

    def chain_copy(goal, slot, piece, other):
        return pltpu.make_async_remote_copy(
            src_ref=chained.at[goal, piece],
            dst_ref=chained.at[slot, piece],
            send_sem=chain_send.at[goal, piece],
            recv_sem=chain_recv.at[slot, piece],
            device_id={"fsdp": other},
            device_id_type=MESH,
        )

    def sums_copy(goal, slot, piece, other):
        return pltpu.make_async_remote_copy(
            src_ref=chained.at[goal, piece, pl.ds(0, 2 * quarter)],
            dst_ref=chained.at[slot, piece, pl.ds(0, 2 * quarter)],
            send_sem=chain_send.at[goal, piece],
            recv_sem=chain_recv.at[slot, piece],
            device_id={"fsdp": other},
            device_id_type=MESH,
        )

    def own_term(goal, piece):
        pair_copy(goal, piece).wait_recv()
        return partial(goal * 2 + core, piece) + paired[goal, piece].astype(jnp.float32)

    def forward(goal, piece, first, slot, other):
        @pl.when(first)
        def _():
            chained[goal, piece] = own_term(goal, piece).astype(jnp.bfloat16)

        @pl.when(jnp.logical_not(first))
        def _():
            term = own_term(goal, piece)
            chain_copy(goal, goal, piece, other).wait_recv()
            chained[goal, piece] = (term + chained[goal, piece].astype(jnp.float32)).astype(
                jnp.bfloat16
            )

        chain_copy(goal, slot, piece, other).start()

    def share_rows(which):
        return pl.ds(pl.multiple_of(which * quarter, quarter), quarter)

    def inbox_rows(which):
        return pl.ds(pl.multiple_of(rows + which * quarter, quarter), quarter)

    def share_copy(layer, piece, k):
        other = peer(k)
        return pltpu.make_async_remote_copy(
            src_ref=paired.at[layer, piece, share_rows(other)],
            dst_ref=weights.at[layer, piece, inbox_rows(group)],
            send_sem=share_send.at[layer, piece],
            recv_sem=share_recv.at[layer, piece],
            device_id={"sample": other},
            device_id_type=MESH,
        )

    def share(layer, piece):
        for k in range(1, groups):
            share_copy(layer, piece, k).start()
        weights[layer, piece, inbox_rows(group)] = paired[layer, piece, share_rows(group)]

    def share_all(layer, piece):
        some = paired.at[layer, piece, pl.ds(0, (groups - 1) * quarter)]
        return pltpu.make_async_remote_copy(
            src_ref=some,
            dst_ref=some,
            send_sem=share_send.at[layer, piece],
            recv_sem=share_recv.at[layer, piece],
            device_id={"sample": lax.rem(group + 1, groups)},
            device_id_type=MESH,
        )

    def combine(layer, piece, store):
        share_all(layer, piece).wait_recv()

        def some(r, carry):
            at = r * strip
            grad_sum = jnp.zeros((strip, part), jnp.float32)
            curv_sum = jnp.zeros((strip, part), jnp.float32)
            for g in range(groups):
                grad = weights[
                    layer, piece, pl.ds(pl.multiple_of(rows + g * quarter + at, strip), strip)
                ].astype(jnp.float32)
                noise = noise_block(
                    first_index(g, layer, group * quarter + at, piece),
                    (strip, part), width, seed, key,
                )
                grad_sum = grad_sum + grad
                curv_sum = curv_sum + grad * noise
            store(at, grad_sum, curv_sum)
            return carry

        lax.fori_loop(0, quarter // strip, some, 0)

    def strip_rows(which, at):
        return pl.ds(pl.multiple_of(which * quarter + at, strip), strip)

    def hold(piece):
        def store(at, grad_sum, curv_sum):
            total[strip_rows(0, at), piece_cols(piece)] = grad_sum
            total[strip_rows(1, at), piece_cols(piece)] = curv_sum

        return store

    def forward_sums(goal, piece, first, slot, other):
        def store_first(at, grad_sum, curv_sum):
            chained[goal, piece, strip_rows(0, at)] = grad_sum.astype(jnp.bfloat16)
            chained[goal, piece, strip_rows(1, at)] = curv_sum.astype(jnp.bfloat16)

        @pl.when(first)
        def _():
            combine(goal, piece, store_first)

        @pl.when(jnp.logical_not(first))
        def _():
            combine(goal, piece, hold(piece))
            sums_copy(goal, goal, piece, other).wait_recv()
            both_sums = pl.ds(0, 2 * quarter)
            chained[goal, piece, both_sums] = (
                total[both_sums, piece_cols(piece)]
                + chained[goal, piece, both_sums].astype(jnp.float32)
            ).astype(jnp.bfloat16)

        sums_copy(goal, slot, piece, other).start()

    def out_copy(piece, k):
        cs = piece_cols(piece)
        return pltpu.make_async_remote_copy(
            src_ref=settings.at[0, piece],
            dst_ref=out.at[:, group, :, cs],
            send_sem=out_send.at[piece],
            recv_sem=out_recv.at[piece],
            device_id={"sample": peer(k)},
            device_id_type=MESH,
        )

    def keep_copy(piece):
        return pltpu.make_async_copy(
            settings.at[0, piece], out.at[:, group, :, piece_cols(piece)], keep_sem.at[piece]
        )

    def publish(piece):
        for k in range(1, groups):
            out_copy(piece, k).start()
        keep_copy(piece).start()

    def close_plain(piece):
        term = own_term(place, piece)

        @pl.when(place > 0)
        def _():
            chain_copy(place, place, piece, below).wait_recv()

        @pl.when(place < last)
        def _():
            chain_copy(place, line, piece, above).wait_recv()

        paired[place, piece] = (
            term
            + chained[place, piece].astype(jnp.float32)
            + chained[line, piece].astype(jnp.float32)
        ).astype(jnp.bfloat16)
        share(place, piece)

    def settle_plain(piece):
        def store(at, grad_sum, curv_sum):
            rs = pl.ds(pl.multiple_of(at, strip), strip)
            settings[0, piece, 0, rs] = grad_sum.astype(jnp.bfloat16)
            settings[0, piece, 1, rs] = curv_sum.astype(jnp.bfloat16)

        combine(place, piece, store)
        publish(piece)

    def settle_sums(piece):
        combine(place, piece, hold(piece))

        @pl.when(place > 0)
        def _():
            sums_copy(place, place, piece, below).wait_recv()

        @pl.when(place < last)
        def _():
            sums_copy(place, line, piece, above).wait_recv()

        for which in range(2):
            rs = pl.ds(which * quarter, quarter)
            settings[0, piece, which] = (
                total[rs, piece_cols(piece)]
                + chained[place, piece, rs].astype(jnp.float32)
                + chained[line, piece, rs].astype(jnp.float32)
            ).astype(jnp.bfloat16)
        publish(piece)

    def give_piece(piece):
        normalise(piece)
        lax.fori_loop(0, line, give_twin, piece)

    give_piece(0)
    lax.fori_loop(0, line, drain_layer, 0)

    def send_on(goal, piece, first, slot, other):
        @pl.when(one_of(piece, PLAIN))
        def _():
            forward(goal, piece, first, slot, other)

        @pl.when(one_of(piece, SUMMED))
        def _():
            forward_sums(goal, piece, first, slot, other)

    def share_layer(i, piece):
        layer = jnp.where(place * 2 < line, last - i, i)
        paired[layer, piece] = own_term(layer, piece).astype(jnp.bfloat16)
        share(layer, piece)
        return piece

    def at_piece(step, lag, which, action):
        since = jnp.maximum(step - lag, 0)
        piece = lax.div(since, last) - 1

        @pl.when((lax.rem(since, last) == 0) & one_of(piece, which))
        def _():
            action(piece)

    def reduce_step(step, carry):
        up_at = step - place
        up_piece = lax.div(jnp.maximum(up_at, 0), last)
        up_goal = last - lax.rem(jnp.maximum(up_at, 0), last)

        @pl.when((up_at >= 0) & (up_piece < PIECES) & (up_goal > place))
        def _():
            send_on(up_goal, up_piece, place == 0, up_goal, above)

        down_at = step - (last - place)
        down_piece = lax.div(jnp.maximum(down_at, 0), last)
        down_goal = lax.rem(jnp.maximum(down_at, 0), last)

        @pl.when((down_at >= 0) & (down_piece < PIECES) & (down_goal < place))
        def _():
            slot = jnp.where(down_goal == place - 1, line, down_goal)
            send_on(down_goal, down_piece, place == last, slot, below)

        @pl.when(step == 0)
        def _():
            give_piece(SUMMED[0])
            pl.semaphore_wait(free, groups - 1)

        @pl.when((lax.rem(step, last) == 0) & one_of(lax.div(step, last) + 1, PLAIN))
        def _():
            give_piece(lax.div(step, last) + 1)

        def summed(early):
            piece = SUMMED[-1]
            for k in range(len(SUMMED) - 1):
                piece = jnp.where(early == k, SUMMED[k], piece)
            return piece

        early = lax.div(step, PACE)

        @pl.when((lax.rem(step, PACE) == 0) & (early < len(SUMMED)))
        def _():
            lax.fori_loop(0, line, share_layer, summed(early))

        @pl.when((lax.rem(step, PACE) == 1) & (early + 1 < len(SUMMED)))
        def _():
            give_piece(summed(early + 1))

        at_piece(step, CLOSE_LAG, PLAIN, close_plain)
        at_piece(step, SETTLE_LAG, PLAIN, settle_plain)
        at_piece(step, SUMS_LAG, SUMMED, settle_sums)
        return carry

    lax.fori_loop(0, PIECES * last + SUMS_LAG + 1, reduce_step, 0)
    lax.fori_loop(0, line, drain_peers, 0)

    def finish(piece, carry):
        def goals(goal, inner):
            pair_copy(goal, piece).wait_send()

            @pl.when((goal != place) & one_of(piece, PLAIN))
            def _():
                chain_copy(goal, goal, piece, above).wait_send()

            @pl.when((goal != place) & one_of(piece, SUMMED))
            def _():
                sums_copy(goal, goal, piece, above).wait_send()

            @pl.when((goal == place) | one_of(piece, SUMMED))
            def _():
                share_all(goal, piece).wait_send()
            return inner

        lax.fori_loop(0, line, goals, 0)
        return carry

    lax.fori_loop(0, PIECES, finish, 0)

    def finish_out(piece, carry):
        keep_copy(piece).wait()
        everything = out.at[:, pl.ds(0, groups - 1), :, piece_cols(piece)]
        arrived = pltpu.make_async_remote_copy(
            src_ref=everything,
            dst_ref=everything,
            send_sem=out_send.at[piece],
            recv_sem=out_recv.at[piece],
            device_id={"sample": lax.rem(group + 1, groups)},
            device_id_type=MESH,
        )
        arrived.wait_send()
        arrived.wait_recv()
        return carry

    lax.fori_loop(0, PIECES, finish_out, 0)


def exchange(seed_step, attn, resid, cotangent, gain, mean, hess, scaling):
    line = lax.axis_size("fsdp") // 2
    groups = lax.axis_size("sample")
    tokens, width = resid.shape
    in_width = attn.shape[1]
    rows = mean.shape[0]
    part = width // PIECES
    quarter = rows // groups
    vmem = pl.BlockSpec(memory_space=pltpu.VMEM)
    hbm = pl.BlockSpec(memory_space=pl.ANY)
    dma = pltpu.SemaphoreType.DMA
    return pl.pallas_call(
        functools.partial(exchange_kernel, line, groups, scaling),
        out_shape=jax.ShapeDtypeStruct((2, groups, quarter, width), jnp.bfloat16),
        in_specs=[pl.BlockSpec(memory_space=pltpu.SMEM), vmem, hbm, hbm, hbm, hbm, hbm],
        out_specs=hbm,
        scratch_shapes=[
            pltpu.VMEM((1, width), jnp.float32),
            pltpu.VMEM((tokens, 128), jnp.float32),
            pltpu.VMEM((tokens, 128), jnp.float32),
            pltpu.VMEM((tokens, in_width), jnp.bfloat16),
            pltpu.VMEM((line, PIECES, 2 * rows, part), jnp.bfloat16),
            pltpu.VMEM((tokens, width), jnp.bfloat16),
            pltpu.VMEM((tokens, width), jnp.float32),
            pltpu.VMEM((line, PIECES, rows, part), jnp.bfloat16),
            pltpu.VMEM((line + 1, PIECES, rows, part), jnp.bfloat16),
            pltpu.VMEM((line, PIECES, 2, quarter, part), jnp.bfloat16),
            pltpu.VMEM((line - 1, PIECES, groups - 1, quarter, part), jnp.bfloat16),
            dma((2,)),
            dma((2, groups)),
            dma((line,)),
            dma((line,)),
            dma((line,)),
            dma((line,)),
            dma((line, PIECES)),
            dma((line - 1,)),
            dma((line, PIECES)),
            dma((line,)),
            dma((line, PIECES)),
            pltpu.SemaphoreType.REGULAR,
            dma((line, PIECES)),
            dma((line, PIECES)),
            dma((line, PIECES)),
            dma((line + 1, PIECES)),
            dma((line, PIECES)),
            dma((line, PIECES)),
            dma((PIECES,)),
            dma((PIECES,)),
            dma((PIECES,)),
        ],
        compiler_params=pltpu.CompilerParams(
            collective_id=0, has_side_effects=True, vmem_limit_bytes=60 * 2**20
        ),
    )(seed_step, gain.reshape(width // 128, 128), attn, mean, hess, resid, cotangent)


def per_device(seed_step, attn, resid, cotangent, gain, mean, hess, momentum):
    in_width = attn.shape[1]
    scaling = in_width ** (-0.5)
    groups = lax.axis_size("sample")
    sums = exchange(seed_step, attn, resid, cotangent, gain, mean, hess, scaling)
    return update(mean, hess, momentum, sums.reshape((2,) + mean.shape), groups)


def solution(mesh):
    placed = (
        P(),
        P(("sample", "fsdp"), None),
        P(("sample", "fsdp"), None),
        P(("sample", "fsdp"), None),
        P(),
        P("fsdp", None),
        P("fsdp", None),
        P("fsdp", None),
    )
    return jax.shard_map(
        per_device,
        mesh=mesh,
        in_specs=placed,
        out_specs=(P("fsdp", None), P("fsdp", None), P("fsdp", None)),
        check_vma=False,
    )
```
